128 devices in a mesh: dp: 16 (over z, x), pair: 8 (over y, core).
Axes of the slice: x: 4, y: 4, z: 4, core: 2. Of those that a mesh axis runs over, the one named last changes fastest.
Arguments:
- table: float32 [65536, 512], P(('dp', 'pair')), may hold values from -6 to 6
- accum: float32 [65536], P(('dp', 'pair')), may hold values from 0.05 to 2
- item_row: int32 [49152], P(('dp', 'pair')), may hold values from 0 to 65535, as said below
- segments: int32 [16, 3072], P('dp'), may hold values from 0 to 1, never falling along the last dimension, each value on 1 to 2880 neighbouring positions
- pairs: int32 [16, 40, 2], P('dp'), may hold values from -1 to 7, as said below
- w_in: bfloat16 [512, 2048], replicated, may hold values from -0.25 to 0.25
- w_out: bfloat16 [512, 512], replicated, may hold values from -0.25 to 0.25
- out_grad: bfloat16 [49152, 512], P(('dp', 'pair')), may hold values from -6 to 6
Outputs:
- layer_out: bfloat16 [49152, 512], P(('dp', 'pair'))
- table_new: float32 [65536, 512], P(('dp', 'pair'))
- accum_new: float32 [65536], P(('dp', 'pair'))
- grad_in: float32 [512, 2048], P(('dp', 'pair'))
- grad_out: float32 [512, 512], P(('dp', 'pair'))
The draws below stay inside these ranges and needn't reach their ends.
Inputs may be any that keep to these rules, and one draw needn't show every extreme that they name: Row r is held by device r // 512 at slot r % 512. The 384 actions of one device (aligned blocks of item_row) name rows of any one device at most 6 times, repeats counted; in every draw one device receives exactly 6 from every device. Row g lists causal block pairs (query block, key block) of the group, key block at most query block, each at most once; every diagonal pair and every pair with key block 0 is listed, the other causal pairs some of them; slots s * 5 to s * 5 + 4 belong to index s of pair; unused slots hold (-1, -1). `segments`: actions with equal ids in a group belong to one history.
All inputs are finite; a program needn't handle non-finite values.
Results may differ from the reference program's by a relative error of at most 0.0025.
The reference program's roundings to bfloat16 on the way count: a program that leaves them out, or rounds other values in their place, can miss the bound.
Values may be sent and summed in bfloat16 or wider, within the bound.
A program may use at most 192 MiB of HBM per device.

```python
import math
import jax
import jax.numpy as jnp
import numpy as np
from jax import lax

D = 512
HEADS = 8
DH = 64
TOK_DEV = 384
ROWS_DEV = 512
SHARDS = 128
SPAN = 8
GROUPS = 16
GROUP_ROWS = 3072
PCAP = 5
TOKENS = 49152
ROWS = 65536


def draw_item_row(key, part):
    per_owner = TOK_DEV // SHARDS
    bound_rows = 2 * per_owner
    halves = SHARDS // 2
    key_list = jax.random.split(key, 6)
    chosen = jax.random.randint(key_list[0], (), 0, halves)
    full_side = jax.random.randint(key_list[1], (), 0, 2)
    first_count = jax.random.randint(key_list[2], (SHARDS, halves), 1, bound_rows)
    flipped = jax.random.randint(key_list[3], (SHARDS, halves), 0, 2)
    first_count = jnp.where(flipped == 1, bound_rows - first_count, first_count)
    full_first = jnp.where(full_side == 0, bound_rows, 0)
    first_count = jnp.where(jnp.arange(halves)[None, :] == chosen, full_first, first_count)
    counts = jnp.stack([first_count, bound_rows - first_count], axis=2).reshape(SHARDS, SHARDS)
    bucket_ends = jnp.cumsum(counts, axis=1)
    places = jnp.arange(TOK_DEV)
    owners = jnp.sum((bucket_ends[:, None, :] <= places[None, :, None]).astype(jnp.int32), axis=2)
    row_keys = jax.random.split(key_list[4], SHARDS)
    owners = jax.vmap(lambda subkey, owner_row: jax.random.permutation(subkey, owner_row))(row_keys, owners)
    row_slots = jax.random.randint(key_list[5], (SHARDS, TOK_DEV), 0, ROWS_DEV)
    return (owners * ROWS_DEV + row_slots).reshape(TOKENS).astype(jnp.int32)


def draw_pairs(key, part):
    pair_total = SPAN * (SPAN + 1) // 2
    order_index = jnp.arange(SPAN * SPAN)
    query_block = order_index // SPAN
    key_block = order_index % SPAN
    priority = jnp.where(query_block >= key_block, 0, 1) * (SPAN * SPAN) + order_index
    ordering = jnp.argsort(priority)[:pair_total]
    causal_query = query_block[ordering]
    causal_key = key_block[ordering]
    always = (causal_query == causal_key) | (causal_key == 0)

    def one_group(group_key):
        key_list = jax.random.split(group_key, 3)
        shuffled = jax.random.permutation(key_list[0], pair_total)
        coin = jax.random.randint(key_list[1], (pair_total,), 0, 2)
        keep = (always | (coin == 1))[shuffled]
        query_list = causal_query[shuffled]
        key_listed = causal_key[shuffled]
        rank = jnp.argsort(jnp.where(keep, 0, 1) * pair_total + jnp.arange(pair_total))
        query_list = query_list[rank]
        key_listed = key_listed[rank]
        keep = keep[rank]
        rotation = jax.random.randint(key_list[2], (), 0, SPAN)
        serial = jnp.arange(pair_total)
        device = (serial + rotation) % SPAN
        slot_number = serial // SPAN
        flat_index = jnp.where(keep, device * PCAP + slot_number, SPAN * PCAP)
        table_out = jnp.full((SPAN * PCAP, 2), -1, jnp.int32)
        return table_out.at[flat_index].set(jnp.stack([query_list, key_listed], axis=1).astype(jnp.int32), mode='drop')
    return jax.vmap(one_group)(jax.random.split(key, GROUPS)).astype(jnp.int32)


def levels(stream_key, extent, cuts, least, top_value):
    gain = 1.0
    for dim, shards_of in cuts:
        draws = jax.random.uniform(jax.random.fold_in(jax.random.fold_in(stream_key, 6), dim), (shards_of,), jnp.float32, least / len(cuts), top_value / len(cuts))
        gain = gain * jnp.repeat(jnp.exp(draws), extent[dim] // shards_of).reshape((-1,) + (1,) * (len(extent) - 1 - dim))
    return gain


def profile(number_of, total, limit, skew):
    portions = [(1 << 20) // math.isqrt(grade ** skew) + 1 for grade in range(2, number_of + 1)]
    spare, given = total - limit - (number_of - 1), [1] * (number_of - 1)
    while spare > 0:
        movable = [i for i in range(number_of - 1) if given[i] < limit]
        whole, remaining = sum([portions[i] for i in movable]), spare
        for i in movable:
            more = min(limit - given[i], max(1, remaining * portions[i] // whole), spare)
            given[i] = given[i] + more
            spare = spare - more
    return np.array([limit] + given)


def uneven_parts(rng, amount, total, bound, lean):
    if amount == 2:
        one = jax.random.randint(rng, (), max(1, total - bound), min(bound, total - 1) + 1)
        return jnp.stack([one, total - one])
    sizes = jnp.asarray(profile(amount, total, bound, lean), jnp.int32)
    couples = (amount - 1) // 2
    giver, taker = sizes[1:1 + 2 * couples:2], sizes[2:2 + 2 * couples:2]
    slack = jnp.minimum(giver - 1, bound - taker)
    shifted = jax.random.randint(jax.random.fold_in(rng, 1), (couples,), 0, 1 << 20) % (slack + 1)
    sizes = sizes.at[1:1 + 2 * couples:2].set(giver - shifted).at[2:2 + 2 * couples:2].set(taker + shifted)
    return sizes[jax.random.permutation(jax.random.fold_in(rng, 2), amount)]


def bell_draw(rng, shape, deviation, bound, pieces=(), kind=jnp.bfloat16):
    values = deviation * jax.random.normal(rng, shape, jnp.float32)
    if pieces:
        values = values * levels(rng, shape, pieces, -0.22, 0.18)
    return jnp.clip(values, -bound, bound).astype(kind)


def setup_inputs(seed: int = 0) -> dict:
    keys = jax.random.split(jax.random.key(seed), 9)
    table = bell_draw(keys[0], (ROWS, D), 1.0, 6.0, ((0, 128),), jnp.float32)
    accum = jnp.clip(jnp.exp(math.log(2.0) - 3.6888794 * jax.random.uniform(keys[1], (ROWS,), jnp.float32) ** levels(keys[1], (ROWS,), ((0, 128),), -0.2, 0.2)), 0.05, 2.0)
    item_row = draw_item_row(jax.random.fold_in(keys[8], 71), 0)
    segments = jax.vmap(lambda own: jnp.searchsorted(jnp.cumsum(uneven_parts(own, 2, GROUP_ROWS, GROUP_ROWS - TOK_DEV // 2, 2)), jnp.arange(GROUP_ROWS), side="right"))(jax.random.split(keys[3], GROUPS)).reshape((GROUPS, GROUP_ROWS)).astype(jnp.int32)
    pairs = draw_pairs(jax.random.fold_in(keys[8], 71), 0)
    w_in = bell_draw(keys[5], (D, 4 * D), D ** -0.5, 0.25)
    w_out = bell_draw(keys[6], (D, D), D ** -0.5, 0.25)
    out_grad = bell_draw(keys[7], (TOKENS, D), 1.0, 6.0, ((0, 128),))
    return dict(table=table, accum=accum, item_row=item_row, segments=segments, pairs=pairs, w_in=w_in, w_out=w_out, out_grad=out_grad)


norm_eps = 1e-05
learn_rate = 0.5

def normalize(values):
    row_mean = lax.optimization_barrier(jnp.mean(values, axis=-1, keepdims=True))
    centred = values - row_mean
    spread = jnp.sqrt(lax.optimization_barrier(jnp.mean(centred * centred, axis=-1, keepdims=True)) + norm_eps)
    return (centred / spread, spread)

def norm_back(grad_rows, normed, spread):
    first_mean = lax.optimization_barrier(jnp.mean(grad_rows, axis=-1, keepdims=True))
    second_mean = lax.optimization_barrier(jnp.mean(grad_rows * normed, axis=-1, keepdims=True))
    return (grad_rows - first_mean - normed * second_mean) / spread

def silu_slope(values):
    sigmoid_value = jax.nn.sigmoid(values)
    return sigmoid_value * (1.0 + values * (1.0 - sigmoid_value))

def round_trip(values):
    return lax.optimization_barrier(values.astype(jnp.bfloat16)).astype(jnp.float32)

def split_heads(matrix):
    return matrix.astype(jnp.float32).reshape(matrix.shape[0], HEADS, DH)

def block_visible(present_group, segment_group, block_index):
    query_pos = jnp.arange(TOK_DEV, dtype=jnp.int32) + block_index * TOK_DEV
    key_pos = jnp.arange(GROUP_ROWS, dtype=jnp.int32)
    listed = present_group[block_index][key_pos // TOK_DEV]
    same = segment_group[key_pos][None, :] == segment_group[query_pos][:, None]
    return listed[None, :] & (key_pos[None, :] <= query_pos[:, None]) & same

def group_forward(operands):
    hidden, segment_group, present_group = operands
    key_rows = split_heads(hidden[:, 3 * D:])
    value_rows = split_heads(hidden[:, D:2 * D])
    results = []
    for block_index in range(SPAN):
        visible = block_visible(present_group, segment_group, block_index)
        query_rows = split_heads(hidden[block_index * TOK_DEV:(block_index + 1) * TOK_DEV, 2 * D:3 * D])
        scores = jnp.einsum('rhd,chd->hrc', query_rows, key_rows) * DH ** (-0.5)
        weights = round_trip(jnp.where(visible[None], jax.nn.silu(scores), 0.0))
        results.append(jnp.einsum('hrc,chd->rhd', weights, value_rows).reshape(TOK_DEV, D))
    return jnp.concatenate(results, axis=0)

def group_backward(operands):
    hidden, grad_attend, segment_group, present_group = operands
    key_rows = split_heads(hidden[:, 3 * D:])
    value_rows = split_heads(hidden[:, D:2 * D])
    grad_key = jnp.zeros((GROUP_ROWS, HEADS, DH), jnp.float32)
    grad_value = jnp.zeros((GROUP_ROWS, HEADS, DH), jnp.float32)
    query_grads = []
    for block_index in range(SPAN):
        visible = block_visible(present_group, segment_group, block_index)
        lower = block_index * TOK_DEV
        upper = lower + TOK_DEV
        query_rows = split_heads(hidden[lower:upper, 2 * D:3 * D])
        grad_rows = split_heads(grad_attend[lower:upper])
        scores = jnp.einsum('rhd,chd->hrc', query_rows, key_rows) * DH ** (-0.5)
        weights = round_trip(jnp.where(visible[None], jax.nn.silu(scores), 0.0))
        grad_weights = jnp.einsum('rhd,chd->hrc', grad_rows, value_rows)
        grad_scores = round_trip(jnp.where(visible[None], grad_weights * silu_slope(scores) * DH ** (-0.5), 0.0))
        query_grads.append(jnp.einsum('hrc,chd->rhd', grad_scores, key_rows).reshape(TOK_DEV, D))
        grad_key = grad_key + jnp.einsum('hrc,rhd->chd', grad_scores, query_rows)
        grad_value = grad_value + jnp.einsum('hrc,rhd->chd', weights, grad_rows)
    return (jnp.concatenate(query_grads, axis=0), grad_key.reshape(GROUP_ROWS, D), grad_value.reshape(GROUP_ROWS, D))

def reference(table, accum, item_row, segments, pairs, w_in, w_out, out_grad):
    action_rows = table[item_row].astype(jnp.bfloat16)
    action_float = action_rows.astype(jnp.float32)
    normed, action_spread = normalize(action_float)
    normed_low = normed.astype(jnp.bfloat16)
    pre_act = jnp.dot(normed_low, w_in, preferred_element_type=jnp.float32)
    hidden = jax.nn.silu(pre_act).astype(jnp.bfloat16)
    blocks = jnp.arange(SPAN, dtype=jnp.int32)
    present = jnp.any((pairs[:, :, 0, None, None] == blocks[None, None, :, None]) & (pairs[:, :, 1, None, None] == blocks[None, None, None, :]), axis=1)
    grouped = hidden.reshape(GROUPS, GROUP_ROWS, 4 * D)
    attended = lax.map(group_forward, (grouped, segments, present)).reshape(TOKENS, D)
    attend_norm, attend_spread = normalize(attended)
    unit_gate = hidden[:, :D].astype(jnp.float32)
    gated = (attend_norm * unit_gate).astype(jnp.bfloat16)
    layer_sum = jnp.dot(gated, w_out, preferred_element_type=jnp.float32) + action_float
    layer_out = layer_sum.astype(jnp.bfloat16)
    grad_scale = TOKENS ** (-0.5)
    grad_out = jnp.dot(gated.T, out_grad, preferred_element_type=jnp.float32) * grad_scale
    grad_gated = jnp.dot(out_grad, w_out.T, preferred_element_type=jnp.float32)
    grad_attend = norm_back(grad_gated * unit_gate, attend_norm, attend_spread).astype(jnp.bfloat16)
    grad_query, grad_key, grad_value = lax.map(group_backward, (grouped, grad_attend.reshape(GROUPS, GROUP_ROWS, D), segments, present))
    grad_hidden = jnp.concatenate([grad_gated * attend_norm, grad_value.reshape(TOKENS, D), grad_query.reshape(TOKENS, D), grad_key.reshape(TOKENS, D)], axis=1)
    grad_pre = (grad_hidden * silu_slope(pre_act)).astype(jnp.bfloat16)
    grad_in = jnp.dot(normed_low.T, grad_pre, preferred_element_type=jnp.float32) * grad_scale
    grad_normed = jnp.dot(grad_pre, w_in.T, preferred_element_type=jnp.float32)
    grad_action = norm_back(grad_normed, normed, action_spread) + out_grad.astype(jnp.float32)
    row_total = jnp.zeros((ROWS, D), jnp.float32).at[item_row].add(grad_action)
    accum_new = accum + lax.optimization_barrier(jnp.mean(row_total * row_total, axis=1))
    table_new = table - learn_rate * row_total / jnp.sqrt(accum_new)[:, None]
    return (layer_out, table_new, accum_new, grad_in, grad_out)
```

```python
import functools
import math

import jax
import jax.numpy as jnp
from jax import lax
from jax.experimental import pallas as pl
from jax.experimental.pallas import tpu as pltpu
from jax.sharding import PartitionSpec as P

HEADS = 8
NORM_EPS = 1e-05
LEARN_RATE = 0.5
F32, BF16, I32 = jnp.float32, jnp.bfloat16, jnp.int32
VMEM = pltpu.VMEM
BIG = 62 * 1024 * 1024


def whole():
    return pl.BlockSpec(memory_space=pltpu.VMEM)


def params(**kw):
    return pltpu.CompilerParams(vmem_limit_bytes=BIG, **kw)


def dot(a, b):
    return lax.dot_general(a, b, (((1,), (0,)), ((), ())), preferred_element_type=F32)


def dot_t(a, b):
    return lax.dot_general(a, b, (((1,), (1,)), ((), ())), preferred_element_type=F32)


def iota(shape, axis):
    return lax.broadcasted_iota(I32, shape, axis)


def normalize(values):
    row_mean = jnp.mean(values, axis=-1, keepdims=True)
    centred = values - row_mean
    spread = jnp.sqrt(jnp.mean(centred * centred, axis=-1, keepdims=True) + NORM_EPS)
    return centred / spread, spread


def norm_back(grad_rows, normed, spread):
    first = jnp.mean(grad_rows, axis=-1, keepdims=True)
    second = jnp.mean(grad_rows * normed, axis=-1, keepdims=True)
    return (grad_rows - first - normed * second) / spread


def even_half(rows):
    lane = iota(rows.shape, 1) & 127
    return jnp.where(lane < 64, rows, jnp.zeros_like(rows))


def odd_half(rows):
    lane = iota(rows.shape, 1) & 127
    return jnp.where(lane < 64, jnp.zeros_like(rows), rows)


def route_kernel(rows_dev, row_ref, col_ref, seg_ref, pair_ref, req_ref, tr_ref, tc_ref, meta_ref, *, width):
    tokens = row_ref.shape[1]
    shards = req_ref.shape[0]
    shift = rows_dev.bit_length() - 1
    owner_r = row_ref[...] >> shift
    slot_r = (row_ref[...] & (rows_dev - 1)).astype(F32)
    owner_c = col_ref[...] >> shift
    same = owner_c == owner_r
    sub, lane = iota((tokens, tokens), 0), iota((tokens, tokens), 1)
    rank_c = jnp.sum(jnp.where(same & (lane < sub), 1.0, 0.0), axis=1, keepdims=True).astype(I32)
    rank_r = jnp.sum(jnp.where(same & (sub < lane), 1.0, 0.0), axis=0, keepdims=True).astype(I32)
    tr_ref[...] = owner_r * width + rank_r
    tc_ref[...] = owner_c * width + rank_c
    dest = iota((shards, tokens), 0) == owner_r
    place = iota((shards, 128), 1)
    req = jnp.zeros((shards, 128), F32)
    for k in range(2 * tokens // shards):
        picked = jnp.sum(jnp.where(dest & (rank_r == k), slot_r, 0.0), axis=1, keepdims=True)
        req = jnp.where(place == k, picked, req)
    req_ref[...] = req.astype(I32)
    own = lax.axis_index("pair")
    first, second = pair_ref[0:1, :], pair_ref[1:2, :]
    span = iota((8, first.shape[1]), 0)
    as_query = jnp.max(jnp.where((first == own) & (second == span), 1.0, 0.0), axis=1, keepdims=True)
    as_key = jnp.max(jnp.where((second == own) & (first == span), 1.0, 0.0), axis=1, keepdims=True)
    zeros = jnp.sum(jnp.where(seg_ref[...] == 0, 1.0, 0.0), axis=1, keepdims=True)
    at = iota((8, 128), 1)
    meta = jnp.where(at == 0, as_query, jnp.where(at == 1, as_key, jnp.where(at == 2, zeros, 0.0))).astype(I32)
    meta_ref[...] = jnp.where(at == 3, own, meta)


def slot_halves(slots):
    high = (slots >> 1).astype(F32).astype(BF16)
    low = (slots & 1).astype(F32).astype(BF16)
    return high, low


def find_kernel(slots_ref, table_ref, found_ref, *, width):
    shards = slots_ref.shape[0]
    rows_dev = table_ref.shape[0]
    count = shards * width
    spread = ((iota((count, shards), 0) // width) == iota((count, shards), 1)).astype(F32).astype(BF16)
    high, low = slot_halves(slots_ref[...])
    value = 2.0 * dot(spread, high) + dot(spread, low)
    mine = iota((count, 128), 1) == (iota((count, 128), 0) % width)
    slot = jnp.sum(jnp.where(mine, value, 0.0), axis=1, keepdims=True).astype(I32)
    pick = jnp.where(iota((count, rows_dev), 1) == slot, 1.0, 0.0).astype(BF16)
    found_ref[...] = dot(pick, table_ref[...].astype(BF16)).astype(BF16)


def project_kernel(fetched_ref, tc_ref, w_ref, x_ref, z_ref, u_ref, q_ref, kv_ref):
    count, width = fetched_ref.shape
    tokens = tc_ref.shape[0]
    pick = jnp.where(iota((tokens, count), 1) == tc_ref[...], 1.0, 0.0).astype(BF16)
    rows = dot(pick, fetched_ref[...])
    x_ref[...] = rows.astype(BF16)
    normed, _ = normalize(rows)
    low = normed.astype(BF16)
    outs = (u_ref.at[...], kv_ref.at[:, width:], q_ref.at[...], kv_ref.at[:, :width])
    for g in range(4):
        z = dot(low, w_ref[:, g * width : (g + 1) * width])
        z_ref[:, g * width : (g + 1) * width] = z
        half = 0.5 * z
        outs[g][...] = (half + half * jnp.tanh(half)).astype(BF16)


def visible(q_axis, size, q_block, k_block, zeros):
    q_pos = iota((size, size), q_axis) + q_block * size
    k_pos = iota((size, size), 1 - q_axis) + k_block * size
    least = jnp.where(q_pos >= zeros, zeros, 0)
    return jnp.where((k_pos >= least) & (k_pos <= q_pos), 1.0, 0.0)


def pair_live(meta_ref, row, lane, q_block, k_block, size):
    zeros = meta_ref[0, 2]
    apart = ((k_block + 1) * size <= zeros) & (q_block * size >= zeros)
    return (meta_ref[row, lane] == 1) & jnp.logical_not(apart)


def forward_kernel(
    meta_ref, q_ref, kv_ref, u_ref, x_ref, w_ref, og_ref, out_ref, da_ref, dhu_ref, gout_ref, qs, acc, mask
):
    j = pl.program_id(0)
    own = meta_ref[0, 3]
    size, width = q_ref.shape

    @pl.when(j == 0)
    def _():
        scaled = q_ref[...] * 0.0625
        qs[0] = even_half(scaled)
        qs[1] = odd_half(scaled)
        acc[...] = jnp.zeros_like(acc)

    @pl.when((j <= own) & pair_live(meta_ref, j, 0, own, j, size))
    def _():
        mask[...] = visible(0, size, own, j, meta_ref[0, 2])
        for s in range(width // 128):
            cols = slice(s * 128, s * 128 + 128)
            keys = kv_ref[:, cols]
            values = kv_ref[:, width + s * 128 : width + s * 128 + 128]
            weights = []
            for half in range(2):
                h = dot_t(qs[half, :, cols], keys)
                weights.append(((h + h * jnp.tanh(h)) * mask[...]).astype(BF16))
            both = jnp.concatenate([even_half(values), odd_half(values)], axis=0)
            acc[:, cols] += dot(jnp.concatenate(weights, axis=1), both)

    @pl.when(j == pl.num_programs(0) - 1)
    def _():
        normed, spread = normalize(acc[...])
        gate = u_ref[...].astype(F32)
        gated = (normed * gate).astype(BF16)
        out_ref[...] = (dot(gated, w_ref[...]) + x_ref[...].astype(F32)).astype(BF16)
        dy = dot_t(og_ref[...], w_ref[...])
        dhu_ref[...] = dy * normed
        da_ref[...] = norm_back(dy * gate, normed, spread).astype(BF16)
        gout_ref[...] = lax.dot_general(gated, og_ref[...], (((0,), (0,)), ((), ())), preferred_element_type=F32)


def query_kernel(meta_ref, q_ref, da_ref, kv_ref, dq_ref, qs, ds, mask):
    j = pl.program_id(0)
    own = meta_ref[0, 3]
    size, width = q_ref.shape

    @pl.when(j == 0)
    def _():
        scaled = q_ref[...] * 0.0625
        qs[0] = even_half(scaled)
        qs[1] = odd_half(scaled)
        scaled = da_ref[...] * 0.0625
        ds[0] = even_half(scaled)
        ds[1] = odd_half(scaled)
        dq_ref[...] = jnp.zeros_like(dq_ref)

    @pl.when((j <= own) & pair_live(meta_ref, j, 0, own, j, size))
    def _():
        mask[...] = visible(0, size, own, j, meta_ref[0, 2])
        for s in range(width // 128):
            cols = slice(s * 128, s * 128 + 128)
            keys = kv_ref[:, cols]
            values = kv_ref[:, width + s * 128 : width + s * 128 + 128]
            grads = []
            for half in range(2):
                h = dot_t(qs[half, :, cols], keys)
                t = jnp.tanh(h)
                slope = (1.0 + t) * (1.0 + h * (1.0 - t))
                grads.append((dot_t(ds[half, :, cols], values) * slope * mask[...]).astype(BF16))
            both = jnp.concatenate([even_half(keys), odd_half(keys)], axis=0)
            dq_ref[:, cols] += dot(jnp.concatenate(grads, axis=1), both)


def key_kernel(meta_ref, kv_ref, q_ref, da_ref, dk_ref, dv_ref, ks, vs, mask):
    i = pl.program_id(0)
    own = meta_ref[0, 3]
    size, width = q_ref.shape

    @pl.when(i == 0)
    def _():
        scaled = kv_ref[...] * 0.0625
        ks[0] = even_half(scaled[:, :width])
        ks[1] = odd_half(scaled[:, :width])
        vs[0] = even_half(scaled[:, width:])
        vs[1] = odd_half(scaled[:, width:])
        dk_ref[...] = jnp.zeros_like(dk_ref)
        dv_ref[...] = jnp.zeros_like(dv_ref)

    @pl.when((i >= own) & pair_live(meta_ref, i, 1, i, own, size))
    def _():
        mask[...] = visible(1, size, i, own, meta_ref[0, 2])
        for s in range(width // 128):
            cols = slice(s * 128, s * 128 + 128)
            queries = q_ref[:, cols]
            dafter = da_ref[:, cols]
            grads, weights = [], []
            for half in range(2):
                h = dot_t(ks[half, :, cols], queries)
                t = jnp.tanh(h)
                weights.append(((h + h * t) * mask[...]).astype(BF16))
                slope = (1.0 + t) * (1.0 + h * (1.0 - t))
                grads.append((dot_t(vs[half, :, cols], dafter) * slope * mask[...]).astype(BF16))
            q_both = jnp.concatenate([even_half(queries), odd_half(queries)], axis=0)
            a_both = jnp.concatenate([even_half(dafter), odd_half(dafter)], axis=0)
            dk_ref[:, cols] += dot(jnp.concatenate(grads, axis=1), q_both)
            dv_ref[:, cols] += dot(jnp.concatenate(weights, axis=1), a_both)


def finish_kernel(z_ref, dhu_ref, dv_ref, dq_ref, dk_ref, x_ref, w_ref, og_ref, tr_ref, gout_ref, grads_ref, send_ref):
    size, width = x_ref.shape
    normed, spread = normalize(x_ref[...].astype(F32))
    turned = jnp.transpose(normed).astype(BF16)
    dxn = jnp.zeros((size, width), F32)
    for g, grad in enumerate((dhu_ref, dv_ref, dq_ref, dk_ref)):
        cols = slice(g * width, (g + 1) * width)
        h = 0.5 * z_ref[:, cols]
        t = jnp.tanh(h)
        slope = 0.5 * (1.0 + t) * (1.0 + h * (1.0 - t))
        dz = (grad[...] * slope).astype(BF16)
        grads_ref[:, cols] = dot(turned, dz)
        dxn += dot_t(dz, w_ref[:, cols])
    grads_ref[:, 4 * width :] = gout_ref[...]
    dx = norm_back(dxn, normed, spread) + og_ref[...].astype(F32)
    count = send_ref.shape[0]
    pick = jnp.where(iota((count, size), 0) == tr_ref[...], 1.0, 0.0).astype(BF16)
    send_ref[...] = dot(pick, dx.astype(BF16)).astype(BF16)


def update_kernel(slots_ref, back_ref, table_ref, accum_ref, tnew_ref, anew_ref, *, width):
    shards = slots_ref.shape[0]
    rows_dev, model = table_ref.shape
    count = shards * width
    spread = ((iota((shards, count), 1) // width) == iota((shards, count), 0)).astype(F32).astype(BF16)
    high, low = slot_halves(slots_ref[...])
    turn = lambda a: lax.dot_general(a, spread, (((0,), (0,)), ((), ())), preferred_element_type=F32)
    value = 2.0 * turn(high) + turn(low)
    mine = iota((128, count), 0) == (iota((128, count), 1) % width)
    slot = jnp.sum(jnp.where(mine, value, 0.0), axis=0, keepdims=True).astype(I32)
    pick = jnp.where(iota((rows_dev, count), 0) == slot, 1.0, 0.0).astype(BF16)
    total = dot(pick, back_ref[...])
    square = jnp.mean(total * total, axis=1, keepdims=True)
    eye = iota((rows_dev, rows_dev), 0) == iota((rows_dev, rows_dev), 1)
    accum = jnp.sum(jnp.where(eye, accum_ref[...], 0.0), axis=1, keepdims=True) + square
    anew_ref[...] = jnp.sum(jnp.where(eye, accum, 0.0), axis=0, keepdims=True)
    tnew_ref[...] = table_ref[...] - LEARN_RATE * total / jnp.sqrt(accum)


def shape(dims, dtype):
    return jax.ShapeDtypeStruct(dims, dtype)


def cost(flops, moved):
    return pl.CostEstimate(flops=flops, bytes_accessed=moved, transcendentals=0)


def body(table, accum, item_row, segments, pairs, w_in, w_out, out_grad):
    tokens = item_row.shape[0]
    rows_dev, model = table.shape
    shards = lax.axis_size(("dp", "pair"))
    span = lax.axis_size("pair")
    width = -(-(2 * tokens // shards) // 8) * 8
    count = shards * width
    everyone = ("dp", "pair")

    call = pl.pallas_call(
        functools.partial(route_kernel, rows_dev, width=width),
        out_shape=(
            shape((shards, 128), I32),
            shape((1, tokens), I32),
            shape((tokens, 1), I32),
            shape((8, 128), I32),
        ),
        in_specs=[whole()] * 4,
        out_specs=[whole()] * 4,
        compiler_params=params(),
    )
    request, target_r, target_c, meta = call(
        item_row.reshape(1, tokens), item_row.reshape(tokens, 1), segments, pairs[0].T
    )
    asked = lax.all_to_all(request[:, :width], everyone, split_axis=0, concat_axis=0, tiled=True)
    slots = jnp.pad(asked, ((0, 0), (0, 128 - width)))
    found = pl.pallas_call(
        functools.partial(find_kernel, width=width),
        out_shape=shape((count, model), BF16),
        in_specs=[whole()] * 2,
        out_specs=whole(),
        compiler_params=params(),
    )(slots, table)
    fetched = lax.all_to_all(
        found.reshape(shards, width, model), everyone, split_axis=0, concat_axis=0, tiled=True
    ).reshape(count, model)
    x, z, u, q, kv = pl.pallas_call(
        project_kernel,
        out_shape=(
            shape((tokens, model), BF16),
            shape((tokens, 4 * model), F32),
            shape((tokens, model), BF16),
            shape((tokens, model), BF16),
            shape((tokens, 2 * model), BF16),
        ),
        in_specs=[whole()] * 3,
        out_specs=[whole()] * 5,
        compiler_params=params(),
    )(fetched, target_c, w_in)

    kv_all = lax.all_gather(kv, "pair", axis=0, tiled=True)
    q_all = lax.all_gather(q, "pair", axis=0, tiled=True)

    fixed = lambda cols: pl.BlockSpec((tokens, cols), lambda i, m: (0, 0))
    square = lambda rows, cols: pl.BlockSpec((rows, cols), lambda i, m: (0, 0))
    low_half = lambda cols: pl.BlockSpec((tokens, cols), lambda i, m: (jnp.minimum(i, m[0, 3]), 0))
    high_half = lambda cols: pl.BlockSpec((tokens, cols), lambda i, m: (jnp.maximum(i, m[0, 3]), 0))
    halves = VMEM((2, tokens, model), BF16)
    grid_spec = lambda ins, outs, scratch: pltpu.PrefetchScalarGridSpec(
        num_scalar_prefetch=1, grid=(span,), in_specs=ins, out_specs=outs, scratch_shapes=scratch
    )
    pair_flops = 2 * tokens * tokens * model * span
    layer_out, da, dhu, gout = pl.pallas_call(
        forward_kernel,
        out_shape=(
            shape((tokens, model), BF16),
            shape((tokens, model), BF16),
            shape((tokens, model), F32),
            shape((model, model), F32),
        ),
        grid_spec=grid_spec(
            [fixed(model), low_half(2 * model), fixed(model), fixed(model), square(model, model), fixed(model)],
            [fixed(model), fixed(model), fixed(model), square(model, model)],
            [halves, VMEM((tokens, model), F32), VMEM((tokens, tokens), F32)],
        ),
        compiler_params=params(),
        cost_estimate=cost(8 * pair_flops, 6 * 2**20),
    )(meta, q, kv_all, u, x, w_out, out_grad)

    da_all = lax.all_gather(da, "pair", axis=0, tiled=True)
    dq = pl.pallas_call(
        query_kernel,
        out_shape=shape((tokens, model), F32),
        grid_spec=grid_spec(
            [fixed(model), fixed(model), low_half(2 * model)],
            fixed(model),
            [halves, halves, VMEM((tokens, tokens), F32)],
        ),
        compiler_params=params(),
        cost_estimate=cost(12 * pair_flops, 6 * 2**20),
    )(meta, q, da, kv_all)
    dk, dv = pl.pallas_call(
        key_kernel,
        out_shape=(shape((tokens, model), F32), shape((tokens, model), F32)),
        grid_spec=grid_spec(
            [fixed(2 * model), high_half(model), high_half(model)],
            [fixed(model), fixed(model)],
            [halves, halves, VMEM((tokens, tokens), F32)],
        ),
        compiler_params=params(),
        cost_estimate=cost(16 * pair_flops, 6 * 2**20),
    )(meta, kv, q_all, da_all)

    grads, send = pl.pallas_call(
        finish_kernel,
        out_shape=(shape((model, 5 * model), F32), shape((count, model), BF16)),
        in_specs=[whole()] * 10,
        out_specs=[whole()] * 2,
        compiler_params=params(),
    )(z, dhu, dv, dq, dk, x, w_in, out_grad, target_r, gout)
    combined = lax.psum_scatter(grads, "dp", scatter_dimension=0, tiled=True)
    combined = lax.psum_scatter(combined, "pair", scatter_dimension=0, tiled=True)
    factor = 1.0 / math.sqrt(tokens * shards)
    back = lax.all_to_all(
        send.reshape(shards, width, model), everyone, split_axis=0, concat_axis=0, tiled=True
    ).reshape(count, model)
    table_new, accum_new = pl.pallas_call(
        functools.partial(update_kernel, width=width),
        out_shape=(shape((rows_dev, model), F32), shape((1, rows_dev), F32)),
        in_specs=[whole()] * 4,
        out_specs=[whole()] * 2,
        compiler_params=params(),
    )(slots, back, table, accum.reshape(1, rows_dev))
    return (
        layer_out,
        table_new,
        accum_new.reshape(rows_dev),
        combined[:, : 4 * model] * factor,
        combined[:, 4 * model :] * factor,
    )


def solution(mesh):
    both = ("dp", "pair")
    return jax.shard_map(
        body,
        mesh=mesh,
        in_specs=(
            P(both, None),
            P(both),
            P(both),
            P("dp", None),
            P("dp", None, None),
            P(),
            P(),
            P(both, None),
        ),
        out_specs=(P(both, None), P(both, None), P(both), P(both, None), P(both, None)),
        check_vma=False,
    )
```

```python
import functools
import math

import jax
import jax.numpy as jnp
from jax import lax
from jax.experimental import pallas as pl
from jax.experimental.pallas import tpu as pltpu
from jax.sharding import PartitionSpec as P

HEADS = 8
NORM_EPS = 1e-05
LEARN_RATE = 0.5
F32, BF16, I32 = jnp.float32, jnp.bfloat16, jnp.int32
VMEM = pltpu.VMEM
MESH = pl.DeviceIdType.MESH
BIG = 62 * 1024 * 1024


def whole():
    return pl.BlockSpec(memory_space=pltpu.VMEM)


def params(**kw):
    return pltpu.CompilerParams(vmem_limit_bytes=BIG, **kw)


def dot(a, b):
    return lax.dot_general(a, b, (((1,), (0,)), ((), ())), preferred_element_type=F32)


def dot_t(a, b):
    return lax.dot_general(a, b, (((1,), (1,)), ((), ())), preferred_element_type=F32)


def iota(shape, axis):
    return lax.broadcasted_iota(I32, shape, axis)


def normalize(values):
    row_mean = jnp.mean(values, axis=-1, keepdims=True)
    centred = values - row_mean
    spread = jnp.sqrt(jnp.mean(centred * centred, axis=-1, keepdims=True) + NORM_EPS)
    return centred / spread, spread


def norm_back(grad_rows, normed, spread):
    first = jnp.mean(grad_rows, axis=-1, keepdims=True)
    second = jnp.mean(grad_rows * normed, axis=-1, keepdims=True)
    return (grad_rows - first - normed * second) / spread


def even_half(rows):
    lane = iota(rows.shape, 1) & 127
    return jnp.where(lane < 64, rows, jnp.zeros_like(rows))


def odd_half(rows):
    lane = iota(rows.shape, 1) & 127
    return jnp.where(lane < 64, jnp.zeros_like(rows), rows)


def route_kernel(rows_dev, row_ref, col_ref, seg_ref, pair_ref, req_ref, tr_ref, tc_ref, meta_ref, *, width):
    tokens = row_ref.shape[1]
    shards = req_ref.shape[0]
    shift = rows_dev.bit_length() - 1
    owner_r = row_ref[...] >> shift
    slot_r = (row_ref[...] & (rows_dev - 1)).astype(F32)
    owner_c = col_ref[...] >> shift
    same = owner_c == owner_r
    sub, lane = iota((tokens, tokens), 0), iota((tokens, tokens), 1)
    rank_c = jnp.sum(jnp.where(same & (lane < sub), 1.0, 0.0), axis=1, keepdims=True).astype(I32)
    rank_r = jnp.sum(jnp.where(same & (sub < lane), 1.0, 0.0), axis=0, keepdims=True).astype(I32)
    tr_ref[...] = owner_r * width + rank_r
    tc_ref[...] = owner_c * width + rank_c
    dest = iota((shards, tokens), 0) == owner_r
    place = iota((shards, 128), 1)
    req = jnp.zeros((shards, 128), F32)
    for k in range(2 * tokens // shards):
        picked = jnp.sum(jnp.where(dest & (rank_r == k), slot_r, 0.0), axis=1, keepdims=True)
        req = jnp.where(place == k, picked, req)
    req_ref[...] = req.astype(I32)
    own = lax.axis_index("pair")
    first, second = pair_ref[0:1, :], pair_ref[1:2, :]
    span = iota((8, first.shape[1]), 0)
    as_query = jnp.max(jnp.where((first == own) & (second == span), 1.0, 0.0), axis=1, keepdims=True)
    as_key = jnp.max(jnp.where((second == own) & (first == span), 1.0, 0.0), axis=1, keepdims=True)
    zeros = jnp.sum(jnp.where(seg_ref[...] == 0, 1.0, 0.0), axis=1, keepdims=True)
    at = iota((8, 128), 1)
    meta = jnp.where(at == 0, as_query, jnp.where(at == 1, as_key, jnp.where(at == 2, zeros, 0.0))).astype(I32)
    meta_ref[...] = jnp.where(at == 3, own, meta)


def slot_halves(slots):
    high = (slots >> 1).astype(F32).astype(BF16)
    low = (slots & 1).astype(F32).astype(BF16)
    return high, low


def find_kernel(slots_ref, table_ref, found_ref, *, width):
    shards = slots_ref.shape[0]
    rows_dev = table_ref.shape[0]
    count = shards * width
    spread = ((iota((count, shards), 0) // width) == iota((count, shards), 1)).astype(F32).astype(BF16)
    high, low = slot_halves(slots_ref[...])
    value = 2.0 * dot(spread, high) + dot(spread, low)
    mine = iota((count, 128), 1) == (iota((count, 128), 0) % width)
    slot = jnp.sum(jnp.where(mine, value, 0.0), axis=1, keepdims=True).astype(I32)
    pick = jnp.where(iota((count, rows_dev), 1) == slot, 1.0, 0.0).astype(BF16)
    found_ref[...] = dot(pick, table_ref[...].astype(BF16)).astype(BF16)


def project_kernel(fetched_ref, tc_ref, w_ref, x_ref, z_ref, u_ref, q_ref, kv_ref):
    count, width = fetched_ref.shape
    tokens = tc_ref.shape[0]
    pick = jnp.where(iota((tokens, count), 1) == tc_ref[...], 1.0, 0.0).astype(BF16)
    rows = dot(pick, fetched_ref[...])
    x_ref[...] = rows.astype(BF16)
    normed, _ = normalize(rows)
    low = normed.astype(BF16)
    outs = (u_ref.at[...], kv_ref.at[:, width:], q_ref.at[...], kv_ref.at[:, :width])
    for g in range(4):
        z = dot(low, w_ref[:, g * width : (g + 1) * width])
        z_ref[:, g * width : (g + 1) * width] = z
        half = 0.5 * z
        outs[g][...] = (half + half * jnp.tanh(half)).astype(BF16)


def visible(q_axis, size, q_block, k_block, zeros):
    q_pos = iota((size, size), q_axis) + q_block * size
    k_pos = iota((size, size), 1 - q_axis) + k_block * size
    least = jnp.where(q_pos >= zeros, zeros, 0)
    return jnp.where((k_pos >= least) & (k_pos <= q_pos), 1.0, 0.0)


def pair_live(meta_ref, row, lane, q_block, k_block, size):
    zeros = meta_ref[0, 2]
    apart = ((k_block + 1) * size <= zeros) & (q_block * size >= zeros)
    return (meta_ref[row, lane] == 1) & jnp.logical_not(apart)


def forward_kernel(
    meta_ref, q_ref, kv_ref, u_ref, x_ref, w_ref, og_ref, out_ref, da_ref, dhu_ref, gout_ref, qs, acc, mask
):
    j = pl.program_id(0)
    own = meta_ref[0, 3]
    size, width = q_ref.shape

    @pl.when(j == 0)
    def _():
        scaled = q_ref[...] * 0.0625
        qs[0] = even_half(scaled)
        qs[1] = odd_half(scaled)
        acc[...] = jnp.zeros_like(acc)

    @pl.when((j <= own) & pair_live(meta_ref, j, 0, own, j, size))
    def _():
        mask[...] = visible(0, size, own, j, meta_ref[0, 2])
        for s in range(width // 128):
            cols = slice(s * 128, s * 128 + 128)
            keys = kv_ref[:, cols]
            values = kv_ref[:, width + s * 128 : width + s * 128 + 128]
            weights = []
            for half in range(2):
                h = dot_t(qs[half, :, cols], keys)
                weights.append(((h + h * jnp.tanh(h)) * mask[...]).astype(BF16))
            both = jnp.concatenate([even_half(values), odd_half(values)], axis=0)
            acc[:, cols] += dot(jnp.concatenate(weights, axis=1), both)

    @pl.when(j == pl.num_programs(0) - 1)
    def _():
        normed, spread = normalize(acc[...])
        gate = u_ref[...].astype(F32)
        gated = (normed * gate).astype(BF16)
        out_ref[...] = (dot(gated, w_ref[...]) + x_ref[...].astype(F32)).astype(BF16)
        dy = dot_t(og_ref[...], w_ref[...])
        dhu_ref[...] = dy * normed
        da_ref[...] = norm_back(dy * gate, normed, spread).astype(BF16)
        gout_ref[...] = lax.dot_general(gated, og_ref[...], (((0,), (0,)), ((), ())), preferred_element_type=F32)


def query_kernel(meta_ref, q_ref, da_ref, kv_ref, dq_ref, qs, ds, mask):
    j = pl.program_id(0)
    own = meta_ref[0, 3]
    size, width = q_ref.shape

    @pl.when(j == 0)
    def _():
        scaled = q_ref[...] * 0.0625
        qs[0] = even_half(scaled)
        qs[1] = odd_half(scaled)
        scaled = da_ref[...] * 0.0625
        ds[0] = even_half(scaled)
        ds[1] = odd_half(scaled)
        dq_ref[...] = jnp.zeros_like(dq_ref)

    @pl.when((j <= own) & pair_live(meta_ref, j, 0, own, j, size))
    def _():
        mask[...] = visible(0, size, own, j, meta_ref[0, 2])
        for s in range(width // 128):
            cols = slice(s * 128, s * 128 + 128)
            keys = kv_ref[:, cols]
            values = kv_ref[:, width + s * 128 : width + s * 128 + 128]
            grads = []
            for half in range(2):
                h = dot_t(qs[half, :, cols], keys)
                t = jnp.tanh(h)
                slope = (1.0 + t) * (1.0 + h * (1.0 - t))
                grads.append((dot_t(ds[half, :, cols], values) * slope * mask[...]).astype(BF16))
            both = jnp.concatenate([even_half(keys), odd_half(keys)], axis=0)
            dq_ref[:, cols] += dot(jnp.concatenate(grads, axis=1), both)


def key_kernel(meta_ref, kv_ref, q_ref, da_ref, dk_ref, dv_ref, ks, vs, mask):
    i = pl.program_id(0)
    own = meta_ref[0, 3]
    size, width = q_ref.shape

    @pl.when(i == 0)
    def _():
        scaled = kv_ref[...] * 0.0625
        ks[0] = even_half(scaled[:, :width])
        ks[1] = odd_half(scaled[:, :width])
        vs[0] = even_half(scaled[:, width:])
        vs[1] = odd_half(scaled[:, width:])
        dk_ref[...] = jnp.zeros_like(dk_ref)
        dv_ref[...] = jnp.zeros_like(dv_ref)

    @pl.when((i >= own) & pair_live(meta_ref, i, 1, i, own, size))
    def _():
        mask[...] = visible(1, size, i, own, meta_ref[0, 2])
        for s in range(width // 128):
            cols = slice(s * 128, s * 128 + 128)
            queries = q_ref[:, cols]
            dafter = da_ref[:, cols]
            grads, weights = [], []
            for half in range(2):
                h = dot_t(ks[half, :, cols], queries)
                t = jnp.tanh(h)
                weights.append(((h + h * t) * mask[...]).astype(BF16))
                slope = (1.0 + t) * (1.0 + h * (1.0 - t))
                grads.append((dot_t(vs[half, :, cols], dafter) * slope * mask[...]).astype(BF16))
            q_both = jnp.concatenate([even_half(queries), odd_half(queries)], axis=0)
            a_both = jnp.concatenate([even_half(dafter), odd_half(dafter)], axis=0)
            dk_ref[:, cols] += dot(jnp.concatenate(grads, axis=1), q_both)
            dv_ref[:, cols] += dot(jnp.concatenate(weights, axis=1), a_both)


def finish_kernel(
    z_ref, dhu_ref, dv_ref, dq_ref, dk_ref, x_ref, w_ref, og_ref, tr_ref, gout_ref, grads_ref, send_ref, hold, *, rows
):
    size, width = x_ref.shape
    normed, spread = normalize(x_ref[...].astype(F32))
    turned = jnp.transpose(normed).astype(BF16)
    dxn = jnp.zeros((size, width), F32)

    def place(upper, lower, at):
        count, cols = upper.shape
        top = (iota((count, cols), 0) % (2 * rows)) < rows
        first = jnp.where(top, upper, pltpu.roll(lower, rows, 0))
        second = jnp.where(top, pltpu.roll(upper, count - rows, 0), lower)
        whole_shape = (count // (2 * rows), 2 * rows, cols)
        grads_ref[0, :, :, at : at + cols] = first.reshape(whole_shape)
        grads_ref[1, :, :, at : at + cols] = second.reshape(whole_shape)

    for g, grad in enumerate((dhu_ref, dv_ref, dq_ref, dk_ref)):
        cols = slice(g * width, (g + 1) * width)
        h = 0.5 * z_ref[:, cols]
        t = jnp.tanh(h)
        slope = 0.5 * (1.0 + t) * (1.0 + h * (1.0 - t))
        dz = (grad[...] * slope).astype(BF16)
        part = dot(turned, dz)
        if g == 0:
            hold[...] = part
        elif g == 1:
            place(part, gout_ref[...], width)
        elif g == 2:
            place(part[:, : width // 2], part[:, width // 2 :], 2 * width)
        else:
            place(hold[...], part, 0)
        dxn += dot_t(dz, w_ref[:, cols])
    dx = norm_back(dxn, normed, spread) + og_ref[...].astype(F32)
    count = send_ref.shape[0]
    pick = jnp.where(iota((count, size), 0) == tr_ref[...], 1.0, 0.0).astype(BF16)
    send_ref[...] = dot(pick, dx.astype(BF16)).astype(BF16)


def partner(k, groups, span):
    g, p = lax.axis_index("dp"), lax.axis_index("pair")
    chips, side = span // 2, math.isqrt(groups)
    to_p = ((p // 2 + (k // 2) % chips) % chips) * 2 + (p % 2 + k % 2) % 2
    shift = k // span
    to_g = ((g // side + shift // side) % side) * side + (g % side + shift % side) % side
    return to_g, to_p


def greet(groups, span):
    barrier = pltpu.get_barrier_semaphore()

    def hello(k, carry):
        pl.semaphore_signal(barrier, inc=1, device_id=partner(k, groups, span), device_id_type=MESH)
        return carry

    lax.fori_loop(1, groups * span, hello, 0)
    pl.semaphore_wait(barrier, groups * span - 1)


def drain(ref, count, sem):
    part = ref.at[pl.ds(0, count)]
    pltpu.make_async_copy(part, part, sem).wait()


def tail_kernel(rows_ref, grads_ref, back_ref, parts_ref, got, part, sems, *, groups, span):
    total = groups * span
    g, p = lax.axis_index("dp"), lax.axis_index("pair")
    me, core = g * span + p, p % 2
    chip, chips = me // 2, total // 2
    own = pltpu.make_async_copy(rows_ref.at[me], back_ref.at[me], sems.at[0])
    own.start()
    greet(groups, span)
    swap = pltpu.make_async_remote_copy(
        src_ref=grads_ref.at[1 - core],
        dst_ref=got,
        send_sem=sems.at[1],
        recv_sem=sems.at[2],
        device_id=(g, p + 1 - 2 * core),
        device_id_type=MESH,
    )
    swap.start()

    def push_rows(k, carry):
        to_g, to_p = partner(k, groups, span)
        pltpu.make_async_remote_copy(
            src_ref=rows_ref.at[to_g * span + to_p],
            dst_ref=back_ref.at[me],
            send_sem=sems.at[3],
            recv_sem=sems.at[4],
            device_id=(to_g, to_p),
            device_id_type=MESH,
        ).start()
        return carry

    lax.fori_loop(1, total, push_rows, 0)
    swap.wait()

    def add(m, carry):
        part[m] = (grads_ref[core, m] + got[m]).astype(BF16)
        return carry

    lax.fori_loop(0, chips, add, 0)
    mine = pltpu.make_async_copy(part.at[chip], parts_ref.at[chip], sems.at[5])
    mine.start()

    def push_part(k, carry):
        to_g, to_p = partner(2 * k, groups, span)
        pltpu.make_async_remote_copy(
            src_ref=part.at[(to_g * span + to_p) // 2],
            dst_ref=parts_ref.at[chip],
            send_sem=sems.at[6],
            recv_sem=sems.at[7],
            device_id=(to_g, to_p),
            device_id_type=MESH,
        ).start()
        return carry

    lax.fori_loop(1, chips, push_part, 0)
    own.wait()
    mine.wait()
    drain(back_ref, total - 1, sems.at[3])
    drain(back_ref, total - 1, sems.at[4])
    drain(parts_ref, chips - 1, sems.at[6])
    drain(parts_ref, chips - 1, sems.at[7])


def update_kernel(
    slots_ref, back_ref, table_ref, accum_ref, parts_ref, tnew_ref, anew_ref, gin_ref, gout_ref, *, width, factor
):
    shards = slots_ref.shape[0]
    rows_dev, model = table_ref.shape
    count = shards * width
    spread = ((iota((shards, count), 1) // width) == iota((shards, count), 0)).astype(F32).astype(BF16)
    high, low = slot_halves(slots_ref[...])
    turn = lambda a: lax.dot_general(a, spread, (((0,), (0,)), ((), ())), preferred_element_type=F32)
    value = 2.0 * turn(high) + turn(low)
    mine = iota((128, count), 0) == (iota((128, count), 1) % width)
    slot = jnp.sum(jnp.where(mine, value, 0.0), axis=0, keepdims=True).astype(I32)
    pick = jnp.where(iota((rows_dev, count), 0) == slot, 1.0, 0.0).astype(BF16)
    total = dot(pick, back_ref[...])
    square = jnp.mean(total * total, axis=1, keepdims=True)
    eye = iota((rows_dev, rows_dev), 0) == iota((rows_dev, rows_dev), 1)
    accum = jnp.sum(jnp.where(eye, accum_ref[...], 0.0), axis=1, keepdims=True) + square
    anew_ref[...] = jnp.sum(jnp.where(eye, accum, 0.0), axis=0, keepdims=True)
    tnew_ref[...] = table_ref[...] - LEARN_RATE * total / jnp.sqrt(accum)

    def add(m, summed):
        return summed + parts_ref[m].astype(F32)

    summed = lax.fori_loop(0, parts_ref.shape[0], add, jnp.zeros(parts_ref.shape[1:], F32)) * factor
    rows = gin_ref.shape[0]
    upper, lower = summed[:rows], summed[rows:]
    gin_ref[:, :model] = upper[:, :model]
    gin_ref[:, model : 2 * model] = upper[:, model : 2 * model]
    gin_ref[:, 2 * model : 2 * model + model // 2] = upper[:, 2 * model :]
    gin_ref[:, 2 * model + model // 2 : 3 * model] = lower[:, 2 * model :]
    gin_ref[:, 3 * model :] = lower[:, :model]
    gout_ref[...] = lower[:, model : 2 * model]


def shape(dims, dtype):
    return jax.ShapeDtypeStruct(dims, dtype)


def cost(flops, moved):
    return pl.CostEstimate(flops=flops, bytes_accessed=moved, transcendentals=0)


def body(table, accum, item_row, segments, pairs, w_in, w_out, out_grad):
    tokens = item_row.shape[0]
    rows_dev, model = table.shape
    shards = lax.axis_size(("dp", "pair"))
    span = lax.axis_size("pair")
    width = -(-(2 * tokens // shards) // 8) * 8
    count = shards * width
    everyone = ("dp", "pair")

    call = pl.pallas_call(
        functools.partial(route_kernel, rows_dev, width=width),
        out_shape=(
            shape((shards, 128), I32),
            shape((1, tokens), I32),
            shape((tokens, 1), I32),
            shape((8, 128), I32),
        ),
        in_specs=[whole()] * 4,
        out_specs=[whole()] * 4,
        compiler_params=params(),
    )
    request, target_r, target_c, meta = call(
        item_row.reshape(1, tokens), item_row.reshape(tokens, 1), segments, pairs[0].T
    )
    asked = lax.all_to_all(request[:, :width], everyone, split_axis=0, concat_axis=0, tiled=True)
    slots = jnp.pad(asked, ((0, 0), (0, 128 - width)))
    found = pl.pallas_call(
        functools.partial(find_kernel, width=width),
        out_shape=shape((count, model), BF16),
        in_specs=[whole()] * 2,
        out_specs=whole(),
        compiler_params=params(),
    )(slots, table)
    fetched = lax.all_to_all(
        found.reshape(shards, width, model), everyone, split_axis=0, concat_axis=0, tiled=True
    ).reshape(count, model)
    x, z, u, q, kv = pl.pallas_call(
        project_kernel,
        out_shape=(
            shape((tokens, model), BF16),
            shape((tokens, 4 * model), F32),
            shape((tokens, model), BF16),
            shape((tokens, model), BF16),
            shape((tokens, 2 * model), BF16),
        ),
        in_specs=[whole()] * 3,
        out_specs=[whole()] * 5,
        compiler_params=params(),
    )(fetched, target_c, w_in)

    kv_all = lax.all_gather(kv, "pair", axis=0, tiled=True)
    q_all = lax.all_gather(q, "pair", axis=0, tiled=True)

    fixed = lambda cols: pl.BlockSpec((tokens, cols), lambda i, m: (0, 0))
    square = lambda rows, cols: pl.BlockSpec((rows, cols), lambda i, m: (0, 0))
    low_half = lambda cols: pl.BlockSpec((tokens, cols), lambda i, m: (jnp.minimum(i, m[0, 3]), 0))
    high_half = lambda cols: pl.BlockSpec((tokens, cols), lambda i, m: (jnp.maximum(i, m[0, 3]), 0))
    halves = VMEM((2, tokens, model), BF16)
    grid_spec = lambda ins, outs, scratch: pltpu.PrefetchScalarGridSpec(
        num_scalar_prefetch=1, grid=(span,), in_specs=ins, out_specs=outs, scratch_shapes=scratch
    )
    pair_flops = 2 * tokens * tokens * model * span
    layer_out, da, dhu, gout = pl.pallas_call(
        forward_kernel,
        out_shape=(
            shape((tokens, model), BF16),
            shape((tokens, model), BF16),
            shape((tokens, model), F32),
            shape((model, model), F32),
        ),
        grid_spec=grid_spec(
            [fixed(model), low_half(2 * model), fixed(model), fixed(model), square(model, model), fixed(model)],
            [fixed(model), fixed(model), fixed(model), square(model, model)],
            [halves, VMEM((tokens, model), F32), VMEM((tokens, tokens), F32)],
        ),
        compiler_params=params(),
        cost_estimate=cost(8 * pair_flops, 6 * 2**20),
    )(meta, q, kv_all, u, x, w_out, out_grad)

    da_all = lax.all_gather(da, "pair", axis=0, tiled=True)
    dq = pl.pallas_call(
        query_kernel,
        out_shape=shape((tokens, model), F32),
        grid_spec=grid_spec(
            [fixed(model), fixed(model), low_half(2 * model)],
            fixed(model),
            [halves, halves, VMEM((tokens, tokens), F32)],
        ),
        compiler_params=params(),
        cost_estimate=cost(12 * pair_flops, 6 * 2**20),
    )(meta, q, da, kv_all)
    dk, dv = pl.pallas_call(
        key_kernel,
        out_shape=(shape((tokens, model), F32), shape((tokens, model), F32)),
        grid_spec=grid_spec(
            [fixed(2 * model), high_half(model), high_half(model)],
            [fixed(model), fixed(model)],
            [halves, halves, VMEM((tokens, tokens), F32)],
        ),
        compiler_params=params(),
        cost_estimate=cost(16 * pair_flops, 6 * 2**20),
    )(meta, kv, q_all, da_all)

    rows = model // shards
    chunk = (2 * rows, 5 * model // 2)
    grads, send = pl.pallas_call(
        functools.partial(finish_kernel, rows=rows),
        out_shape=(shape((2, shards // 2) + chunk, F32), shape((count, model), BF16)),
        in_specs=[whole()] * 10,
        out_specs=[whole()] * 2,
        scratch_shapes=[VMEM((model, model), F32)],
        compiler_params=params(),
    )(z, dhu, dv, dq, dk, x, w_in, out_grad, target_r, gout)
    back, parts = pl.pallas_call(
        functools.partial(tail_kernel, groups=shards // span, span=span),
        out_shape=(shape((shards, width, model), BF16), shape((shards // 2,) + chunk, BF16)),
        in_specs=[whole()] * 2,
        out_specs=[whole()] * 2,
        scratch_shapes=[
            VMEM((shards // 2,) + chunk, F32),
            VMEM((shards // 2,) + chunk, BF16),
            pltpu.SemaphoreType.DMA((8,)),
        ],
        compiler_params=params(collective_id=0, has_side_effects=True),
    )(send.reshape(shards, width, model), grads)
    table_new, accum_new, grad_in, grad_out = pl.pallas_call(
        functools.partial(update_kernel, width=width, factor=1.0 / math.sqrt(tokens * shards)),
        out_shape=(
            shape((rows_dev, model), F32),
            shape((1, rows_dev), F32),
            shape((rows, 4 * model), F32),
            shape((rows, model), F32),
        ),
        in_specs=[whole()] * 5,
        out_specs=[whole()] * 4,
        compiler_params=params(),
    )(slots, back.reshape(count, model), table, accum.reshape(1, rows_dev), parts)
    return layer_out, table_new, accum_new.reshape(rows_dev), grad_in, grad_out


def solution(mesh):
    both = ("dp", "pair")
    return jax.shard_map(
        body,
        mesh=mesh,
        in_specs=(
            P(both, None),
            P(both),
            P(both),
            P("dp", None),
            P("dp", None, None),
            P(),
            P(),
            P(both, None),
        ),
        out_specs=(P(both, None), P(both, None), P(both), P(both, None), P(both, None)),
        check_vma=False,
    )
```

```python
import functools
import math

import jax
import jax.numpy as jnp
from jax import lax
from jax.experimental import pallas as pl
from jax.experimental.pallas import tpu as pltpu
from jax.sharding import PartitionSpec as P

HEADS = 8
NORM_EPS = 1e-05
LEARN_RATE = 0.5
F32, BF16, I32 = jnp.float32, jnp.bfloat16, jnp.int32
VMEM = pltpu.VMEM
MESH = pl.DeviceIdType.MESH
BIG = 62 * 1024 * 1024


def whole():
    return pl.BlockSpec(memory_space=pltpu.VMEM)


def params(**kw):
    return pltpu.CompilerParams(vmem_limit_bytes=BIG, **kw)


def dot(a, b):
    return lax.dot_general(a, b, (((1,), (0,)), ((), ())), preferred_element_type=F32)


def dot_t(a, b):
    return lax.dot_general(a, b, (((1,), (1,)), ((), ())), preferred_element_type=F32)


def iota(shape, axis):
    return lax.broadcasted_iota(I32, shape, axis)


def normalize(values):
    row_mean = jnp.mean(values, axis=-1, keepdims=True)
    centred = values - row_mean
    spread = jnp.sqrt(jnp.mean(centred * centred, axis=-1, keepdims=True) + NORM_EPS)
    return centred / spread, spread


def norm_back(grad_rows, normed, spread):
    first = jnp.mean(grad_rows, axis=-1, keepdims=True)
    second = jnp.mean(grad_rows * normed, axis=-1, keepdims=True)
    return (grad_rows - first - normed * second) / spread


def even_half(rows):
    lane = iota(rows.shape, 1) & 127
    return jnp.where(lane < 64, rows, jnp.zeros_like(rows))


def odd_half(rows):
    lane = iota(rows.shape, 1) & 127
    return jnp.where(lane < 64, jnp.zeros_like(rows), rows)


def route_kernel(rows_dev, row_ref, col_ref, seg_ref, pair_ref, req_ref, tr_ref, tc_ref, meta_ref, *, width):
    tokens = row_ref.shape[1]
    shards = req_ref.shape[0]
    shift = rows_dev.bit_length() - 1
    owner_r = row_ref[...] >> shift
    slot_r = (row_ref[...] & (rows_dev - 1)).astype(F32)
    owner_c = col_ref[...] >> shift
    same = owner_c == owner_r
    sub, lane = iota((tokens, tokens), 0), iota((tokens, tokens), 1)
    rank_c = jnp.sum(jnp.where(same & (lane < sub), 1.0, 0.0), axis=1, keepdims=True).astype(I32)
    rank_r = jnp.sum(jnp.where(same & (sub < lane), 1.0, 0.0), axis=0, keepdims=True).astype(I32)
    tr_ref[...] = owner_r * width + rank_r
    tc_ref[...] = owner_c * width + rank_c
    dest = iota((shards, tokens), 0) == owner_r
    place = iota((shards, 128), 1)
    req = jnp.zeros((shards, 128), F32)
    for k in range(2 * tokens // shards):
        picked = jnp.sum(jnp.where(dest & (rank_r == k), slot_r, 0.0), axis=1, keepdims=True)
        req = jnp.where(place == k, picked, req)
    req_ref[...] = req.astype(I32)
    own = lax.axis_index("pair")
    first, second = pair_ref[0:1, :], pair_ref[1:2, :]
    span = iota((8, first.shape[1]), 0)
    as_query = jnp.max(jnp.where((first == own) & (second == span), 1.0, 0.0), axis=1, keepdims=True)
    as_key = jnp.max(jnp.where((second == own) & (first == span), 1.0, 0.0), axis=1, keepdims=True)
    zeros = jnp.sum(jnp.where(seg_ref[...] == 0, 1.0, 0.0), axis=1, keepdims=True)
    at = iota((8, 128), 1)
    meta = jnp.where(at == 0, as_query, jnp.where(at == 1, as_key, jnp.where(at == 2, zeros, 0.0))).astype(I32)
    meta_ref[...] = jnp.where(at == 3, own, meta)


def slot_halves(slots):
    high = (slots >> 1).astype(F32).astype(BF16)
    low = (slots & 1).astype(F32).astype(BF16)
    return high, low


def find_kernel(slots_ref, table_ref, found_ref, *, width):
    shards = slots_ref.shape[0]
    rows_dev = table_ref.shape[0]
    count = shards * width
    spread = ((iota((count, shards), 0) // width) == iota((count, shards), 1)).astype(F32).astype(BF16)
    high, low = slot_halves(slots_ref[...])
    value = 2.0 * dot(spread, high) + dot(spread, low)
    mine = iota((count, 128), 1) == (iota((count, 128), 0) % width)
    slot = jnp.sum(jnp.where(mine, value, 0.0), axis=1, keepdims=True).astype(I32)
    pick = jnp.where(iota((count, rows_dev), 1) == slot, 1.0, 0.0).astype(BF16)
    found_ref[...] = dot(pick, table_ref[...].astype(BF16)).astype(BF16)


def project_kernel(fetched_ref, tc_ref, w_ref, x_ref, z_ref, u_ref, q_ref, kv_ref):
    count, width = fetched_ref.shape
    tokens = tc_ref.shape[0]
    pick = jnp.where(iota((tokens, count), 1) == tc_ref[...], 1.0, 0.0).astype(BF16)
    rows = dot(pick, fetched_ref[...])
    x_ref[...] = rows.astype(BF16)
    normed, _ = normalize(rows)
    low = normed.astype(BF16)
    outs = (u_ref.at[...], kv_ref.at[:, width:], q_ref.at[...], kv_ref.at[:, :width])
    for g in range(4):
        z = dot(low, w_ref[:, g * width : (g + 1) * width])
        z_ref[:, g * width : (g + 1) * width] = z
        half = 0.5 * z
        outs[g][...] = (half + half * jnp.tanh(half)).astype(BF16)


def visible(q_axis, size, q_block, k_block, zeros):
    q_pos = iota((size, size), q_axis) + q_block * size
    k_pos = iota((size, size), 1 - q_axis) + k_block * size
    least = jnp.where(q_pos >= zeros, zeros, 0)
    return jnp.where((k_pos >= least) & (k_pos <= q_pos), 1.0, 0.0)


class Ring:
    def __init__(self, source, gathered, send, recv, local, span):
        self.source, self.gathered, self.send, self.recv, self.local = source, gathered, send, recv, local
        chips = span // 2
        self.g, self.p = lax.axis_index("dp"), lax.axis_index("pair")
        core, chip = self.p % 2, self.p // 2
        at = lambda step: ((chip + step) % chips) * 2 + core
        self.up, self.down, self.far = at(1), at(chips - 1), at(2)
        self.other = chip * 2 + 1 - core

    def copy(self, i):
        p, up, down, far, other = self.p, self.up, self.down, self.far, self.other
        owner, part, to = (
            (p, 0, up),
            (p, 1, up),
            (p, 1, down),
            (p, 0, down),
            (p, 0, other),
            (p, 1, other),
            (down, 0, up),
            (up, 1, down),
            (down, 0, other),
            (down, 1, other),
            (up, 1, other),
            (up, 0, other),
            (far, 0, other),
            (far, 1, other),
        )[i]
        half = self.source.shape[0] // 2
        rows = pl.ds(part * half, half)
        return pltpu.make_async_remote_copy(
            src_ref=self.source.at[rows] if i < 6 else self.gathered.at[owner, rows],
            dst_ref=self.gathered.at[owner, rows],
            send_sem=self.send.at[i],
            recv_sem=self.recv.at[i],
            device_id=(self.g, to),
            device_id_type=MESH,
        )

    def own(self):
        return pltpu.make_async_copy(self.source, self.gathered.at[self.p], self.local)

    def start(self):
        self.own().start()
        for i in (0, 2, 1, 3, 4, 5):
            self.copy(i).start()

    def arrive(self, *which):
        for i in which:
            self.copy(i).wait_recv()

    def after(self, arrived, *sent):
        self.arrive(arrived)
        for i in sent:
            self.copy(i).start()

    def first(self):
        self.after(0, 6, 8)
        self.after(2, 7, 10)

    def second(self):
        self.after(1, 9)
        self.after(3, 11)

    def last(self):
        self.after(6, 12)
        self.after(7, 13)

    def sent(self):
        for i in range(14):
            self.copy(i).wait_send()


def attend_kernel(
    meta_ref,
    q_ref,
    kv_ref,
    u_ref,
    x_ref,
    w_ref,
    og_ref,
    out_ref,
    dhu_ref,
    gout_ref,
    dq_ref,
    dk_ref,
    dv_ref,
    kv_all,
    q_all,
    da_all,
    da,
    parts,
    acc,
    mask,
    local,
    send,
    recv,
    *,
    span,
):
    own = lax.axis_index("pair")
    chips, core, chip = span // 2, own % 2, own // 2
    size, width = q_ref.shape
    kv_ring, q_ring, da_ring = (
        Ring(source, gathered, send.at[i], recv.at[i], local.at[i], span)
        for i, (source, gathered) in enumerate(((kv_ref, kv_all), (q_ref, q_all), (da, da_all)))
    )
    barrier = pltpu.get_barrier_semaphore()
    for to in (kv_ring.other, kv_ring.up, kv_ring.down):
        pl.semaphore_signal(barrier, inc=1, device_id=(kv_ring.g, to), device_id_type=MESH)
    pl.semaphore_wait(barrier, 3)
    kv_ring.start()

    def block_at(step):
        turn = step // 2
        shift = (3 * turn - (turn * (turn - 1)) // 2) % 4
        return ((chip + shift) % chips) * 2 + (core + step % 2) % 2

    def split(value, at):
        parts[at] = even_half(value)
        parts[at + 1] = odd_half(value)

    def slabs(work):
        def one(s, carry):
            first = pl.multiple_of(s * 128, 128)
            work(pl.ds(first, 128), pl.ds(pl.multiple_of(width + s * 128, 128), 128))
            return carry

        lax.fori_loop(0, width // 128, one, 0)

    def both(rows):
        return jnp.concatenate([even_half(rows), odd_half(rows)], axis=0)

    zeros = meta_ref[0, 2]
    split(q_ref[...] * 0.0625, 0)
    split(kv_ref[:, :width] * 0.0625, 4)
    split(kv_ref[:, width:] * 0.0625, 6)
    acc[...] = jnp.zeros_like(acc)
    dq_ref[...] = jnp.zeros_like(dq_ref)
    dk_ref[...] = jnp.zeros_like(dk_ref)
    dv_ref[...] = jnp.zeros_like(dv_ref)

    def forward(step, carry):
        j = block_at(step)

        @pl.when(step == 0)
        def _():
            kv_ring.own().wait()

        @pl.when(step == 1)
        def _():
            kv_ring.arrive(4, 5)

        @pl.when(step == 2)
        def _():
            kv_ring.first()
            kv_ring.second()
            q_ring.start()

        @pl.when(step == 3)
        def _():
            kv_ring.arrive(8, 9)

        @pl.when(step == 5)
        def _():
            kv_ring.arrive(10, 11)

        @pl.when(step == 6)
        def _():
            kv_ring.last()

        @pl.when(step == 7)
        def _():
            kv_ring.arrive(12, 13)

        @pl.when(j <= own)
        def _():
            mask[...] = visible(0, size, own, j, zeros) * meta_ref[j, 0].astype(F32)

            def work(cols, late):
                keys = kv_all[j, :, cols]
                weights = []
                for half in range(2):
                    h = dot_t(parts[half, :, cols], keys)
                    weights.append(((h + h * jnp.tanh(h)) * mask[...]).astype(BF16))
                acc[:, cols] += dot(jnp.concatenate(weights, axis=1), both(kv_all[j, :, late]))

            slabs(work)

        return carry

    lax.fori_loop(0, span, forward, 0)

    normed, spread = normalize(acc[...])
    gate = u_ref[...].astype(F32)
    gated = (normed * gate).astype(BF16)
    dy = dot_t(og_ref[...], w_ref[...])
    da[...] = norm_back(dy * gate, normed, spread).astype(BF16)
    q_ring.first()
    da_ring.start()
    split(da[...] * 0.0625, 2)
    dhu_ref[...] = dy * normed
    out_ref[...] = (dot(gated, w_ref[...]) + x_ref[...].astype(F32)).astype(BF16)
    gout_ref[...] = lax.dot_general(gated, og_ref[...], (((0,), (0,)), ((), ())), preferred_element_type=F32)
    q_ring.second()

    def by_query(step, carry):
        j = block_at(step)

        @pl.when(step == 4)
        def _():
            q_ring.last()

        @pl.when(j <= own)
        def _():
            mask[...] = visible(0, size, own, j, zeros) * meta_ref[j, 0].astype(F32)

            def work(cols, late):
                keys = kv_all[j, :, cols]
                values = kv_all[j, :, late]
                grads = []
                for half in range(2):
                    h = dot_t(parts[half, :, cols], keys)
                    t = jnp.tanh(h)
                    slope = (1.0 + t) * (1.0 + h * (1.0 - t))
                    grads.append((dot_t(parts[2 + half, :, cols], values) * slope * mask[...]).astype(BF16))
                dq_ref[:, cols] += dot(jnp.concatenate(grads, axis=1), both(keys))

            slabs(work)

        return carry

    lax.fori_loop(0, span, by_query, 0)

    def by_key(step, carry):
        i = block_at(step)

        @pl.when(step == 0)
        def _():
            q_ring.own().wait()
            da_ring.own().wait()

        @pl.when(step == 1)
        def _():
            q_ring.arrive(4, 5)
            da_ring.arrive(4, 5)

        @pl.when(step == 2)
        def _():
            da_ring.first()
            da_ring.second()

        @pl.when(step == 3)
        def _():
            q_ring.arrive(8, 9)
            da_ring.arrive(8, 9)

        @pl.when(step == 5)
        def _():
            q_ring.arrive(10, 11)
            da_ring.arrive(10, 11)

        @pl.when(step == 6)
        def _():
            da_ring.last()

        @pl.when(step == 7)
        def _():
            q_ring.arrive(12, 13)
            da_ring.arrive(12, 13)

        @pl.when(i >= own)
        def _():
            mask[...] = visible(1, size, i, own, zeros) * meta_ref[i, 1].astype(F32)

            def work(cols, late):
                queries = q_all[i, :, cols]
                dafter = da_all[i, :, cols]
                grads, weights = [], []
                for half in range(2):
                    h = dot_t(parts[4 + half, :, cols], queries)
                    t = jnp.tanh(h)
                    weights.append(((h + h * t) * mask[...]).astype(BF16))
                    slope = (1.0 + t) * (1.0 + h * (1.0 - t))
                    grads.append((dot_t(parts[6 + half, :, cols], dafter) * slope * mask[...]).astype(BF16))
                dk_ref[:, cols] += dot(jnp.concatenate(grads, axis=1), both(queries))
                dv_ref[:, cols] += dot(jnp.concatenate(weights, axis=1), both(dafter))

            slabs(work)

        return carry

    lax.fori_loop(0, span, by_key, 0)
    for ring in (kv_ring, q_ring, da_ring):
        ring.sent()


def finish_kernel(
    z_ref, dhu_ref, dv_ref, dq_ref, dk_ref, x_ref, w_ref, og_ref, tr_ref, gout_ref, grads_ref, send_ref, hold, *, rows
):
    size, width = x_ref.shape
    normed, spread = normalize(x_ref[...].astype(F32))
    turned = jnp.transpose(normed).astype(BF16)
    dxn = jnp.zeros((size, width), F32)

    def place(upper, lower, at):
        count, cols = upper.shape
        top = (iota((count, cols), 0) % (2 * rows)) < rows
        first = jnp.where(top, upper, pltpu.roll(lower, rows, 0))
        second = jnp.where(top, pltpu.roll(upper, count - rows, 0), lower)
        whole_shape = (count // (2 * rows), 2 * rows, cols)
        grads_ref[0, :, :, at : at + cols] = first.reshape(whole_shape)
        grads_ref[1, :, :, at : at + cols] = second.reshape(whole_shape)

    for g, grad in enumerate((dhu_ref, dv_ref, dq_ref, dk_ref)):
        cols = slice(g * width, (g + 1) * width)
        h = 0.5 * z_ref[:, cols]
        t = jnp.tanh(h)
        slope = 0.5 * (1.0 + t) * (1.0 + h * (1.0 - t))
        dz = (grad[...] * slope).astype(BF16)
        part = dot(turned, dz)
        if g == 0:
            hold[...] = part
        elif g == 1:
            place(part, gout_ref[...], width)
        elif g == 2:
            place(part[:, : width // 2], part[:, width // 2 :], 2 * width)
        else:
            place(hold[...], part, 0)
        dxn += dot_t(dz, w_ref[:, cols])
    dx = norm_back(dxn, normed, spread) + og_ref[...].astype(F32)
    count = send_ref.shape[0]
    pick = jnp.where(iota((count, size), 0) == tr_ref[...], 1.0, 0.0).astype(BF16)
    send_ref[...] = dot(pick, dx.astype(BF16)).astype(BF16)


def partner(k, groups, span):
    g, p = lax.axis_index("dp"), lax.axis_index("pair")
    chips, side = span // 2, math.isqrt(groups)
    to_p = ((p // 2 + (k // 2) % chips) % chips) * 2 + (p % 2 + k % 2) % 2
    shift = k // span
    to_g = ((g // side + shift // side) % side) * side + (g % side + shift % side) % side
    return to_g, to_p


def greet(groups, span):
    barrier = pltpu.get_barrier_semaphore()

    def hello(k, carry):
        pl.semaphore_signal(barrier, inc=1, device_id=partner(k, groups, span), device_id_type=MESH)
        return carry

    lax.fori_loop(1, groups * span, hello, 0)
    pl.semaphore_wait(barrier, groups * span - 1)


def drain(ref, count, sem):
    part = ref.at[pl.ds(0, count)]
    pltpu.make_async_copy(part, part, sem).wait()


def tail_kernel(rows_ref, grads_ref, back_ref, parts_ref, got, part, sems, *, groups, span):
    total = groups * span
    g, p = lax.axis_index("dp"), lax.axis_index("pair")
    me, core = g * span + p, p % 2
    chip, chips = me // 2, total // 2
    own = pltpu.make_async_copy(rows_ref.at[me], back_ref.at[me], sems.at[0])
    own.start()
    greet(groups, span)
    swap = pltpu.make_async_remote_copy(
        src_ref=grads_ref.at[1 - core],
        dst_ref=got,
        send_sem=sems.at[1],
        recv_sem=sems.at[2],
        device_id=(g, p + 1 - 2 * core),
        device_id_type=MESH,
    )
    swap.start()

    def push_rows(k, carry):
        to_g, to_p = partner(k, groups, span)
        pltpu.make_async_remote_copy(
            src_ref=rows_ref.at[to_g * span + to_p],
            dst_ref=back_ref.at[me],
            send_sem=sems.at[3],
            recv_sem=sems.at[4],
            device_id=(to_g, to_p),
            device_id_type=MESH,
        ).start()
        return carry

    lax.fori_loop(1, total, push_rows, 0)
    swap.wait()

    def add(m, carry):
        part[m] = (grads_ref[core, m] + got[m]).astype(BF16)
        return carry

    lax.fori_loop(0, chips, add, 0)
    mine = pltpu.make_async_copy(part.at[chip], parts_ref.at[chip], sems.at[5])
    mine.start()

    def push_part(k, carry):
        to_g, to_p = partner(2 * k, groups, span)
        pltpu.make_async_remote_copy(
            src_ref=part.at[(to_g * span + to_p) // 2],
            dst_ref=parts_ref.at[chip],
            send_sem=sems.at[6],
            recv_sem=sems.at[7],
            device_id=(to_g, to_p),
            device_id_type=MESH,
        ).start()
        return carry

    lax.fori_loop(1, chips, push_part, 0)
    own.wait()
    mine.wait()
    drain(back_ref, total - 1, sems.at[3])
    drain(back_ref, total - 1, sems.at[4])
    drain(parts_ref, chips - 1, sems.at[6])
    drain(parts_ref, chips - 1, sems.at[7])


def update_kernel(
    slots_ref, back_ref, table_ref, accum_ref, parts_ref, tnew_ref, anew_ref, gin_ref, gout_ref, *, width, factor
):
    shards = slots_ref.shape[0]
    rows_dev, model = table_ref.shape
    count = shards * width
    spread = ((iota((shards, count), 1) // width) == iota((shards, count), 0)).astype(F32).astype(BF16)
    high, low = slot_halves(slots_ref[...])
    turn = lambda a: lax.dot_general(a, spread, (((0,), (0,)), ((), ())), preferred_element_type=F32)
    value = 2.0 * turn(high) + turn(low)
    mine = iota((128, count), 0) == (iota((128, count), 1) % width)
    slot = jnp.sum(jnp.where(mine, value, 0.0), axis=0, keepdims=True).astype(I32)
    pick = jnp.where(iota((rows_dev, count), 0) == slot, 1.0, 0.0).astype(BF16)
    total = dot(pick, back_ref[...])
    square = jnp.mean(total * total, axis=1, keepdims=True)
    eye = iota((rows_dev, rows_dev), 0) == iota((rows_dev, rows_dev), 1)
    accum = jnp.sum(jnp.where(eye, accum_ref[...], 0.0), axis=1, keepdims=True) + square
    anew_ref[...] = jnp.sum(jnp.where(eye, accum, 0.0), axis=0, keepdims=True)
    tnew_ref[...] = table_ref[...] - LEARN_RATE * total / jnp.sqrt(accum)

    def add(m, summed):
        return summed + parts_ref[m].astype(F32)

    summed = lax.fori_loop(0, parts_ref.shape[0], add, jnp.zeros(parts_ref.shape[1:], F32)) * factor
    rows = gin_ref.shape[0]
    upper, lower = summed[:rows], summed[rows:]
    gin_ref[:, :model] = upper[:, :model]
    gin_ref[:, model : 2 * model] = upper[:, model : 2 * model]
    gin_ref[:, 2 * model : 2 * model + model // 2] = upper[:, 2 * model :]
    gin_ref[:, 2 * model + model // 2 : 3 * model] = lower[:, 2 * model :]
    gin_ref[:, 3 * model :] = lower[:, :model]
    gout_ref[...] = lower[:, model : 2 * model]


def shape(dims, dtype):
    return jax.ShapeDtypeStruct(dims, dtype)


def cost(flops, moved):
    return pl.CostEstimate(flops=flops, bytes_accessed=moved, transcendentals=0)


def body(table, accum, item_row, segments, pairs, w_in, w_out, out_grad):
    tokens = item_row.shape[0]
    rows_dev, model = table.shape
    shards = lax.axis_size(("dp", "pair"))
    span = lax.axis_size("pair")
    width = -(-(2 * tokens // shards) // 8) * 8
    count = shards * width
    everyone = ("dp", "pair")

    call = pl.pallas_call(
        functools.partial(route_kernel, rows_dev, width=width),
        out_shape=(
            shape((shards, 128), I32),
            shape((1, tokens), I32),
            shape((tokens, 1), I32),
            shape((8, 128), I32),
        ),
        in_specs=[whole()] * 4,
        out_specs=[whole()] * 4,
        compiler_params=params(),
    )
    request, target_r, target_c, meta = call(
        item_row.reshape(1, tokens), item_row.reshape(tokens, 1), segments, pairs[0].T
    )
    asked = lax.all_to_all(request[:, :width], everyone, split_axis=0, concat_axis=0, tiled=True)
    slots = jnp.pad(asked, ((0, 0), (0, 128 - width)))
    found = pl.pallas_call(
        functools.partial(find_kernel, width=width),
        out_shape=shape((count, model), BF16),
        in_specs=[whole()] * 2,
        out_specs=whole(),
        compiler_params=params(),
    )(slots, table)
    fetched = lax.all_to_all(
        found.reshape(shards, width, model), everyone, split_axis=0, concat_axis=0, tiled=True
    ).reshape(count, model)
    x, z, u, q, kv = pl.pallas_call(
        project_kernel,
        out_shape=(
            shape((tokens, model), BF16),
            shape((tokens, 4 * model), F32),
            shape((tokens, model), BF16),
            shape((tokens, model), BF16),
            shape((tokens, 2 * model), BF16),
        ),
        in_specs=[whole()] * 3,
        out_specs=[whole()] * 5,
        compiler_params=params(),
    )(fetched, target_c, w_in)

    block = lambda cols, dtype: VMEM((span, tokens, cols), dtype)
    layer_out, dhu, gout, dq, dk, dv = pl.pallas_call(
        functools.partial(attend_kernel, span=span),
        out_shape=(
            shape((tokens, model), BF16),
            shape((tokens, model), F32),
            shape((model, model), F32),
            shape((tokens, model), F32),
            shape((tokens, model), F32),
            shape((tokens, model), F32),
        ),
        in_specs=[pl.BlockSpec(memory_space=pltpu.SMEM)] + [whole()] * 6,
        out_specs=[whole()] * 6,
        scratch_shapes=[
            block(2 * model, BF16),
            block(model, BF16),
            block(model, BF16),
            VMEM((tokens, model), BF16),
            VMEM((8, tokens, model), BF16),
            VMEM((tokens, model), F32),
            VMEM((tokens, tokens), F32),
            pltpu.SemaphoreType.DMA((3,)),
            pltpu.SemaphoreType.DMA((3, 14)),
            pltpu.SemaphoreType.DMA((3, 14)),
        ],
        compiler_params=params(collective_id=1, has_side_effects=True),
    )(meta, q, kv, u, x, w_out, out_grad)

    rows = model // shards
    chunk = (2 * rows, 5 * model // 2)
    grads, send = pl.pallas_call(
        functools.partial(finish_kernel, rows=rows),
        out_shape=(shape((2, shards // 2) + chunk, F32), shape((count, model), BF16)),
        in_specs=[whole()] * 10,
        out_specs=[whole()] * 2,
        scratch_shapes=[VMEM((model, model), F32)],
        compiler_params=params(),
    )(z, dhu, dv, dq, dk, x, w_in, out_grad, target_r, gout)
    back, parts = pl.pallas_call(
        functools.partial(tail_kernel, groups=shards // span, span=span),
        out_shape=(shape((shards, width, model), BF16), shape((shards // 2,) + chunk, BF16)),
        in_specs=[whole()] * 2,
        out_specs=[whole()] * 2,
        scratch_shapes=[
            VMEM((shards // 2,) + chunk, F32),
            VMEM((shards // 2,) + chunk, BF16),
            pltpu.SemaphoreType.DMA((8,)),
        ],
        compiler_params=params(collective_id=0, has_side_effects=True),
    )(send.reshape(shards, width, model), grads)
    table_new, accum_new, grad_in, grad_out = pl.pallas_call(
        functools.partial(update_kernel, width=width, factor=1.0 / math.sqrt(tokens * shards)),
        out_shape=(
            shape((rows_dev, model), F32),
            shape((1, rows_dev), F32),
            shape((rows, 4 * model), F32),
            shape((rows, model), F32),
        ),
        in_specs=[whole()] * 5,
        out_specs=[whole()] * 4,
        compiler_params=params(),
    )(slots, back.reshape(count, model), table, accum.reshape(1, rows_dev), parts)
    return layer_out, table_new, accum_new.reshape(rows_dev), grad_in, grad_out


def solution(mesh):
    both = ("dp", "pair")
    return jax.shard_map(
        body,
        mesh=mesh,
        in_specs=(
            P(both, None),
            P(both),
            P(both),
            P("dp", None),
            P("dp", None, None),
            P(),
            P(),
            P(both, None),
        ),
        out_specs=(P(both, None), P(both, None), P(both), P(both, None), P(both, None)),
        check_vma=False,
    )
```

```python
import functools
import math

import jax
import jax.numpy as jnp
from jax import lax
from jax.experimental import pallas as pl
from jax.experimental.pallas import tpu as pltpu
from jax.sharding import PartitionSpec as P

HEADS = 8
NORM_EPS = 1e-05
LEARN_RATE = 0.5
F32, BF16, I32 = jnp.float32, jnp.bfloat16, jnp.int32
VMEM = pltpu.VMEM
MESH = pl.DeviceIdType.MESH
BIG = 62 * 1024 * 1024


def whole():
    return pl.BlockSpec(memory_space=pltpu.VMEM)


def params(**kw):
    return pltpu.CompilerParams(vmem_limit_bytes=BIG, **kw)


def dot(a, b):
    return lax.dot_general(a, b, (((1,), (0,)), ((), ())), preferred_element_type=F32)


def dot_t(a, b):
    return lax.dot_general(a, b, (((1,), (1,)), ((), ())), preferred_element_type=F32)


def iota(shape, axis):
    return lax.broadcasted_iota(I32, shape, axis)


def normalize(values):
    row_mean = jnp.mean(values, axis=-1, keepdims=True)
    centred = values - row_mean
    spread = jnp.sqrt(jnp.mean(centred * centred, axis=-1, keepdims=True) + NORM_EPS)
    return centred / spread, spread


def norm_back(grad_rows, normed, spread):
    first = jnp.mean(grad_rows, axis=-1, keepdims=True)
    second = jnp.mean(grad_rows * normed, axis=-1, keepdims=True)
    return (grad_rows - first - normed * second) / spread


def even_half(rows):
    lane = iota(rows.shape, 1) & 127
    return jnp.where(lane < 64, rows, jnp.zeros_like(rows))


def odd_half(rows):
    lane = iota(rows.shape, 1) & 127
    return jnp.where(lane < 64, jnp.zeros_like(rows), rows)


def route_kernel(rows_dev, row_ref, col_ref, seg_ref, pair_ref, req_ref, tr_ref, tc_ref, meta_ref, *, width):
    tokens = row_ref.shape[1]
    shards = req_ref.shape[0]
    shift = rows_dev.bit_length() - 1
    owner_r = row_ref[...] >> shift
    slot_r = (row_ref[...] & (rows_dev - 1)).astype(F32)
    owner_c = col_ref[...] >> shift
    same = owner_c == owner_r
    sub, lane = iota((tokens, tokens), 0), iota((tokens, tokens), 1)
    rank_c = jnp.sum(jnp.where(same & (lane < sub), 1.0, 0.0), axis=1, keepdims=True).astype(I32)
    rank_r = jnp.sum(jnp.where(same & (sub < lane), 1.0, 0.0), axis=0, keepdims=True).astype(I32)
    tr_ref[...] = owner_r * width + rank_r
    tc_ref[...] = owner_c * width + rank_c
    dest = iota((shards, tokens), 0) == owner_r
    place = iota((shards, 128), 1)
    req = jnp.zeros((shards, 128), F32)
    for k in range(2 * tokens // shards):
        picked = jnp.sum(jnp.where(dest & (rank_r == k), slot_r, 0.0), axis=1, keepdims=True)
        req = jnp.where(place == k, picked, req)
    req_ref[...] = req.astype(I32)
    own = lax.axis_index("pair")
    first, second = pair_ref[0:1, :], pair_ref[1:2, :]
    span = iota((8, first.shape[1]), 0)
    as_query = jnp.max(jnp.where((first == own) & (second == span), 1.0, 0.0), axis=1, keepdims=True)
    as_key = jnp.max(jnp.where((second == own) & (first == span), 1.0, 0.0), axis=1, keepdims=True)
    zeros = jnp.sum(jnp.where(seg_ref[...] == 0, 1.0, 0.0), axis=1, keepdims=True)
    at = iota((8, 128), 1)
    meta = jnp.where(at == 0, as_query, jnp.where(at == 1, as_key, jnp.where(at == 2, zeros, 0.0))).astype(I32)
    meta_ref[...] = jnp.where(at == 3, own, meta)


def slot_halves(slots):
    high = (slots >> 1).astype(F32).astype(BF16)
    low = (slots & 1).astype(F32).astype(BF16)
    return high, low


def find_kernel(slots_ref, table_ref, found_ref, *, width):
    shards = slots_ref.shape[0]
    rows_dev = table_ref.shape[0]
    count = shards * width
    spread = ((iota((count, shards), 0) // width) == iota((count, shards), 1)).astype(F32).astype(BF16)
    high, low = slot_halves(slots_ref[...])
    value = 2.0 * dot(spread, high) + dot(spread, low)
    mine = iota((count, 128), 1) == (iota((count, 128), 0) % width)
    slot = jnp.sum(jnp.where(mine, value, 0.0), axis=1, keepdims=True).astype(I32)
    pick = jnp.where(iota((count, rows_dev), 1) == slot, 1.0, 0.0).astype(BF16)
    found_ref[...] = dot(pick, table_ref[...].astype(BF16)).astype(BF16)


def project(fetched_ref, tc_ref, w_ref, x_ref, z_ref, u_ref, q_ref, kv_ref):
    width = fetched_ref.shape[2]
    count = fetched_ref.shape[0] * fetched_ref.shape[1]
    tokens = tc_ref.shape[0]
    pick = jnp.where(iota((tokens, count), 1) == tc_ref[...], 1.0, 0.0).astype(BF16)
    rows = dot(pick, fetched_ref[...].reshape(count, width))
    x_ref[...] = rows.astype(BF16)
    normed, _ = normalize(rows)
    low = normed.astype(BF16)
    outs = (u_ref.at[...], kv_ref.at[:, width:], q_ref.at[...], kv_ref.at[:, :width])
    for g in range(4):
        z = dot(low, w_ref[:, g * width : (g + 1) * width])
        z_ref[:, g * width : (g + 1) * width] = z
        half = 0.5 * z
        outs[g][...] = (half + half * jnp.tanh(half)).astype(BF16)


def visible(q_axis, size, q_block, k_block, zeros):
    q_pos = iota((size, size), q_axis) + q_block * size
    k_pos = iota((size, size), 1 - q_axis) + k_block * size
    least = jnp.where(q_pos >= zeros, zeros, 0)
    return jnp.where((k_pos >= least) & (k_pos <= q_pos), 1.0, 0.0)


class Ring:
    SENDS = ((0, 1, 2, 3, 4, 5, 7), (0, 1, 2, 4, 5, 6, 8, 9), (0, 1, 4, 5, 6, 8, 9, 12, 13), (4, 5, 7, 8, 9, 10, 11, 12, 13))

    def __init__(self, source, gathered, send, recv, local, span, falling):
        self.source, self.gathered, self.send, self.recv, self.local = source, gathered, send, recv, local
        chips = span // 2
        self.g, self.p = lax.axis_index("dp"), lax.axis_index("pair")
        core, chip = self.p % 2, self.p // 2
        at = lambda step: ((chip + step) % chips) * 2 + core
        self.up, self.down, self.far = at(chips - 1 if falling else 1), at(1 if falling else chips - 1), at(2)
        self.rank = chips - 1 - chip if falling else chip
        self.other = chip * 2 + 1 - core

    def copy(self, i):
        p, up, down, far, other = self.p, self.up, self.down, self.far, self.other
        owner, part, to = (
            (p, 0, up),
            (p, 1, up),
            (p, 1, down),
            (p, 0, down),
            (p, 0, other),
            (p, 1, other),
            (down, 0, up),
            (up, 1, down),
            (down, 0, other),
            (down, 1, other),
            (up, 1, other),
            (up, 0, other),
            (far, 0, other),
            (far, 1, other),
        )[i]
        half = self.source.shape[0] // 2
        rows = pl.ds(part * half, half)
        return pltpu.make_async_remote_copy(
            src_ref=self.source.at[rows] if i < 6 else self.gathered.at[owner, rows],
            dst_ref=self.gathered.at[owner, rows],
            send_sem=self.send.at[i],
            recv_sem=self.recv.at[i],
            device_id=(self.g, to),
            device_id_type=MESH,
        )

    def own(self):
        return pltpu.make_async_copy(self.source, self.gathered.at[self.p], self.local)

    def when(self, *ranks):
        def decorate(steps):
            for rank in ranks:
                pl.when(self.rank == rank)(functools.partial(steps, rank))

        return decorate

    def start(self):
        self.own().start()

        @self.when(0, 1, 2, 3)
        def _(rank):
            for i in (0, 2, 1, 3, 4, 5):
                if i in self.SENDS[rank]:
                    self.copy(i).start()

    def arrive(self, *which):
        for i in which:
            self.copy(i).wait_recv()

    def after(self, arrived, *sent):
        self.arrive(arrived)
        for i in sent:
            self.copy(i).start()

    def relay(self, *ranks):
        @self.when(*ranks)
        def _(rank):
            if rank == 0:
                self.after(2, 7)
            elif rank == 3:
                self.after(2, 7, 10)
                self.after(0, 8)
                self.after(3, 11)
                self.after(1, 9)
            else:
                self.after(0, 6, 8)
                self.after(1, 9)

    def relay_far(self):
        @self.when(2, 3)
        def _(rank):
            self.after(6, 12)
            self.after(7, 13)

    def handed(self, step):
        if step == 1:
            self.arrive(4, 5)
        elif step == 3:

            @self.when(1, 2, 3)
            def _(rank):
                self.arrive(8, 9)

        elif step == 5:

            @self.when(3)
            def _(rank):
                self.arrive(10, 11)

        elif step == 7:

            @self.when(2, 3)
            def _(rank):
                self.arrive(12, 13)

    def sent(self):
        @self.when(0, 1, 2, 3)
        def _(rank):
            for i in self.SENDS[rank]:
                self.copy(i).wait_send()


def attend(
    meta_ref, q_ref, kv_ref, u_ref, x_ref, w_ref, og_ref, out_ref, dhu_ref, gout_ref, dq_ref, dk_ref, dv_ref, kv_all,
    q_all, da_all, da, parts, acc, mask, local, send, recv, *, span
):
    own = lax.axis_index("pair")
    chips, core, chip = span // 2, own % 2, own // 2
    size, width = q_ref.shape
    kv_ring, q_ring, da_ring = (
        Ring(source, gathered, send.at[i], recv.at[i], local.at[i], span, falling)
        for i, (source, gathered, falling) in enumerate(
            ((kv_ref, kv_all, False), (q_ref, q_all, True), (da, da_all, True))
        )
    )
    kv_ring.start()
    q_ring.start()

    def at_steps(step, *rings):
        for k in (1, 3, 5, 7):

            @pl.when(step == k)
            def _():
                for ring in rings:
                    ring.handed(k)

    def block_at(step, falling):
        turn = step // 2
        shift = (3 * turn - (turn * (turn - 1)) // 2) % 4
        if falling:
            shift = (chips - shift) % chips
        return ((chip + shift) % chips) * 2 + (core + step % 2) % 2

    def split(value, at):
        parts[at] = even_half(value)
        parts[at + 1] = odd_half(value)

    def slabs(work):
        def one(s, carry):
            first = pl.multiple_of(s * 128, 128)
            work(pl.ds(first, 128), pl.ds(pl.multiple_of(width + s * 128, 128), 128))
            return carry

        lax.fori_loop(0, width // 128, one, 0)

    def both(rows):
        return jnp.concatenate([even_half(rows), odd_half(rows)], axis=0)

    zeros = meta_ref[0, 2]
    split(q_ref[...] * 0.0625, 0)
    split(kv_ref[:, :width] * 0.0625, 4)
    split(kv_ref[:, width:] * 0.0625, 6)
    acc[...] = jnp.zeros_like(acc)
    dq_ref[...] = jnp.zeros_like(dq_ref)
    dk_ref[...] = jnp.zeros_like(dk_ref)
    dv_ref[...] = jnp.zeros_like(dv_ref)

    def forward(step, carry):
        j = block_at(step, False)

        @pl.when(step == 0)
        def _():
            kv_ring.own().wait()

        @pl.when(step == 2)
        def _():
            kv_ring.relay(0, 1, 2, 3)
            q_ring.relay(0, 1, 2, 3)

        @pl.when(step == 6)
        def _():
            kv_ring.relay_far()
            q_ring.relay_far()

        at_steps(step, kv_ring)

        @pl.when(j <= own)
        def _():
            mask[...] = visible(0, size, own, j, zeros) * meta_ref[j, 0].astype(F32)

            def work(cols, late):
                keys = kv_all[j, :, cols]
                weights = []
                for half in range(2):
                    h = dot_t(parts[half, :, cols], keys)
                    weights.append(((h + h * jnp.tanh(h)) * mask[...]).astype(BF16))
                acc[:, cols] += dot(jnp.concatenate(weights, axis=1), both(kv_all[j, :, late]))

            slabs(work)

        return carry

    lax.fori_loop(0, span, forward, 0)

    normed, spread = normalize(acc[...])
    gate = u_ref[...].astype(F32)
    gated = (normed * gate).astype(BF16)
    dy = dot_t(og_ref[...], w_ref[...])
    da[...] = norm_back(dy * gate, normed, spread).astype(BF16)
    da_ring.start()
    split(da[...] * 0.0625, 2)
    dhu_ref[...] = dy * normed
    out_ref[...] = (dot(gated, w_ref[...]) + x_ref[...].astype(F32)).astype(BF16)
    gout_ref[...] = lax.dot_general(gated, og_ref[...], (((0,), (0,)), ((), ())), preferred_element_type=F32)
    def by_query(step, carry):
        j = block_at(step, False)

        @pl.when(step == 1)
        def _():
            da_ring.relay(0)

        @pl.when(j <= own)
        def _():
            mask[...] = visible(0, size, own, j, zeros) * meta_ref[j, 0].astype(F32)

            def work(cols, late):
                keys = kv_all[j, :, cols]
                values = kv_all[j, :, late]
                grads = []
                for half in range(2):
                    h = dot_t(parts[half, :, cols], keys)
                    t = jnp.tanh(h)
                    slope = (1.0 + t) * (1.0 + h * (1.0 - t))
                    grads.append((dot_t(parts[2 + half, :, cols], values) * slope * mask[...]).astype(BF16))
                dq_ref[:, cols] += dot(jnp.concatenate(grads, axis=1), both(keys))

            slabs(work)

        return carry

    lax.fori_loop(0, span, by_query, 0)

    def by_key(step, carry):
        i = block_at(step, True)

        @pl.when(step == 0)
        def _():
            q_ring.own().wait()
            da_ring.own().wait()

        @pl.when(step == 2)
        def _():
            da_ring.relay(1, 2, 3)

        @pl.when(step == 6)
        def _():
            da_ring.relay_far()

        at_steps(step, q_ring, da_ring)

        @pl.when(i >= own)
        def _():
            mask[...] = visible(1, size, i, own, zeros) * meta_ref[i, 1].astype(F32)

            def work(cols, late):
                queries = q_all[i, :, cols]
                dafter = da_all[i, :, cols]
                grads, weights = [], []
                for half in range(2):
                    h = dot_t(parts[4 + half, :, cols], queries)
                    t = jnp.tanh(h)
                    weights.append(((h + h * t) * mask[...]).astype(BF16))
                    slope = (1.0 + t) * (1.0 + h * (1.0 - t))
                    grads.append((dot_t(parts[6 + half, :, cols], dafter) * slope * mask[...]).astype(BF16))
                dk_ref[:, cols] += dot(jnp.concatenate(grads, axis=1), both(queries))
                dv_ref[:, cols] += dot(jnp.concatenate(weights, axis=1), both(dafter))

            slabs(work)

        return carry

    lax.fori_loop(0, span, by_key, 0)
    for ring in (kv_ring, q_ring, da_ring):
        ring.sent()


def finish(
    z_ref, dhu_ref, dv_ref, dq_ref, dk_ref, x_ref, w_ref, og_ref, tr_ref, gout_ref, grads_ref, send_ref, hold, *, rows
):
    size, width = x_ref.shape
    normed, spread = normalize(x_ref[...].astype(F32))
    turned = jnp.transpose(normed).astype(BF16)
    dxn = jnp.zeros((size, width), F32)

    def place(upper, lower, at):
        count, cols = upper.shape
        top = (iota((count, cols), 0) % (2 * rows)) < rows
        first = jnp.where(top, upper, pltpu.roll(lower, rows, 0))
        second = jnp.where(top, pltpu.roll(upper, count - rows, 0), lower)
        whole_shape = (count // (2 * rows), 2 * rows, cols)
        grads_ref[0, :, :, at : at + cols] = first.reshape(whole_shape)
        grads_ref[1, :, :, at : at + cols] = second.reshape(whole_shape)

    for g, grad in enumerate((dhu_ref, dv_ref, dq_ref, dk_ref)):
        cols = slice(g * width, (g + 1) * width)
        h = 0.5 * z_ref[:, cols]
        t = jnp.tanh(h)
        slope = 0.5 * (1.0 + t) * (1.0 + h * (1.0 - t))
        dz = (grad[...] * slope).astype(BF16)
        part = dot(turned, dz)
        if g == 0:
            hold[...] = part
        elif g == 1:
            place(part, gout_ref[...], width)
        elif g == 2:
            place(part[:, : width // 2], part[:, width // 2 :], 2 * width)
        else:
            place(hold[...], part, 0)
        dxn += dot_t(dz, w_ref[:, cols])
    dx = norm_back(dxn, normed, spread) + og_ref[...].astype(F32)
    count = send_ref.shape[0] * send_ref.shape[1]
    pick = jnp.where(iota((count, size), 0) == tr_ref[...], 1.0, 0.0).astype(BF16)
    send_ref[...] = dot(pick, dx.astype(BF16)).astype(BF16).reshape(send_ref.shape)


def partner(k, groups, span):
    g, p = lax.axis_index("dp"), lax.axis_index("pair")
    chips, side = span // 2, math.isqrt(groups)
    to_p = ((p // 2 + (k // 2) % chips) % chips) * 2 + (p % 2 + k % 2) % 2
    shift = k // span
    to_g = ((g // side + shift // side) % side) * side + (g % side + shift % side) % side
    return to_g, to_p


def greet(groups, span):
    barrier = pltpu.get_barrier_semaphore()

    def hello(k, carry):
        pl.semaphore_signal(barrier, inc=1, device_id=partner(k, groups, span), device_id_type=MESH)
        return carry

    lax.fori_loop(1, groups * span, hello, 0)
    return lambda: pl.semaphore_wait(barrier, groups * span - 1)


def drain(ref, count, sem):
    part = ref.at[pl.ds(0, count)]
    pltpu.make_async_copy(part, part, sem).wait()


def exchange_gradients(rows_ref, grads_ref, back_ref, parts_ref, got, part, sems, *, groups, span):
    total = groups * span
    g, p = lax.axis_index("dp"), lax.axis_index("pair")
    me, core = g * span + p, p % 2
    chip, chips = me // 2, total // 2
    own = pltpu.make_async_copy(rows_ref.at[me], back_ref.at[me], sems.at[0])
    own.start()
    swap = pltpu.make_async_remote_copy(
        src_ref=grads_ref.at[1 - core],
        dst_ref=got,
        send_sem=sems.at[1],
        recv_sem=sems.at[2],
        device_id=(g, p + 1 - 2 * core),
        device_id_type=MESH,
    )
    swap.start()

    def push_rows(k, carry):
        to_g, to_p = partner(k, groups, span)
        pltpu.make_async_remote_copy(
            src_ref=rows_ref.at[to_g * span + to_p],
            dst_ref=back_ref.at[me],
            send_sem=sems.at[3],
            recv_sem=sems.at[4],
            device_id=(to_g, to_p),
            device_id_type=MESH,
        ).start()
        return carry

    lax.fori_loop(1, total, push_rows, 0)
    swap.wait()

    def add(m, carry):
        part[m] = (grads_ref[core, m] + got[m]).astype(BF16)
        return carry

    lax.fori_loop(0, chips, add, 0)
    mine = pltpu.make_async_copy(part.at[chip], parts_ref.at[chip], sems.at[5])
    mine.start()

    def push_part(k, carry):
        to_g, to_p = partner(2 * k, groups, span)
        pltpu.make_async_remote_copy(
            src_ref=part.at[(to_g * span + to_p) // 2],
            dst_ref=parts_ref.at[chip],
            send_sem=sems.at[6],
            recv_sem=sems.at[7],
            device_id=(to_g, to_p),
            device_id_type=MESH,
        ).start()
        return carry

    lax.fori_loop(1, chips, push_part, 0)
    own.wait()
    mine.wait()
    drain(back_ref, total - 1, sems.at[3])
    drain(back_ref, total - 1, sems.at[4])
    drain(parts_ref, chips - 1, sems.at[6])
    drain(parts_ref, chips - 1, sems.at[7])


def update(
    slots_ref, back_ref, table_ref, accum_ref, parts_ref, tnew_ref, anew_ref, gin_ref, gout_ref, *, width, factor
):
    shards = slots_ref.shape[0]
    rows_dev, model = table_ref.shape
    count = shards * width
    spread = ((iota((shards, count), 1) // width) == iota((shards, count), 0)).astype(F32).astype(BF16)
    high, low = slot_halves(slots_ref[...])
    turn = lambda a: lax.dot_general(a, spread, (((0,), (0,)), ((), ())), preferred_element_type=F32)
    value = 2.0 * turn(high) + turn(low)
    mine = iota((128, count), 0) == (iota((128, count), 1) % width)
    slot = jnp.sum(jnp.where(mine, value, 0.0), axis=0, keepdims=True).astype(I32)
    pick = jnp.where(iota((rows_dev, count), 0) == slot, 1.0, 0.0).astype(BF16)
    total = dot(pick, back_ref[...].reshape(count, model))
    square = jnp.mean(total * total, axis=1, keepdims=True)
    eye = iota((rows_dev, rows_dev), 0) == iota((rows_dev, rows_dev), 1)
    accum = jnp.sum(jnp.where(eye, accum_ref[...], 0.0), axis=1, keepdims=True) + square
    anew_ref[...] = jnp.sum(jnp.where(eye, accum, 0.0), axis=0, keepdims=True)
    tnew_ref[...] = table_ref[...] - LEARN_RATE * total / jnp.sqrt(accum)

    def add(m, summed):
        return summed + parts_ref[m].astype(F32)

    summed = lax.fori_loop(0, parts_ref.shape[0], add, jnp.zeros(parts_ref.shape[1:], F32)) * factor
    rows = gin_ref.shape[0]
    upper, lower = summed[:rows], summed[rows:]
    gin_ref[:, :model] = upper[:, :model]
    gin_ref[:, model : 2 * model] = upper[:, model : 2 * model]
    gin_ref[:, 2 * model : 2 * model + model // 2] = upper[:, 2 * model :]
    gin_ref[:, 2 * model + model // 2 : 3 * model] = lower[:, 2 * model :]
    gin_ref[:, 3 * model :] = lower[:, :model]
    gout_ref[...] = lower[:, model : 2 * model]


def layer_kernel(
    meta_ref, fetched_ref, tc_ref, tr_ref, w_in_ref, w_out_ref, og_ref, slots_ref, table_ref, accum_ref, out_ref,
    tnew_ref, anew_ref, gin_ref, gout_ref, x, z, u, q, kv, dhu, wgrad, dq, dk, dv, kv_all, q_all, da_all, da, parts, acc,
    mask, grads, hold, sending, back, got, part, landed, local, send, recv, sems, *, groups, span, width, rows, factor
):
    ready = greet(groups, span)
    project(fetched_ref, tc_ref, w_in_ref, x, z, u, q, kv)
    ready()
    attend(
        meta_ref, q, kv, u, x, w_out_ref, og_ref, out_ref, dhu, wgrad, dq, dk, dv, kv_all, q_all, da_all, da, parts, acc,
        mask, local, send, recv, span=span
    )
    finish(z, dhu, dv, dq, dk, x, w_in_ref, og_ref, tr_ref, wgrad, grads, sending, hold, rows=rows)
    exchange_gradients(sending, grads, back, landed, got, part, sems, groups=groups, span=span)
    update(
        slots_ref, back, table_ref, accum_ref, landed, tnew_ref, anew_ref, gin_ref, gout_ref, width=width, factor=factor
    )


def shape(dims, dtype):
    return jax.ShapeDtypeStruct(dims, dtype)


def cost(flops, moved):
    return pl.CostEstimate(flops=flops, bytes_accessed=moved, transcendentals=0)


def body(table, accum, item_row, segments, pairs, w_in, w_out, out_grad):
    tokens = item_row.shape[0]
    rows_dev, model = table.shape
    shards = lax.axis_size(("dp", "pair"))
    span = lax.axis_size("pair")
    width = -(-(2 * tokens // shards) // 8) * 8
    count = shards * width
    everyone = ("dp", "pair")

    call = pl.pallas_call(
        functools.partial(route_kernel, rows_dev, width=width),
        out_shape=(
            shape((shards, 128), I32),
            shape((1, tokens), I32),
            shape((tokens, 1), I32),
            shape((8, 128), I32),
        ),
        in_specs=[whole()] * 4,
        out_specs=[whole()] * 4,
        compiler_params=params(),
    )
    request, target_r, target_c, meta = call(
        item_row.reshape(1, tokens), item_row.reshape(tokens, 1), segments, pairs[0].T
    )
    asked = lax.all_to_all(request[:, :width], everyone, split_axis=0, concat_axis=0, tiled=True)
    slots = jnp.pad(asked, ((0, 0), (0, 128 - width)))
    found = pl.pallas_call(
        functools.partial(find_kernel, width=width),
        out_shape=shape((count, model), BF16),
        in_specs=[whole()] * 2,
        out_specs=whole(),
        compiler_params=params(),
    )(slots, table)
    fetched = lax.all_to_all(
        found.reshape(shards, width, model), everyone, split_axis=0, concat_axis=0, tiled=True
    )
    rows = model // shards
    chunk = (2 * rows, 5 * model // 2)
    half_grads = (shards // 2,) + chunk
    block = lambda cols: VMEM((span, tokens, cols), BF16)
    low = lambda cols: VMEM((tokens, cols), BF16)
    high = lambda cols: VMEM((tokens, cols), F32)
    layer_out, table_new, accum_new, grad_in, grad_out = pl.pallas_call(
        functools.partial(
            layer_kernel,
            groups=shards // span,
            span=span,
            width=width,
            rows=rows,
            factor=1.0 / math.sqrt(tokens * shards),
        ),
        out_shape=(
            shape((tokens, model), BF16),
            shape((rows_dev, model), F32),
            shape((1, rows_dev), F32),
            shape((rows, 4 * model), F32),
            shape((rows, model), F32),
        ),
        in_specs=[pl.BlockSpec(memory_space=pltpu.SMEM)] + [whole()] * 9,
        out_specs=[whole()] * 5,
        scratch_shapes=[
            low(model),
            high(4 * model),
            low(model),
            low(model),
            low(2 * model),
            high(model),
            VMEM((model, model), F32),
            high(model),
            high(model),
            high(model),
            block(2 * model),
            block(model),
            block(model),
            low(model),
            VMEM((8, tokens, model), BF16),
            high(model),
            high(tokens),
            VMEM((2,) + half_grads, F32),
            VMEM((model, model), F32),
            VMEM((shards, width, model), BF16),
            VMEM((shards, width, model), BF16),
            VMEM(half_grads, F32),
            VMEM(half_grads, BF16),
            VMEM(half_grads, BF16),
            pltpu.SemaphoreType.DMA((3,)),
            pltpu.SemaphoreType.DMA((3, 14)),
            pltpu.SemaphoreType.DMA((3, 14)),
            pltpu.SemaphoreType.DMA((8,)),
        ],
        compiler_params=params(collective_id=0, has_side_effects=True),
    )(meta, fetched, target_c, target_r, w_in, w_out, out_grad, slots, table, accum.reshape(1, rows_dev))
    return layer_out, table_new, accum_new.reshape(rows_dev), grad_in, grad_out


def solution(mesh):
    both = ("dp", "pair")
    return jax.shard_map(
        body,
        mesh=mesh,
        in_specs=(
            P(both, None),
            P(both),
            P(both),
            P("dp", None),
            P("dp", None, None),
            P(),
            P(),
            P(both, None),
        ),
        out_specs=(P(both, None), P(both, None), P(both), P(both, None), P(both, None)),
        check_vma=False,
    )
```

```python
import functools
import math

import jax
import jax.numpy as jnp
from jax import lax
from jax.experimental import pallas as pl
from jax.experimental.pallas import tpu as pltpu
from jax.sharding import PartitionSpec as P

HEADS = 8
NORM_EPS = 1e-05
LEARN_RATE = 0.5
F32, BF16, I32 = jnp.float32, jnp.bfloat16, jnp.int32
VMEM = pltpu.VMEM
MESH = pl.DeviceIdType.MESH
BIG = 62 * 1024 * 1024


def whole():
    return pl.BlockSpec(memory_space=pltpu.VMEM)


def params(**kw):
    return pltpu.CompilerParams(vmem_limit_bytes=BIG, **kw)


def dot(a, b):
    return lax.dot_general(a, b, (((1,), (0,)), ((), ())), preferred_element_type=F32)


def dot_t(a, b):
    return lax.dot_general(a, b, (((1,), (1,)), ((), ())), preferred_element_type=F32)


def iota(shape, axis):
    return lax.broadcasted_iota(I32, shape, axis)


def normalize(values):
    row_mean = jnp.mean(values, axis=-1, keepdims=True)
    centred = values - row_mean
    spread = jnp.sqrt(jnp.mean(centred * centred, axis=-1, keepdims=True) + NORM_EPS)
    return centred / spread, spread


def norm_back(grad_rows, normed, spread):
    first = jnp.mean(grad_rows, axis=-1, keepdims=True)
    second = jnp.mean(grad_rows * normed, axis=-1, keepdims=True)
    return (grad_rows - first - normed * second) / spread


def even_half(rows):
    lane = iota(rows.shape, 1) & 127
    return jnp.where(lane < 64, rows, jnp.zeros_like(rows))


def odd_half(rows):
    lane = iota(rows.shape, 1) & 127
    return jnp.where(lane < 64, jnp.zeros_like(rows), rows)


def route(row_ref, seg_ref, pair_ref, req_ref, tr_ref, tc_ref, meta_ref, *, rows_dev, width):
    tokens = row_ref.shape[1]
    shards = req_ref.shape[0]
    shift = rows_dev.bit_length() - 1
    sub, lane = iota((tokens, tokens), 0), iota((tokens, tokens), 1)
    owner_r = row_ref[...] >> shift
    slot_r = (row_ref[...] & (rows_dev - 1)).astype(F32)
    owner_c = jnp.sum(jnp.where(sub == lane, owner_r.astype(F32), 0.0), axis=1, keepdims=True).astype(I32)
    same = owner_c == owner_r
    rank_c = jnp.sum(jnp.where(same & (lane < sub), 1.0, 0.0), axis=1, keepdims=True).astype(I32)
    rank_r = jnp.sum(jnp.where(same & (sub < lane), 1.0, 0.0), axis=0, keepdims=True).astype(I32)
    tr_ref[...] = owner_r * width + rank_r
    tc_ref[...] = owner_c * width + rank_c
    dest = iota((shards, tokens), 0) == owner_r
    place = iota((shards, 128), 1)
    req = jnp.zeros((shards, 128), F32)
    for k in range(2 * tokens // shards):
        picked = jnp.sum(jnp.where(dest & (rank_r == k), slot_r, 0.0), axis=1, keepdims=True)
        req = jnp.where(place == k, picked, req)
    req_ref[...] = req.astype(I32).reshape(req_ref.shape)
    own = lax.axis_index("pair")
    first, second = pair_ref[0:1, :], pair_ref[1:2, :]
    span = iota((8, first.shape[1]), 0)
    as_query = jnp.max(jnp.where((first == own) & (second == span), 1.0, 0.0), axis=1, keepdims=True)
    as_key = jnp.max(jnp.where((second == own) & (first == span), 1.0, 0.0), axis=1, keepdims=True)
    zeros = jnp.sum(jnp.where(seg_ref[...] == 0, 1.0, 0.0), axis=1, keepdims=True)
    at = iota((8, 128), 1)
    meta_ref[...] = jnp.where(at == 0, as_query, jnp.where(at == 1, as_key, jnp.where(at == 2, zeros, 0.0)))


def slot_halves(slots):
    high = (slots >> 1).astype(F32).astype(BF16)
    low = (slots & 1).astype(F32).astype(BF16)
    return high, low


def find(slots_ref, table_ref, found_ref, *, width):
    shards = slots_ref.shape[0]
    rows_dev = table_ref.shape[0]
    count = shards * width
    spread = ((iota((count, shards), 0) // width) == iota((count, shards), 1)).astype(F32).astype(BF16)
    high, low = slot_halves(slots_ref[...].reshape(shards, 128))
    value = 2.0 * dot(spread, high) + dot(spread, low)
    mine = iota((count, 128), 1) == (iota((count, 128), 0) % width)
    slot = jnp.sum(jnp.where(mine, value, 0.0), axis=1, keepdims=True).astype(I32)
    pick = jnp.where(iota((count, rows_dev), 1) == slot, 1.0, 0.0).astype(BF16)
    found_ref[...] = dot(pick, table_ref[...].astype(BF16)).astype(BF16).reshape(found_ref.shape)


def project(fetched_ref, tc_ref, w_ref, x_ref, z_ref, u_ref, q_ref, kv_ref):
    width = fetched_ref.shape[2]
    count = fetched_ref.shape[0] * fetched_ref.shape[1]
    tokens = tc_ref.shape[0]
    pick = jnp.where(iota((tokens, count), 1) == tc_ref[...], 1.0, 0.0).astype(BF16)
    rows = dot(pick, fetched_ref[...].reshape(count, width))
    x_ref[...] = rows.astype(BF16)
    normed, _ = normalize(rows)
    low = normed.astype(BF16)
    outs = (u_ref.at[...], kv_ref.at[:, width:], q_ref.at[...], kv_ref.at[:, :width])

    def group(g):
        z = dot(low, w_ref[:, g * width : (g + 1) * width])
        z_ref[:, g * width : (g + 1) * width] = z
        half = 0.5 * z
        outs[g][...] = (half + half * jnp.tanh(half)).astype(BF16)

    return group


def visible(q_axis, size, q_block, k_block, zeros):
    q_pos = iota((size, size), q_axis) + q_block * size
    k_pos = iota((size, size), 1 - q_axis) + k_block * size
    least = jnp.where(q_pos >= zeros, zeros, 0)
    return jnp.where((k_pos >= least) & (k_pos <= q_pos), 1.0, 0.0)


class Ring:
    RISING = (0, 1, 2, 3, 4, 5, 7), (0, 1, 2, 4, 5, 6, 8, 9), (0, 1, 4, 5, 6, 8, 9, 12, 13), (4, 5, 7, 8, 9, 10, 11, 12, 13)
    FALLING = (0, 1, 2, 3, 4, 5), (0, 1, 4, 5, 6, 8, 9), (0, 1, 4, 5, 6, 14, 8, 9, 12, 13), (4, 5, 7, 8, 9, 10, 11, 12, 13)

    def __init__(self, source, gathered, send, recv, local, span, falling):
        self.source, self.gathered, self.send, self.recv, self.local = source, gathered, send, recv, local
        chips = span // 2
        self.g, self.p = lax.axis_index("dp"), lax.axis_index("pair")
        core, chip = self.p % 2, self.p // 2
        at = lambda step: ((chip + step) % chips) * 2 + core
        self.up, self.down, self.far = at(chips - 1 if falling else 1), at(1 if falling else chips - 1), at(2)
        self.rank = chips - 1 - chip if falling else chip
        self.falling, self.sends = falling, self.FALLING if falling else self.RISING
        self.other = chip * 2 + 1 - core

    def copy(self, i):
        p, up, down, far, other = self.p, self.up, self.down, self.far, self.other
        owner, part, to = (
            (p, 0, up),
            (p, 1, up),
            (p, 1, down),
            (p, 0, down),
            (p, 0, other),
            (p, 1, other),
            (down, 0, up),
            (up, 1, down),
            (down, 0, other),
            (down, 1, other),
            (up, 1, other),
            (up, 0, other),
            (far, 0, other),
            (far, 1, other),
            (down, 1, up),
        )[i]
        half = self.source.shape[0] // 2
        rows = pl.ds(part * half, half)
        return pltpu.make_async_remote_copy(
            src_ref=self.source.at[rows] if i < 6 else self.gathered.at[owner, rows],
            dst_ref=self.gathered.at[owner, rows],
            send_sem=self.send.at[i],
            recv_sem=self.recv.at[i],
            device_id=(self.g, to),
            device_id_type=MESH,
        )

    def own(self):
        return pltpu.make_async_copy(self.source, self.gathered.at[self.p], self.local)

    def when(self, *ranks):
        def decorate(steps):
            for rank in ranks:
                pl.when(self.rank == rank)(functools.partial(steps, rank))

        return decorate

    def start(self):
        self.own().start()

        @self.when(0, 1, 2, 3)
        def _(rank):
            for i in (0, 2, 1, 3, 4, 5):
                if i in self.sends[rank]:
                    self.copy(i).start()

    def arrive(self, *which):
        for i in which:
            self.copy(i).wait_recv()

    def after(self, arrived, *sent):
        self.arrive(arrived)
        for i in sent:
            self.copy(i).start()

    def relay_near(self):
        @self.when(0, 1, 2, 3)
        def _(rank):
            if rank == 0:
                if not self.falling:
                    self.after(2, 7)
            elif rank == 3:
                self.after(0, 8)
                self.after(1, 9)
            else:
                self.after(0, 6, 8)
                self.after(1, *((14, 9) if self.falling and rank == 2 else (9,)))

    def relay_wrap(self):
        @self.when(3)
        def _(rank):
            self.after(2, 7, 10)
            self.after(3, 11)

    def relay_far(self):
        @self.when(2, 3)
        def _(rank):
            self.after(6, 12)
            self.after(14 if self.falling and rank == 3 else 7, 13)

    def handed_own(self):
        self.arrive(4, 5)

    def handed_near(self):
        @self.when(1, 2, 3)
        def _(rank):
            self.arrive(8, 9)

    def handed_wrap(self):
        @self.when(3)
        def _(rank):
            self.arrive(10, 11)

    def handed_far(self):
        @self.when(2, 3)
        def _(rank):
            self.arrive(12, 13)

    def sent(self):
        @self.when(0, 1, 2, 3)
        def _(rank):
            for i in self.sends[rank]:
                self.copy(i).wait_send()


def attend(
    meta_ref, q_ref, kv_ref, u_ref, x_ref, w_ref, og_ref, out_ref, dhu_ref, gout_ref, dq_ref, dk_ref, dv_ref, kv_all,
    q_all, da_all, da, parts, acc, mask, local, send, recv, group, *, span
):
    own = lax.axis_index("pair")
    chips, core, chip = span // 2, own % 2, own // 2
    size, width = q_ref.shape
    kv_ring, q_ring, da_ring = (
        Ring(source, gathered, send.at[i], recv.at[i], local.at[i], span, falling)
        for i, (source, gathered, falling) in enumerate(
            ((kv_ref, kv_all, False), (q_ref, q_all, True), (da, da_all, True))
        )
    )
    for g in (3, 1, 2):
        group(g)
    kv_ring.start()
    q_ring.start()
    group(0)
    dhu_ref[...] = dot_t(og_ref[...], w_ref[...])

    def on_step(step, *actions):
        for k, action in enumerate(actions):
            if action:
                pl.when(step == k)(action)

    def block_at(step, falling):
        turn = step // 2
        shift = turn if falling else (3 * turn - (turn * (turn - 1)) // 2) % 4
        return ((chip + shift) % chips) * 2 + (core + step % 2) % 2

    def split(value, at):
        parts[at] = even_half(value)
        parts[at + 1] = odd_half(value)

    def slabs(work):
        def one(s, carry):
            first = pl.multiple_of(s * 128, 128)
            work(pl.ds(first, 128), pl.ds(pl.multiple_of(width + s * 128, 128), 128))
            return carry

        lax.fori_loop(0, width // 128, one, 0)

    def both(rows):
        return jnp.concatenate([even_half(rows), odd_half(rows)], axis=0)

    zeros = meta_ref[0:1, 2:3].astype(I32)
    split(q_ref[...] * 0.0625, 0)
    split(kv_ref[:, :width] * 0.0625, 4)
    split(kv_ref[:, width:] * 0.0625, 6)
    acc[...] = jnp.zeros_like(acc)
    dq_ref[...] = jnp.zeros_like(dq_ref)
    dk_ref[...] = jnp.zeros_like(dk_ref)
    dv_ref[...] = jnp.zeros_like(dv_ref)

    def forward(step, carry):
        j = block_at(step, False)

        def near():
            kv_ring.relay_wrap()
            kv_ring.relay_near()
            q_ring.relay_near()
            q_ring.relay_wrap()

        def far():
            kv_ring.relay_far()
            q_ring.relay_far()

        on_step(
            step, kv_ring.own().wait, kv_ring.handed_own, near, kv_ring.handed_near, None, kv_ring.handed_wrap, far,
            kv_ring.handed_far
        )

        @pl.when(j <= own)
        def _():
            mask[...] = visible(0, size, own, j, zeros) * meta_ref[pl.ds(j, 1), 0:1]

            def work(cols, late):
                keys = kv_all[j, :, cols]
                weights = []
                for half in range(2):
                    h = dot_t(parts[half, :, cols], keys)
                    weights.append(((h + h * jnp.tanh(h)) * mask[...]).astype(BF16))
                acc[:, cols] += dot(jnp.concatenate(weights, axis=1), both(kv_all[j, :, late]))

            slabs(work)

        return carry

    lax.fori_loop(0, span, forward, 0)

    normed, spread = normalize(acc[...])
    gate = u_ref[...].astype(F32)
    gated = (normed * gate).astype(BF16)
    dy = dhu_ref[...]
    da[...] = norm_back(dy * gate, normed, spread).astype(BF16)
    da_ring.start()
    split(da[...] * 0.0625, 2)
    dhu_ref[...] = dy * normed
    out_ref[...] = (dot(gated, w_ref[...]) + x_ref[...].astype(F32)).astype(BF16)
    gout_ref[...] = lax.dot_general(gated, og_ref[...], (((0,), (0,)), ((), ())), preferred_element_type=F32)
    def by_query(step, carry):
        j = block_at(step, False)

        @pl.when(j <= own)
        def _():
            mask[...] = visible(0, size, own, j, zeros) * meta_ref[pl.ds(j, 1), 0:1]

            def work(cols, late):
                keys = kv_all[j, :, cols]
                values = kv_all[j, :, late]
                grads = []
                for half in range(2):
                    h = dot_t(parts[half, :, cols], keys)
                    t = jnp.tanh(h)
                    slope = (1.0 + t) * (1.0 + h * (1.0 - t))
                    grads.append((dot_t(parts[2 + half, :, cols], values) * slope * mask[...]).astype(BF16))
                dq_ref[:, cols] += dot(jnp.concatenate(grads, axis=1), both(keys))

            slabs(work)

        return carry

    lax.fori_loop(0, span, by_query, 0)

    def by_key(step, carry):
        i = block_at(step, True)

        def mine():
            q_ring.own().wait()
            da_ring.own().wait()

        def pair(name):
            def action():
                getattr(q_ring, name)()
                getattr(da_ring, name)()

            return action

        on_step(
            step, mine, pair("handed_own"), da_ring.relay_near, pair("handed_near"), da_ring.relay_far, pair("handed_far"),
            da_ring.relay_wrap, pair("handed_wrap")
        )

        @pl.when(i >= own)
        def _():
            mask[...] = visible(1, size, i, own, zeros) * meta_ref[pl.ds(i, 1), 1:2]

            def work(cols, late):
                queries = q_all[i, :, cols]
                dafter = da_all[i, :, cols]
                grads, weights = [], []
                for half in range(2):
                    h = dot_t(parts[4 + half, :, cols], queries)
                    t = jnp.tanh(h)
                    weights.append(((h + h * t) * mask[...]).astype(BF16))
                    slope = (1.0 + t) * (1.0 + h * (1.0 - t))
                    grads.append((dot_t(parts[6 + half, :, cols], dafter) * slope * mask[...]).astype(BF16))
                dk_ref[:, cols] += dot(jnp.concatenate(grads, axis=1), both(queries))
                dv_ref[:, cols] += dot(jnp.concatenate(weights, axis=1), both(dafter))

            slabs(work)

        return carry

    lax.fori_loop(0, span, by_key, 0)
    for ring in (kv_ring, q_ring, da_ring):
        ring.sent()


def finish(
    z_ref, dhu_ref, dv_ref, dq_ref, dk_ref, x_ref, w_ref, og_ref, tr_ref, gout_ref, grads_ref, send_ref, hold, *, rows
):
    size, width = x_ref.shape
    normed, spread = normalize(x_ref[...].astype(F32))
    turned = jnp.transpose(normed).astype(BF16)
    dxn = jnp.zeros((size, width), F32)

    def place(upper, lower, at):
        count, cols = upper.shape
        top = (iota((count, cols), 0) % (2 * rows)) < rows
        first = jnp.where(top, upper, pltpu.roll(lower, rows, 0))
        second = jnp.where(top, pltpu.roll(upper, count - rows, 0), lower)
        whole_shape = (count // (2 * rows), 2 * rows, cols)
        grads_ref[0, :, :, at : at + cols] = first.reshape(whole_shape)
        grads_ref[1, :, :, at : at + cols] = second.reshape(whole_shape)

    for g, grad in enumerate((dhu_ref, dv_ref, dq_ref, dk_ref)):
        cols = slice(g * width, (g + 1) * width)
        h = 0.5 * z_ref[:, cols]
        t = jnp.tanh(h)
        slope = 0.5 * (1.0 + t) * (1.0 + h * (1.0 - t))
        dz = (grad[...] * slope).astype(BF16)
        part = dot(turned, dz)
        if g == 0:
            hold[...] = part
        elif g == 1:
            place(part, gout_ref[...], width)
        elif g == 2:
            place(part[:, : width // 2], part[:, width // 2 :], 2 * width)
        else:
            place(hold[...], part, 0)
        dxn += dot_t(dz, w_ref[:, cols])
    dx = norm_back(dxn, normed, spread) + og_ref[...].astype(F32)
    count = send_ref.shape[0] * send_ref.shape[1]
    pick = jnp.where(iota((count, size), 0) == tr_ref[...], 1.0, 0.0).astype(BF16)
    send_ref[...] = dot(pick, dx.astype(BF16)).astype(BF16).reshape(send_ref.shape)


def partner(k, groups, span):
    g, p = lax.axis_index("dp"), lax.axis_index("pair")
    chips, side = span // 2, math.isqrt(groups)
    to_p = ((p // 2 + (k // 2) % chips) % chips) * 2 + (p % 2 + k % 2) % 2
    shift = k // span
    to_g = ((g // side + shift // side) % side) * side + (g % side + shift % side) % side
    return to_g, to_p


def greet(groups, span):
    barrier = pltpu.get_barrier_semaphore()

    def hello(k, carry):
        pl.semaphore_signal(barrier, inc=1, device_id=partner(k, groups, span), device_id_type=MESH)
        return carry

    lax.fori_loop(1, groups * span, hello, 0)
    return lambda: pl.semaphore_wait(barrier, groups * span - 1)


def drain(ref, count, sem):
    part = ref.at[pl.ds(0, count)]
    pltpu.make_async_copy(part, part, sem).wait()


def push_all(source, target, send, recv, groups, span, rows):
    me = lax.axis_index("dp") * span + lax.axis_index("pair")
    used = pl.ds(0, rows)

    def push(k, carry):
        to_g, to_p = partner(k, groups, span)
        pltpu.make_async_remote_copy(
            src_ref=source.at[to_g * span + to_p, used],
            dst_ref=target.at[me, used],
            send_sem=send,
            recv_sem=recv,
            device_id=(to_g, to_p),
            device_id_type=MESH,
        ).start()
        return carry

    lax.fori_loop(1, groups * span, push, 0)

    def wait():
        all_of = target.at[pl.ds(0, groups * span - 1), used]
        pltpu.make_async_copy(all_of, all_of, send).wait()
        pltpu.make_async_copy(all_of, all_of, recv).wait()

    return wait


def keep(source, target, sem, span):
    me = lax.axis_index("dp") * span + lax.axis_index("pair")
    copy = pltpu.make_async_copy(source.at[me], target.at[me], sem)
    copy.start()
    return copy


def exchange_gradients(rows_ref, grads_ref, back_ref, parts_ref, got, part, sems, *, groups, span, bound):
    total = groups * span
    g, p = lax.axis_index("dp"), lax.axis_index("pair")
    me, core = g * span + p, p % 2
    chip, chips = me // 2, total // 2
    swap = pltpu.make_async_remote_copy(
        src_ref=grads_ref.at[1 - core],
        dst_ref=got,
        send_sem=sems.at[1],
        recv_sem=sems.at[2],
        device_id=(g, p + 1 - 2 * core),
        device_id_type=MESH,
    )
    swap.start()
    own = keep(rows_ref, back_ref, sems.at[0], span)
    landed = push_all(rows_ref, back_ref, sems.at[3], sems.at[4], groups, span, bound)
    swap.wait()

    def add(m, carry):
        part[m] = (grads_ref[core, m] + got[m]).astype(BF16)
        return carry

    lax.fori_loop(0, chips, add, 0)
    mine = pltpu.make_async_copy(part.at[chip], parts_ref.at[chip], sems.at[5])
    mine.start()

    def push_part(k, carry):
        to_g, to_p = partner(2 * k, groups, span)
        pltpu.make_async_remote_copy(
            src_ref=part.at[(to_g * span + to_p) // 2],
            dst_ref=parts_ref.at[chip],
            send_sem=sems.at[6],
            recv_sem=sems.at[7],
            device_id=(to_g, to_p),
            device_id_type=MESH,
        ).start()
        return carry

    lax.fori_loop(1, chips, push_part, 0)
    own.wait()
    mine.wait()
    landed()
    drain(parts_ref, chips - 1, sems.at[6])
    drain(parts_ref, chips - 1, sems.at[7])


def update(
    slots_ref, back_ref, table_ref, accum_ref, parts_ref, tnew_ref, anew_ref, gin_ref, gout_ref, *, width, factor
):
    shards = slots_ref.shape[0]
    rows_dev, model = table_ref.shape
    count = shards * width
    spread = ((iota((shards, count), 1) // width) == iota((shards, count), 0)).astype(F32).astype(BF16)
    high, low = slot_halves(slots_ref[...].reshape(shards, 128))
    turn = lambda a: lax.dot_general(a, spread, (((0,), (0,)), ((), ())), preferred_element_type=F32)
    value = 2.0 * turn(high) + turn(low)
    mine = iota((128, count), 0) == (iota((128, count), 1) % width)
    slot = jnp.sum(jnp.where(mine, value, 0.0), axis=0, keepdims=True).astype(I32)
    pick = jnp.where(iota((rows_dev, count), 0) == slot, 1.0, 0.0).astype(BF16)
    total = dot(pick, back_ref[...].reshape(count, model))
    square = jnp.mean(total * total, axis=1, keepdims=True)
    eye = iota((rows_dev, rows_dev), 0) == iota((rows_dev, rows_dev), 1)
    accum = jnp.sum(jnp.where(eye, accum_ref[...], 0.0), axis=1, keepdims=True) + square
    anew_ref[...] = jnp.sum(jnp.where(eye, accum, 0.0), axis=0, keepdims=True)
    tnew_ref[...] = table_ref[...] - LEARN_RATE * total / jnp.sqrt(accum)

    def add(m, summed):
        return summed + parts_ref[m].astype(F32)

    summed = lax.fori_loop(0, parts_ref.shape[0], add, jnp.zeros(parts_ref.shape[1:], F32)) * factor
    rows = gin_ref.shape[0]
    upper, lower = summed[:rows], summed[rows:]
    gin_ref[:, :model] = upper[:, :model]
    gin_ref[:, model : 2 * model] = upper[:, model : 2 * model]
    gin_ref[:, 2 * model : 2 * model + model // 2] = upper[:, 2 * model :]
    gin_ref[:, 2 * model + model // 2 : 3 * model] = lower[:, 2 * model :]
    gin_ref[:, 3 * model :] = lower[:, :model]
    gout_ref[...] = lower[:, model : 2 * model]


def layer_kernel(
    row_ref, seg_ref, pair_ref, w_in_ref, w_out_ref, og_ref, table_ref, accum_ref, out_ref, tnew_ref, anew_ref, gin_ref,
    gout_ref, request, slots, target_r, target_c, meta, found, fetched, x, z, u, q, kv, dhu, wgrad, dq, dk, dv, kv_all,
    q_all, da_all, da, parts, acc, mask, grads, hold, sending, back, got, part, landed, local, send, recv, front, sems, *,
    groups, span, width, rows, factor
):
    tokens, rows_dev = row_ref.shape[1], table_ref.shape[0]
    bound = 2 * tokens // (groups * span)
    fetched[...] = jnp.zeros_like(fetched)
    back[...] = jnp.zeros_like(back)
    ready = greet(groups, span)
    route(row_ref, seg_ref, pair_ref, request, target_r, target_c, meta, rows_dev=rows_dev, width=width)
    ready()
    own = keep(request, slots, front.at[0], span)
    asked = push_all(request, slots, front.at[1], front.at[2], groups, span, 1)
    own.wait()
    asked()
    find(slots, table_ref, found, width=width)
    own = keep(found, fetched, front.at[3], span)
    answered = push_all(found, fetched, front.at[4], front.at[5], groups, span, bound)
    own.wait()
    answered()
    group = project(fetched, target_c, w_in_ref, x, z, u, q, kv)
    attend(
        meta, q, kv, u, x, w_out_ref, og_ref, out_ref, dhu, wgrad, dq, dk, dv, kv_all, q_all, da_all, da, parts, acc,
        mask, local, send, recv, group, span=span
    )
    finish(z, dhu, dv, dq, dk, x, w_in_ref, og_ref, target_r, wgrad, grads, sending, hold, rows=rows)
    exchange_gradients(
        sending, grads, back, landed, got, part, sems, groups=groups, span=span, bound=bound
    )
    update(
        slots, back, table_ref, accum_ref, landed, tnew_ref, anew_ref, gin_ref, gout_ref, width=width, factor=factor
    )


def shape(dims, dtype):
    return jax.ShapeDtypeStruct(dims, dtype)


def body(table, accum, item_row, segments, pairs, w_in, w_out, out_grad):
    tokens = item_row.shape[0]
    rows_dev, model = table.shape
    shards = lax.axis_size(("dp", "pair"))
    span = lax.axis_size("pair")
    width = -(-(2 * tokens // shards) // 8) * 8
    rows = model // shards
    chunk = (2 * rows, 5 * model // 2)
    half_grads = (shards // 2,) + chunk
    block = lambda cols: VMEM((span, tokens, cols), BF16)
    low = lambda cols: VMEM((tokens, cols), BF16)
    high = lambda cols: VMEM((tokens, cols), F32)
    layer_out, table_new, accum_new, grad_in, grad_out = pl.pallas_call(
        functools.partial(
            layer_kernel,
            groups=shards // span,
            span=span,
            width=width,
            rows=rows,
            factor=1.0 / math.sqrt(tokens * shards),
        ),
        out_shape=(
            shape((tokens, model), BF16),
            shape((rows_dev, model), F32),
            shape((1, rows_dev), F32),
            shape((rows, 4 * model), F32),
            shape((rows, model), F32),
        ),
        in_specs=[whole()] * 8,
        out_specs=[whole()] * 5,
        scratch_shapes=[
            VMEM((shards, 1, 128), I32),
            VMEM((shards, 1, 128), I32),
            VMEM((1, tokens), I32),
            VMEM((tokens, 1), I32),
            VMEM((8, 128), F32),
            VMEM((shards, width, model), BF16),
            VMEM((shards, width, model), BF16),
            low(model),
            high(4 * model),
            low(model),
            low(model),
            low(2 * model),
            high(model),
            VMEM((model, model), F32),
            high(model),
            high(model),
            high(model),
            block(2 * model),
            block(model),
            block(model),
            low(model),
            VMEM((8, tokens, model), BF16),
            high(model),
            high(tokens),
            VMEM((2,) + half_grads, F32),
            VMEM((model, model), F32),
            VMEM((shards, width, model), BF16),
            VMEM((shards, width, model), BF16),
            VMEM(half_grads, F32),
            VMEM(half_grads, BF16),
            VMEM(half_grads, BF16),
            pltpu.SemaphoreType.DMA((3,)),
            pltpu.SemaphoreType.DMA((3, 15)),
            pltpu.SemaphoreType.DMA((3, 15)),
            pltpu.SemaphoreType.DMA((6,)),
            pltpu.SemaphoreType.DMA((8,)),
        ],
        compiler_params=params(collective_id=0, has_side_effects=True),
    )(item_row.reshape(1, tokens), segments, pairs[0].T, w_in, w_out, out_grad, table, accum.reshape(1, rows_dev))
    return layer_out, table_new, accum_new.reshape(rows_dev), grad_in, grad_out


def solution(mesh):
    both = ("dp", "pair")
    return jax.shard_map(
        body,
        mesh=mesh,
        in_specs=(
            P(both, None),
            P(both),
            P(both),
            P("dp", None),
            P("dp", None, None),
            P(),
            P(),
            P(both, None),
        ),
        out_specs=(P(both, None), P(both, None), P(both), P(both, None), P(both, None)),
        check_vma=False,
    )
```

```python
import functools
import math

import jax
import jax.numpy as jnp
from jax import lax
from jax.experimental import pallas as pl
from jax.experimental.pallas import tpu as pltpu
from jax.sharding import PartitionSpec as P

HEADS = 8
NORM_EPS = 1e-05
LEARN_RATE = 0.5
F32, BF16, I32 = jnp.float32, jnp.bfloat16, jnp.int32
VMEM = pltpu.VMEM
MESH = pl.DeviceIdType.MESH
BIG = 62 * 1024 * 1024


def whole():
    return pl.BlockSpec(memory_space=pltpu.VMEM)


def params(**kw):
    return pltpu.CompilerParams(vmem_limit_bytes=BIG, **kw)


def dot(a, b):
    return lax.dot_general(a, b, (((1,), (0,)), ((), ())), preferred_element_type=F32)


def dot_t(a, b):
    return lax.dot_general(a, b, (((1,), (1,)), ((), ())), preferred_element_type=F32)


def iota(shape, axis):
    return lax.broadcasted_iota(I32, shape, axis)


def normalize(values):
    row_mean = jnp.mean(values, axis=-1, keepdims=True)
    centred = values - row_mean
    spread = jnp.sqrt(jnp.mean(centred * centred, axis=-1, keepdims=True) + NORM_EPS)
    return centred / spread, spread


def norm_back(grad_rows, normed, spread):
    first = jnp.mean(grad_rows, axis=-1, keepdims=True)
    second = jnp.mean(grad_rows * normed, axis=-1, keepdims=True)
    return (grad_rows - first - normed * second) / spread


def even_half(rows):
    lane = iota(rows.shape, 1) & 127
    return jnp.where(lane < 64, rows, jnp.zeros_like(rows))


def odd_half(rows):
    lane = iota(rows.shape, 1) & 127
    return jnp.where(lane < 64, jnp.zeros_like(rows), rows)


def route(row_ref, seg_ref, pair_ref, req_ref, tr_ref, tc_ref, meta_ref, *, rows_dev, width):
    tokens = row_ref.shape[1]
    shards = req_ref.shape[0] * req_ref.shape[1]
    shift = rows_dev.bit_length() - 1
    sub, lane = iota((tokens, tokens), 0), iota((tokens, tokens), 1)
    owner_r = row_ref[...] >> shift
    slot_r = (row_ref[...] & (rows_dev - 1)).astype(F32)
    owner_c = jnp.sum(jnp.where(sub == lane, owner_r.astype(F32), 0.0), axis=1, keepdims=True).astype(I32)
    same = owner_c == owner_r
    rank_c = jnp.sum(jnp.where(same & (lane < sub), 1.0, 0.0), axis=1, keepdims=True).astype(I32)
    rank_r = jnp.sum(jnp.where(same & (sub < lane), 1.0, 0.0), axis=0, keepdims=True).astype(I32)
    tr_ref[...] = owner_r * width + rank_r
    tc_ref[...] = owner_c * width + rank_c
    dest = iota((shards, tokens), 0) == owner_r
    place = iota((shards, 128), 1)
    req = jnp.zeros((shards, 128), F32)
    for k in range(2 * tokens // shards):
        picked = jnp.sum(jnp.where(dest & (rank_r == k), slot_r, 0.0), axis=1, keepdims=True)
        req = jnp.where(place == k, picked, req)
    req_ref[...] = req.astype(I32).reshape(req_ref.shape)
    own = lax.axis_index("pair")
    first, second = pair_ref[0:1, :], pair_ref[1:2, :]
    span = iota((8, first.shape[1]), 0)
    as_query = jnp.max(jnp.where((first == own) & (second == span), 1.0, 0.0), axis=1, keepdims=True)
    as_key = jnp.max(jnp.where((second == own) & (first == span), 1.0, 0.0), axis=1, keepdims=True)
    zeros = jnp.sum(jnp.where(seg_ref[...] == 0, 1.0, 0.0), axis=1, keepdims=True)
    at = iota((8, 128), 1)
    meta_ref[...] = jnp.where(at == 0, as_query, jnp.where(at == 1, as_key, jnp.where(at == 2, zeros, 0.0)))


def slot_halves(slots):
    high = (slots >> 1).astype(F32).astype(BF16)
    low = (slots & 1).astype(F32).astype(BF16)
    return high, low


def find(slots_ref, table_ref, found_ref, *, width):
    shards = slots_ref.shape[0] * slots_ref.shape[1]
    rows_dev = table_ref.shape[0]
    count = shards * width
    spread = ((iota((count, shards), 0) // width) == iota((count, shards), 1)).astype(F32).astype(BF16)
    high, low = slot_halves(slots_ref[...].reshape(shards, 128))
    value = 2.0 * dot(spread, high) + dot(spread, low)
    mine = iota((count, 128), 1) == (iota((count, 128), 0) % width)
    slot = jnp.sum(jnp.where(mine, value, 0.0), axis=1, keepdims=True).astype(I32)
    pick = jnp.where(iota((count, rows_dev), 1) == slot, 1.0, 0.0).astype(BF16)
    found_ref[...] = dot(pick, table_ref[...].astype(BF16)).astype(BF16).reshape(found_ref.shape)


def project(fetched_ref, tc_ref, w_ref, x_ref, z_ref, u_ref, q_ref, kv_ref):
    width = fetched_ref.shape[2]
    count = fetched_ref.shape[0] * fetched_ref.shape[1]
    tokens = tc_ref.shape[0]
    pick = jnp.where(iota((tokens, count), 1) == tc_ref[...], 1.0, 0.0).astype(BF16)
    rows = dot(pick, fetched_ref[...].reshape(count, width))
    x_ref[...] = rows.astype(BF16)
    normed, _ = normalize(rows)
    low = normed.astype(BF16)
    outs = (u_ref.at[...], kv_ref.at[:, width:], q_ref.at[...], kv_ref.at[:, :width])

    def group(g):
        z = dot(low, w_ref[:, g * width : (g + 1) * width])
        z_ref[:, g * width : (g + 1) * width] = z
        half = 0.5 * z
        outs[g][...] = (half + half * jnp.tanh(half)).astype(BF16)

    return group


def visible(q_axis, size, q_block, k_block, zeros):
    q_pos = iota((size, size), q_axis) + q_block * size
    k_pos = iota((size, size), 1 - q_axis) + k_block * size
    least = jnp.where(q_pos >= zeros, zeros, 0)
    return jnp.where((k_pos >= least) & (k_pos <= q_pos), 1.0, 0.0)


class Ring:
    RISING = (0, 1, 2, 3, 4, 5, 7), (0, 1, 2, 4, 5, 6, 8, 9), (0, 1, 4, 5, 6, 8, 9, 12, 13), (4, 5, 7, 8, 9, 10, 11, 12, 13)
    FALLING = (0, 1, 2, 3, 4, 5), (0, 1, 4, 5, 6, 8, 9), (0, 1, 4, 5, 6, 14, 8, 9, 12, 13), (4, 5, 7, 8, 9, 10, 11, 12, 13)

    def __init__(self, source, gathered, send, recv, local, span, falling):
        self.source, self.gathered, self.send, self.recv, self.local = source, gathered, send, recv, local
        chips = span // 2
        self.g, self.p = lax.axis_index("dp"), lax.axis_index("pair")
        core, chip = self.p % 2, self.p // 2
        at = lambda step: ((chip + step) % chips) * 2 + core
        self.up, self.down, self.far = at(chips - 1 if falling else 1), at(1 if falling else chips - 1), at(2)
        self.rank = chips - 1 - chip if falling else chip
        self.falling, self.sends = falling, self.FALLING if falling else self.RISING
        self.other = chip * 2 + 1 - core

    def copy(self, i):
        p, up, down, far, other = self.p, self.up, self.down, self.far, self.other
        owner, part, to = (
            (p, 0, up),
            (p, 1, up),
            (p, 1, down),
            (p, 0, down),
            (p, 0, other),
            (p, 1, other),
            (down, 0, up),
            (up, 1, down),
            (down, 0, other),
            (down, 1, other),
            (up, 1, other),
            (up, 0, other),
            (far, 0, other),
            (far, 1, other),
            (down, 1, up),
        )[i]
        half = self.source.shape[0] // 2
        rows = pl.ds(part * half, half)
        return pltpu.make_async_remote_copy(
            src_ref=self.source.at[rows] if i < 6 else self.gathered.at[owner, rows],
            dst_ref=self.gathered.at[owner, rows],
            send_sem=self.send.at[i],
            recv_sem=self.recv.at[i],
            device_id=(self.g, to),
            device_id_type=MESH,
        )

    def own(self):
        return pltpu.make_async_copy(self.source, self.gathered.at[self.p], self.local)

    def when(self, *ranks):
        def decorate(steps):
            for rank in ranks:
                pl.when(self.rank == rank)(functools.partial(steps, rank))

        return decorate

    def start(self):
        self.own().start()

        @self.when(0, 1, 2, 3)
        def _(rank):
            for i in (0, 2, 1, 3, 4, 5):
                if i in self.sends[rank]:
                    self.copy(i).start()

    def arrive(self, *which):
        for i in which:
            self.copy(i).wait_recv()

    def after(self, arrived, *sent):
        self.arrive(arrived)
        for i in sent:
            self.copy(i).start()

    def relay_near(self):
        @self.when(0, 1, 2, 3)
        def _(rank):
            if rank == 0:
                if not self.falling:
                    self.after(2, 7)
            elif rank == 3:
                self.after(0, 8)
                self.after(1, 9)
            else:
                self.after(0, 6, 8)
                self.after(1, *((14, 9) if self.falling and rank == 2 else (9,)))

    def relay_wrap(self):
        @self.when(3)
        def _(rank):
            self.after(2, 7, 10)
            self.after(3, 11)

    def relay_far(self):
        @self.when(2, 3)
        def _(rank):
            self.after(6, 12)
            self.after(14 if self.falling and rank == 3 else 7, 13)

    def handed_own(self):
        self.arrive(4, 5)

    def handed_near(self):
        @self.when(1, 2, 3)
        def _(rank):
            self.arrive(8, 9)

    def handed_wrap(self):
        @self.when(3)
        def _(rank):
            self.arrive(10, 11)

    def handed_far(self):
        @self.when(2, 3)
        def _(rank):
            self.arrive(12, 13)

    def sent(self):
        @self.when(0, 1, 2, 3)
        def _(rank):
            for i in self.sends[rank]:
                self.copy(i).wait_send()


def attend(
    meta_ref, q_ref, kv_ref, u_ref, x_ref, w_ref, og_ref, out_ref, dhu_ref, gout_ref, dq_ref, dk_ref, dv_ref, kv_all,
    q_all, da_all, da, parts, acc, mask, local, send, recv, group, *, span
):
    own = lax.axis_index("pair")
    chips, core, chip = span // 2, own % 2, own // 2
    size, width = q_ref.shape
    kv_ring, q_ring, da_ring = (
        Ring(source, gathered, send.at[i], recv.at[i], local.at[i], span, falling)
        for i, (source, gathered, falling) in enumerate(
            ((kv_ref, kv_all, False), (q_ref, q_all, True), (da, da_all, True))
        )
    )
    for g in (3, 1, 2):
        group(g)
    kv_ring.start()
    q_ring.start()
    group(0)
    dhu_ref[...] = dot_t(og_ref[...], w_ref[...])

    def on_step(step, *actions):
        for k, action in enumerate(actions):
            if action:
                pl.when(step == k)(action)

    def block_at(step, falling):
        turn = step // 2
        shift = turn if falling else (3 * turn - (turn * (turn - 1)) // 2) % 4
        return ((chip + shift) % chips) * 2 + (core + step % 2) % 2

    def split(value, at):
        parts[at] = even_half(value)
        parts[at + 1] = odd_half(value)

    def slabs(work):
        def one(s, carry):
            first = pl.multiple_of(s * 128, 128)
            work(pl.ds(first, 128), pl.ds(pl.multiple_of(width + s * 128, 128), 128))
            return carry

        lax.fori_loop(0, width // 128, one, 0)

    def both(rows):
        return jnp.concatenate([even_half(rows), odd_half(rows)], axis=0)

    zeros = meta_ref[0:1, 2:3].astype(I32)
    split(q_ref[...] * 0.0625, 0)
    split(kv_ref[:, :width] * 0.0625, 4)
    split(kv_ref[:, width:] * 0.0625, 6)
    acc[...] = jnp.zeros_like(acc)
    dq_ref[...] = jnp.zeros_like(dq_ref)
    dk_ref[...] = jnp.zeros_like(dk_ref)
    dv_ref[...] = jnp.zeros_like(dv_ref)

    def forward(step, carry):
        j = block_at(step, False)

        def near():
            kv_ring.relay_wrap()
            kv_ring.relay_near()
            q_ring.relay_near()
            q_ring.relay_wrap()

        def far():
            kv_ring.relay_far()
            q_ring.relay_far()

        on_step(
            step, kv_ring.own().wait, kv_ring.handed_own, near, kv_ring.handed_near, None, kv_ring.handed_wrap, far,
            kv_ring.handed_far
        )

        @pl.when(j <= own)
        def _():
            mask[...] = visible(0, size, own, j, zeros) * meta_ref[pl.ds(j, 1), 0:1]

            def work(cols, late):
                keys = kv_all[j, :, cols]
                weights = []
                for half in range(2):
                    h = dot_t(parts[half, :, cols], keys)
                    weights.append((h * ((1.0 + jnp.tanh(h)) * mask[...])).astype(BF16))
                acc[:, cols] += dot(jnp.concatenate(weights, axis=1), both(kv_all[j, :, late]))

            slabs(work)

        return carry

    lax.fori_loop(0, span, forward, 0)

    normed, spread = normalize(acc[...])
    gate = u_ref[...].astype(F32)
    gated = (normed * gate).astype(BF16)
    dy = dhu_ref[...]
    da[...] = norm_back(dy * gate, normed, spread).astype(BF16)
    da_ring.start()
    split(da[...] * 0.0625, 2)
    dhu_ref[...] = dy * normed
    out_ref[...] = (dot(gated, w_ref[...]) + x_ref[...].astype(F32)).astype(BF16)
    gout_ref[...] = lax.dot_general(gated, og_ref[...], (((0,), (0,)), ((), ())), preferred_element_type=F32)
    def by_query(step, carry):
        j = block_at(step, False)

        @pl.when(j <= own)
        def _():
            mask[...] = visible(0, size, own, j, zeros) * meta_ref[pl.ds(j, 1), 0:1]

            def work(cols, late):
                keys = kv_all[j, :, cols]
                values = kv_all[j, :, late]
                grads = []
                for half in range(2):
                    h = dot_t(parts[half, :, cols], keys)
                    u = 1.0 + jnp.tanh(h)
                    seen = u * mask[...]
                    slope = seen + h * seen * (2.0 - u)
                    grads.append((dot_t(parts[2 + half, :, cols], values) * slope).astype(BF16))
                dq_ref[:, cols] += dot(jnp.concatenate(grads, axis=1), both(keys))

            slabs(work)

        return carry

    lax.fori_loop(0, span, by_query, 0)

    def by_key(step, carry):
        i = block_at(step, True)

        def mine():
            q_ring.own().wait()
            da_ring.own().wait()

        def pair(name):
            def action():
                getattr(q_ring, name)()
                getattr(da_ring, name)()

            return action

        on_step(
            step, mine, pair("handed_own"), da_ring.relay_near, pair("handed_near"), da_ring.relay_far, pair("handed_far"),
            da_ring.relay_wrap, pair("handed_wrap")
        )

        @pl.when(i >= own)
        def _():
            mask[...] = visible(1, size, i, own, zeros) * meta_ref[pl.ds(i, 1), 1:2]

            def work(cols, late):
                queries = q_all[i, :, cols]
                dafter = da_all[i, :, cols]
                grads, weights = [], []
                for half in range(2):
                    h = dot_t(parts[4 + half, :, cols], queries)
                    u = 1.0 + jnp.tanh(h)
                    seen = u * mask[...]
                    weight = h * seen
                    weights.append(weight.astype(BF16))
                    slope = seen + weight * (2.0 - u)
                    grads.append((dot_t(parts[6 + half, :, cols], dafter) * slope).astype(BF16))
                dk_ref[:, cols] += dot(jnp.concatenate(grads, axis=1), both(queries))
                dv_ref[:, cols] += dot(jnp.concatenate(weights, axis=1), both(dafter))

            slabs(work)

        return carry

    lax.fori_loop(0, span, by_key, 0)
    for ring in (kv_ring, q_ring, da_ring):
        ring.sent()


def finish(
    z_ref, dhu_ref, dv_ref, dq_ref, dk_ref, x_ref, w_ref, og_ref, tr_ref, gout_ref, grads_ref, send_ref, hold, *, rows
):
    size, width = x_ref.shape
    normed, spread = normalize(x_ref[...].astype(F32))
    turned = jnp.transpose(normed).astype(BF16)
    dxn = jnp.zeros((size, width), F32)

    def place(upper, lower, at):
        count, cols = upper.shape
        top = (iota((count, cols), 0) % (2 * rows)) < rows
        first = jnp.where(top, upper, pltpu.roll(lower, rows, 0))
        second = jnp.where(top, pltpu.roll(upper, count - rows, 0), lower)
        whole_shape = (count // (2 * rows), 2 * rows, cols)
        grads_ref[0, :, :, at : at + cols] = first.reshape(whole_shape)
        grads_ref[1, :, :, at : at + cols] = second.reshape(whole_shape)

    for g, grad in enumerate((dhu_ref, dv_ref, dq_ref, dk_ref)):
        cols = slice(g * width, (g + 1) * width)
        h = 0.5 * z_ref[:, cols]
        t = jnp.tanh(h)
        slope = 0.5 * (1.0 + t) * (1.0 + h * (1.0 - t))
        dz = (grad[...] * slope).astype(BF16)
        part = dot(turned, dz)
        if g == 0:
            hold[...] = part
        elif g == 1:
            place(part, gout_ref[...], width)
        elif g == 2:
            place(part[:, : width // 2], part[:, width // 2 :], 2 * width)
        else:
            place(hold[...], part, 0)
        dxn += dot_t(dz, w_ref[:, cols])
    dx = norm_back(dxn, normed, spread) + og_ref[...].astype(F32)
    count = send_ref.shape[0] * send_ref.shape[1]
    pick = jnp.where(iota((count, size), 0) == tr_ref[...], 1.0, 0.0).astype(BF16)
    send_ref[...] = dot(pick, dx.astype(BF16)).astype(BF16).reshape(send_ref.shape)


def partner(k, groups, span):
    g, p = lax.axis_index("dp"), lax.axis_index("pair")
    chips, side = span // 2, math.isqrt(groups)
    to_p = ((p // 2 + (k // 2) % chips) % chips) * 2 + (p % 2 + k % 2) % 2
    shift = k // span
    to_g = ((g // side + shift // side) % side) * side + (g % side + shift % side) % side
    return to_g, to_p


def greet(groups, span):
    g, p = lax.axis_index("dp"), lax.axis_index("pair")
    barrier = pltpu.get_barrier_semaphore()

    def hello(device):
        pl.semaphore_signal(barrier, inc=1, device_id=device, device_id_type=MESH)

    def hello_pair(k, carry):
        hello((g, partner(k, groups, span)[1]))
        return carry

    def hello_group(k, carry):
        hello((partner(k * span, groups, span)[0], p))
        return carry

    lax.fori_loop(1, span, hello_pair, 0)
    lax.fori_loop(1, groups, hello_group, 0)
    return lambda: pl.semaphore_wait(barrier, span + groups - 2)


def ask(request, middle, slots, sems, groups, span):
    g, p = lax.axis_index("dp"), lax.axis_index("pair")
    own = pltpu.make_async_copy(request.at[:, p], middle.at[p], sems.at[0])
    own.start()

    def over_pair(k, carry):
        to_p = partner(k, groups, span)[1]
        pltpu.make_async_remote_copy(
            src_ref=request.at[:, to_p],
            dst_ref=middle.at[p],
            send_sem=sems.at[1],
            recv_sem=sems.at[2],
            device_id=(g, to_p),
            device_id_type=MESH,
        ).start()
        return carry

    lax.fori_loop(1, span, over_pair, 0)
    own.wait()
    drain(middle, span - 1, sems.at[1])
    drain(middle, span - 1, sems.at[2])
    own = pltpu.make_async_copy(middle.at[:, g], slots.at[g], sems.at[3])
    own.start()

    def over_groups(k, carry):
        to_g = partner(k * span, groups, span)[0]
        pltpu.make_async_remote_copy(
            src_ref=middle.at[:, to_g],
            dst_ref=slots.at[g],
            send_sem=sems.at[4],
            recv_sem=sems.at[5],
            device_id=(to_g, p),
            device_id_type=MESH,
        ).start()
        return carry

    lax.fori_loop(1, groups, over_groups, 0)
    own.wait()
    if groups > 1:
        drain(slots, groups - 1, sems.at[4])
        drain(slots, groups - 1, sems.at[5])


def drain(ref, count, sem):
    part = ref.at[pl.ds(0, count)]
    pltpu.make_async_copy(part, part, sem).wait()


def push_all(source, target, send, recv, groups, span, rows):
    me = lax.axis_index("dp") * span + lax.axis_index("pair")
    used = pl.ds(0, rows)

    def push(k, carry):
        to_g, to_p = partner(k, groups, span)
        pltpu.make_async_remote_copy(
            src_ref=source.at[to_g * span + to_p, used],
            dst_ref=target.at[me, used],
            send_sem=send,
            recv_sem=recv,
            device_id=(to_g, to_p),
            device_id_type=MESH,
        ).start()
        return carry

    lax.fori_loop(1, groups * span, push, 0)

    def wait():
        all_of = target.at[pl.ds(0, groups * span - 1), used]
        pltpu.make_async_copy(all_of, all_of, send).wait()
        pltpu.make_async_copy(all_of, all_of, recv).wait()

    return wait


def keep(source, target, sem, span):
    me = lax.axis_index("dp") * span + lax.axis_index("pair")
    copy = pltpu.make_async_copy(source.at[me], target.at[me], sem)
    copy.start()
    return copy


def exchange_gradients(rows_ref, grads_ref, back_ref, parts_ref, got, part, sems, *, groups, span, bound):
    total = groups * span
    g, p = lax.axis_index("dp"), lax.axis_index("pair")
    me, core = g * span + p, p % 2
    chip, chips = me // 2, total // 2
    swap = pltpu.make_async_remote_copy(
        src_ref=grads_ref.at[1 - core],
        dst_ref=got,
        send_sem=sems.at[1],
        recv_sem=sems.at[2],
        device_id=(g, p + 1 - 2 * core),
        device_id_type=MESH,
    )
    swap.start()
    own = keep(rows_ref, back_ref, sems.at[0], span)
    landed = push_all(rows_ref, back_ref, sems.at[3], sems.at[4], groups, span, bound)
    swap.wait()

    def add(m, carry):
        part[m] = (grads_ref[core, m] + got[m]).astype(BF16)
        return carry

    lax.fori_loop(0, chips, add, 0)
    mine = pltpu.make_async_copy(part.at[chip], parts_ref.at[chip], sems.at[5])
    mine.start()

    def push_part(k, carry):
        to_g, to_p = partner(2 * k, groups, span)
        pltpu.make_async_remote_copy(
            src_ref=part.at[(to_g * span + to_p) // 2],
            dst_ref=parts_ref.at[chip],
            send_sem=sems.at[6],
            recv_sem=sems.at[7],
            device_id=(to_g, to_p),
            device_id_type=MESH,
        ).start()
        return carry

    lax.fori_loop(1, chips, push_part, 0)
    own.wait()
    mine.wait()
    landed()
    drain(parts_ref, chips - 1, sems.at[6])
    drain(parts_ref, chips - 1, sems.at[7])


def update(
    slots_ref, back_ref, table_ref, accum_ref, parts_ref, tnew_ref, anew_ref, gin_ref, gout_ref, *, width, factor
):
    shards = slots_ref.shape[0] * slots_ref.shape[1]
    rows_dev, model = table_ref.shape
    count = shards * width
    spread = ((iota((shards, count), 1) // width) == iota((shards, count), 0)).astype(F32).astype(BF16)
    high, low = slot_halves(slots_ref[...].reshape(shards, 128))
    turn = lambda a: lax.dot_general(a, spread, (((0,), (0,)), ((), ())), preferred_element_type=F32)
    value = 2.0 * turn(high) + turn(low)
    mine = iota((128, count), 0) == (iota((128, count), 1) % width)
    slot = jnp.sum(jnp.where(mine, value, 0.0), axis=0, keepdims=True).astype(I32)
    pick = jnp.where(iota((rows_dev, count), 0) == slot, 1.0, 0.0).astype(BF16)
    total = dot(pick, back_ref[...].reshape(count, model))
    square = jnp.mean(total * total, axis=1, keepdims=True)
    eye = iota((rows_dev, rows_dev), 0) == iota((rows_dev, rows_dev), 1)
    accum = jnp.sum(jnp.where(eye, accum_ref[...], 0.0), axis=1, keepdims=True) + square
    anew_ref[...] = jnp.sum(jnp.where(eye, accum, 0.0), axis=0, keepdims=True)
    tnew_ref[...] = table_ref[...] - LEARN_RATE * total / jnp.sqrt(accum)

    def add(m, summed):
        return summed + parts_ref[m].astype(F32)

    summed = lax.fori_loop(0, parts_ref.shape[0], add, jnp.zeros(parts_ref.shape[1:], F32)) * factor
    rows = gin_ref.shape[0]
    upper, lower = summed[:rows], summed[rows:]
    gin_ref[:, :model] = upper[:, :model]
    gin_ref[:, model : 2 * model] = upper[:, model : 2 * model]
    gin_ref[:, 2 * model : 2 * model + model // 2] = upper[:, 2 * model :]
    gin_ref[:, 2 * model + model // 2 : 3 * model] = lower[:, 2 * model :]
    gin_ref[:, 3 * model :] = lower[:, :model]
    gout_ref[...] = lower[:, model : 2 * model]


def layer_kernel(
    row_ref, seg_ref, pair_ref, w_in_ref, w_out_ref, og_ref, table_ref, accum_ref, out_ref, tnew_ref, anew_ref, gin_ref,
    gout_ref, request, middle, slots, target_r, target_c, meta, found, fetched, x, z, u, q, kv, dhu, wgrad, dq, dk, dv, kv_all,
    q_all, da_all, da, parts, acc, mask, grads, hold, sending, back, got, part, landed, local, send, recv, front, sems, *,
    groups, span, width, rows, factor
):
    tokens, rows_dev = row_ref.shape[1], table_ref.shape[0]
    bound = 2 * tokens // (groups * span)
    fetched[...] = jnp.zeros_like(fetched)
    back[...] = jnp.zeros_like(back)
    ready = greet(groups, span)
    route(row_ref, seg_ref, pair_ref, request, target_r, target_c, meta, rows_dev=rows_dev, width=width)
    ready()
    ask(request, middle, slots, front, groups, span)
    find(slots, table_ref, found, width=width)
    own = keep(found, fetched, front.at[6], span)
    answered = push_all(found, fetched, front.at[7], front.at[8], groups, span, bound)
    own.wait()
    answered()
    group = project(fetched, target_c, w_in_ref, x, z, u, q, kv)
    attend(
        meta, q, kv, u, x, w_out_ref, og_ref, out_ref, dhu, wgrad, dq, dk, dv, kv_all, q_all, da_all, da, parts, acc,
        mask, local, send, recv, group, span=span
    )
    finish(z, dhu, dv, dq, dk, x, w_in_ref, og_ref, target_r, wgrad, grads, sending, hold, rows=rows)
    exchange_gradients(
        sending, grads, back, landed, got, part, sems, groups=groups, span=span, bound=bound
    )
    update(
        slots, back, table_ref, accum_ref, landed, tnew_ref, anew_ref, gin_ref, gout_ref, width=width, factor=factor
    )


def shape(dims, dtype):
    return jax.ShapeDtypeStruct(dims, dtype)


def body(table, accum, item_row, segments, pairs, w_in, w_out, out_grad):
    tokens = item_row.shape[0]
    rows_dev, model = table.shape
    shards = lax.axis_size(("dp", "pair"))
    span = lax.axis_size("pair")
    width = -(-(2 * tokens // shards) // 8) * 8
    rows = model // shards
    chunk = (2 * rows, 5 * model // 2)
    half_grads = (shards // 2,) + chunk
    block = lambda cols: VMEM((span, tokens, cols), BF16)
    low = lambda cols: VMEM((tokens, cols), BF16)
    high = lambda cols: VMEM((tokens, cols), F32)
    layer_out, table_new, accum_new, grad_in, grad_out = pl.pallas_call(
        functools.partial(
            layer_kernel,
            groups=shards // span,
            span=span,
            width=width,
            rows=rows,
            factor=1.0 / math.sqrt(tokens * shards),
        ),
        out_shape=(
            shape((tokens, model), BF16),
            shape((rows_dev, model), F32),
            shape((1, rows_dev), F32),
            shape((rows, 4 * model), F32),
            shape((rows, model), F32),
        ),
        in_specs=[whole()] * 8,
        out_specs=[whole()] * 5,
        scratch_shapes=[
            VMEM((shards // span, span, 1, 128), I32),
            VMEM((span, shards // span, 1, 128), I32),
            VMEM((shards // span, span, 1, 128), I32),
            VMEM((1, tokens), I32),
            VMEM((tokens, 1), I32),
            VMEM((8, 128), F32),
            VMEM((shards, width, model), BF16),
            VMEM((shards, width, model), BF16),
            low(model),
            high(4 * model),
            low(model),
            low(model),
            low(2 * model),
            high(model),
            VMEM((model, model), F32),
            high(model),
            high(model),
            high(model),
            block(2 * model),
            block(model),
            block(model),
            low(model),
            VMEM((8, tokens, model), BF16),
            high(model),
            high(tokens),
            VMEM((2,) + half_grads, F32),
            VMEM((model, model), F32),
            VMEM((shards, width, model), BF16),
            VMEM((shards, width, model), BF16),
            VMEM(half_grads, F32),
            VMEM(half_grads, BF16),
            VMEM(half_grads, BF16),
            pltpu.SemaphoreType.DMA((3,)),
            pltpu.SemaphoreType.DMA((3, 15)),
            pltpu.SemaphoreType.DMA((3, 15)),
            pltpu.SemaphoreType.DMA((9,)),
            pltpu.SemaphoreType.DMA((8,)),
        ],
        compiler_params=params(collective_id=0, has_side_effects=True),
    )(item_row.reshape(1, tokens), segments, pairs[0].T, w_in, w_out, out_grad, table, accum.reshape(1, rows_dev))
    return layer_out, table_new, accum_new.reshape(rows_dev), grad_in, grad_out


def solution(mesh):
    both = ("dp", "pair")
    return jax.shard_map(
        body,
        mesh=mesh,
        in_specs=(
            P(both, None),
            P(both),
            P(both),
            P("dp", None),
            P("dp", None, None),
            P(),
            P(),
            P(both, None),
        ),
        out_specs=(P(both, None), P(both, None), P(both), P(both, None), P(both, None)),
        check_vma=False,
    )
```

```python
import functools
import math

import jax
import jax.numpy as jnp
from jax import lax
from jax.experimental import pallas as pl
from jax.experimental.pallas import tpu as pltpu
from jax.sharding import PartitionSpec as P

HEADS = 8
NORM_EPS = 1e-05
LEARN_RATE = 0.5
F32, BF16, I32 = jnp.float32, jnp.bfloat16, jnp.int32
VMEM = pltpu.VMEM
MESH = pl.DeviceIdType.MESH
BIG = 62 * 1024 * 1024


def whole():
    return pl.BlockSpec(memory_space=pltpu.VMEM)


def params(**kw):
    return pltpu.CompilerParams(vmem_limit_bytes=BIG, **kw)


def dot(a, b):
    return lax.dot_general(a, b, (((1,), (0,)), ((), ())), preferred_element_type=F32)


def dot_t(a, b):
    return lax.dot_general(a, b, (((1,), (1,)), ((), ())), preferred_element_type=F32)


def iota(shape, axis):
    return lax.broadcasted_iota(I32, shape, axis)


def normalize(values):
    row_mean = jnp.mean(values, axis=-1, keepdims=True)
    centred = values - row_mean
    spread = jnp.sqrt(jnp.mean(centred * centred, axis=-1, keepdims=True) + NORM_EPS)
    return centred / spread, spread


def norm_back(grad_rows, normed, spread):
    first = jnp.mean(grad_rows, axis=-1, keepdims=True)
    second = jnp.mean(grad_rows * normed, axis=-1, keepdims=True)
    return (grad_rows - first - normed * second) / spread


def even_half(rows):
    lane = iota(rows.shape, 1) & 127
    return jnp.where(lane < 64, rows, jnp.zeros_like(rows))


def odd_half(rows):
    lane = iota(rows.shape, 1) & 127
    return jnp.where(lane < 64, jnp.zeros_like(rows), rows)


def route(row_ref, seg_ref, pair_ref, req_ref, tr_ref, tc_ref, meta_ref, *, rows_dev, width):
    tokens = row_ref.shape[1]
    shards = req_ref.shape[0] * req_ref.shape[1]
    shift = rows_dev.bit_length() - 1
    sub, lane = iota((tokens, tokens), 0), iota((tokens, tokens), 1)
    owner_r = row_ref[...] >> shift
    slot_r = (row_ref[...] & (rows_dev - 1)).astype(F32)
    owner_c = jnp.sum(jnp.where(sub == lane, owner_r.astype(F32), 0.0), axis=1, keepdims=True).astype(I32)
    same = owner_c == owner_r
    rank_c = jnp.sum(jnp.where(same & (lane < sub), 1.0, 0.0), axis=1, keepdims=True).astype(I32)
    rank_r = jnp.sum(jnp.where(same & (sub < lane), 1.0, 0.0), axis=0, keepdims=True).astype(I32)
    tr_ref[...] = owner_r * width + rank_r
    tc_ref[...] = owner_c * width + rank_c
    dest = iota((shards, tokens), 0) == owner_r
    place = iota((shards, 128), 1)
    req = jnp.zeros((shards, 128), F32)
    for k in range(2 * tokens // shards):
        picked = jnp.sum(jnp.where(dest & (rank_r == k), slot_r, 0.0), axis=1, keepdims=True)
        req = jnp.where(place == k, picked, req)
    req_ref[...] = req.astype(I32).reshape(req_ref.shape)
    own = lax.axis_index("pair")
    first, second = pair_ref[0:1, :], pair_ref[1:2, :]
    span = iota((8, first.shape[1]), 0)
    as_query = jnp.max(jnp.where((first == own) & (second == span), 1.0, 0.0), axis=1, keepdims=True)
    as_key = jnp.max(jnp.where((second == own) & (first == span), 1.0, 0.0), axis=1, keepdims=True)
    zeros = jnp.sum(jnp.where(seg_ref[...] == 0, 1.0, 0.0), axis=1, keepdims=True)
    at = iota((8, 128), 1)
    meta_ref[...] = jnp.where(at == 0, as_query, jnp.where(at == 1, as_key, jnp.where(at == 2, zeros, 0.0)))


def slot_halves(slots):
    high = (slots >> 1).astype(F32).astype(BF16)
    low = (slots & 1).astype(F32).astype(BF16)
    return high, low


def find(slots_ref, table_ref, found_ref, *, width):
    shards = slots_ref.shape[0] * slots_ref.shape[1]
    rows_dev = table_ref.shape[0]
    count = shards * width
    spread = ((iota((count, shards), 0) // width) == iota((count, shards), 1)).astype(F32).astype(BF16)
    high, low = slot_halves(slots_ref[...].reshape(shards, 128))
    value = 2.0 * dot(spread, high) + dot(spread, low)
    mine = iota((count, 128), 1) == (iota((count, 128), 0) % width)
    slot = jnp.sum(jnp.where(mine, value, 0.0), axis=1, keepdims=True).astype(I32)
    pick = jnp.where(iota((count, rows_dev), 1) == slot, 1.0, 0.0).astype(BF16)
    found_ref[...] = dot(pick, table_ref[...].astype(BF16)).astype(BF16).reshape(found_ref.shape)


def project(fetched_ref, tc_ref, w_ref, x_ref, z_ref, u_ref, q_ref, kv_ref, turned_ref):
    width = fetched_ref.shape[2]
    count = fetched_ref.shape[0] * fetched_ref.shape[1]
    tokens = tc_ref.shape[0]
    pick = jnp.where(iota((tokens, count), 1) == tc_ref[...], 1.0, 0.0).astype(BF16)
    rows = dot(pick, fetched_ref[...].reshape(count, width))
    x_ref[...] = rows.astype(BF16)
    normed, _ = normalize(rows)
    low = normed.astype(BF16)
    turned_ref[...] = jnp.transpose(normed).astype(BF16)
    outs = (u_ref.at[...], kv_ref.at[:, width:], q_ref.at[...], kv_ref.at[:, :width])

    def group(g):
        z = dot(low, w_ref[:, g * width : (g + 1) * width])
        z_ref[:, g * width : (g + 1) * width] = z
        half = 0.5 * z
        outs[g][...] = (half + half * jnp.tanh(half)).astype(BF16)

    return group


def visible(q_axis, size, q_block, k_block, zeros):
    q_pos = iota((size, size), q_axis) + q_block * size
    k_pos = iota((size, size), 1 - q_axis) + k_block * size
    least = jnp.where(q_pos >= zeros, zeros, 0)
    return jnp.where((k_pos >= least) & (k_pos <= q_pos), 1.0, 0.0)


class Ring:
    RISING = (0, 1, 2, 3, 4, 5, 7), (0, 1, 2, 4, 5, 6, 8, 9), (0, 1, 4, 5, 6, 8, 9, 12, 13), (4, 5, 7, 8, 9, 10, 11, 12, 13)
    FALLING = (0, 1, 2, 3, 4, 5), (0, 1, 4, 5, 6, 8, 9), (0, 1, 4, 5, 6, 14, 8, 9, 12, 13), (4, 5, 7, 8, 9, 10, 11, 12, 13)

    def __init__(self, source, gathered, send, recv, local, span, falling):
        self.source, self.gathered, self.send, self.recv, self.local = source, gathered, send, recv, local
        chips = span // 2
        self.g, self.p = lax.axis_index("dp"), lax.axis_index("pair")
        core, chip = self.p % 2, self.p // 2
        at = lambda step: ((chip + step) % chips) * 2 + core
        self.up, self.down, self.far = at(chips - 1 if falling else 1), at(1 if falling else chips - 1), at(2)
        self.rank = chips - 1 - chip if falling else chip
        self.falling, self.sends = falling, self.FALLING if falling else self.RISING
        self.other = chip * 2 + 1 - core

    def copy(self, i):
        p, up, down, far, other = self.p, self.up, self.down, self.far, self.other
        owner, part, to = (
            (p, 0, up),
            (p, 1, up),
            (p, 1, down),
            (p, 0, down),
            (p, 0, other),
            (p, 1, other),
            (down, 0, up),
            (up, 1, down),
            (down, 0, other),
            (down, 1, other),
            (up, 1, other),
            (up, 0, other),
            (far, 0, other),
            (far, 1, other),
            (down, 1, up),
        )[i]
        half = self.source.shape[0] // 2
        rows = pl.ds(part * half, half)
        return pltpu.make_async_remote_copy(
            src_ref=self.source.at[rows] if i < 6 else self.gathered.at[owner, rows],
            dst_ref=self.gathered.at[owner, rows],
            send_sem=self.send.at[i],
            recv_sem=self.recv.at[i],
            device_id=(self.g, to),
            device_id_type=MESH,
        )

    def own(self):
        return pltpu.make_async_copy(self.source, self.gathered.at[self.p], self.local)

    def when(self, *ranks):
        def decorate(steps):
            for rank in ranks:
                pl.when(self.rank == rank)(functools.partial(steps, rank))

        return decorate

    def start(self):
        self.own().start()

        @self.when(0, 1, 2, 3)
        def _(rank):
            for i in (0, 2, 1, 3, 4, 5):
                if i in self.sends[rank]:
                    self.copy(i).start()

    def arrive(self, *which):
        for i in which:
            self.copy(i).wait_recv()

    def after(self, arrived, *sent):
        self.arrive(arrived)
        for i in sent:
            self.copy(i).start()

    def relay_near(self):
        @self.when(0, 1, 2, 3)
        def _(rank):
            if rank == 0:
                if not self.falling:
                    self.after(2, 7)
            elif rank == 3:
                self.after(0, 8)
                self.after(1, 9)
            else:
                self.after(0, 6, 8)
                self.after(1, *((14, 9) if self.falling and rank == 2 else (9,)))

    def relay_wrap(self):
        @self.when(3)
        def _(rank):
            self.after(2, 7, 10)
            self.after(3, 11)

    def relay_far(self):
        @self.when(2, 3)
        def _(rank):
            self.after(6, 12)
            self.after(14 if self.falling and rank == 3 else 7, 13)

    def handed_own(self):
        self.arrive(4, 5)

    def handed_near(self):
        @self.when(1, 2, 3)
        def _(rank):
            self.arrive(8, 9)

    def handed_wrap(self):
        @self.when(3)
        def _(rank):
            self.arrive(10, 11)

    def handed_far(self):
        @self.when(2, 3)
        def _(rank):
            self.arrive(12, 13)

    def sent(self):
        @self.when(0, 1, 2, 3)
        def _(rank):
            for i in self.sends[rank]:
                self.copy(i).wait_send()


def attend(
    meta_ref, q_ref, kv_ref, u_ref, x_ref, w_ref, og_ref, out_ref, dhu_ref, gout_ref, dq_ref, dk_ref, dv_ref, kv_all,
    q_all, da_all, da, parts, acc, mask, local, send, recv, group, early, *, span
):
    own = lax.axis_index("pair")
    chips, core, chip = span // 2, own % 2, own // 2
    size, width = q_ref.shape
    kv_ring, q_ring, da_ring = (
        Ring(source, gathered, send.at[i], recv.at[i], local.at[i], span, falling)
        for i, (source, gathered, falling) in enumerate(
            ((kv_ref, kv_all, False), (q_ref, q_all, True), (da, da_all, True))
        )
    )
    for g in (3, 1, 2):
        group(g)
    kv_ring.start()
    q_ring.start()
    group(0)
    dhu_ref[...] = dot_t(og_ref[...], w_ref[...])

    def on_step(step, *actions):
        for k, action in enumerate(actions):
            if action:
                pl.when(step == k)(action)

    def block_at(step, falling):
        turn = step // 2
        shift = turn if falling else (3 * turn - (turn * (turn - 1)) // 2) % 4
        return ((chip + shift) % chips) * 2 + (core + step % 2) % 2

    def split(value, at):
        parts[at] = even_half(value)
        parts[at + 1] = odd_half(value)

    def slabs(work):
        def one(s, carry):
            first = pl.multiple_of(s * 128, 128)
            work(pl.ds(first, 128), pl.ds(pl.multiple_of(width + s * 128, 128), 128))
            return carry

        lax.fori_loop(0, width // 128, one, 0)

    def both(rows):
        return jnp.concatenate([even_half(rows), odd_half(rows)], axis=0)

    zeros = meta_ref[0:1, 2:3].astype(I32)
    split(q_ref[...] * 0.0625, 0)
    split(kv_ref[:, :width] * 0.0625, 4)
    split(kv_ref[:, width:] * 0.0625, 6)
    acc[...] = jnp.zeros_like(acc)
    dq_ref[...] = jnp.zeros_like(dq_ref)
    dk_ref[...] = jnp.zeros_like(dk_ref)
    dv_ref[...] = jnp.zeros_like(dv_ref)

    def forward(step, carry):
        j = block_at(step, False)

        def near():
            kv_ring.relay_wrap()
            kv_ring.relay_near()
            q_ring.relay_near()
            q_ring.relay_wrap()

        def far():
            kv_ring.relay_far()
            q_ring.relay_far()

        on_step(
            step, kv_ring.own().wait, kv_ring.handed_own, near, kv_ring.handed_near, None, kv_ring.handed_wrap, far,
            kv_ring.handed_far
        )

        @pl.when(j <= own)
        def _():
            mask[...] = visible(0, size, own, j, zeros) * meta_ref[pl.ds(j, 1), 0:1]

            def work(cols, late):
                keys = kv_all[j, :, cols]
                weights = []
                for half in range(2):
                    h = dot_t(parts[half, :, cols], keys)
                    weights.append((h * ((1.0 + jnp.tanh(h)) * mask[...])).astype(BF16))
                acc[:, cols] += dot(jnp.concatenate(weights, axis=1), both(kv_all[j, :, late]))

            slabs(work)

        return carry

    lax.fori_loop(0, span, forward, 0)

    normed, spread = normalize(acc[...])
    gate = u_ref[...].astype(F32)
    gated = (normed * gate).astype(BF16)
    dy = dhu_ref[...]
    da[...] = norm_back(dy * gate, normed, spread).astype(BF16)
    da_ring.start()
    split(da[...] * 0.0625, 2)
    dhu_ref[...] = dy * normed
    out_ref[...] = (dot(gated, w_ref[...]) + x_ref[...].astype(F32)).astype(BF16)
    gout_ref[...] = lax.dot_general(gated, og_ref[...], (((0,), (0,)), ((), ())), preferred_element_type=F32)
    early(0)

    def by_query(step, carry):
        j = block_at(step, False)

        @pl.when(j <= own)
        def _():
            mask[...] = visible(0, size, own, j, zeros) * meta_ref[pl.ds(j, 1), 0:1]

            def work(cols, late):
                keys = kv_all[j, :, cols]
                values = kv_all[j, :, late]
                grads = []
                for half in range(2):
                    h = dot_t(parts[half, :, cols], keys)
                    u = 1.0 + jnp.tanh(h)
                    seen = u * mask[...]
                    slope = seen + h * seen * (2.0 - u)
                    grads.append((dot_t(parts[2 + half, :, cols], values) * slope).astype(BF16))
                dq_ref[:, cols] += dot(jnp.concatenate(grads, axis=1), both(keys))

            slabs(work)

        return carry

    lax.fori_loop(0, span, by_query, 0)
    early(1)

    def by_key(step, carry):
        i = block_at(step, True)

        def mine():
            q_ring.own().wait()
            da_ring.own().wait()

        def pair(name):
            def action():
                getattr(q_ring, name)()
                getattr(da_ring, name)()

            return action

        on_step(
            step, mine, pair("handed_own"), da_ring.relay_near, pair("handed_near"), da_ring.relay_far, pair("handed_far"),
            da_ring.relay_wrap, pair("handed_wrap")
        )

        @pl.when(i >= own)
        def _():
            mask[...] = visible(1, size, i, own, zeros) * meta_ref[pl.ds(i, 1), 1:2]

            def work(cols, late):
                queries = q_all[i, :, cols]
                dafter = da_all[i, :, cols]
                grads, weights = [], []
                for half in range(2):
                    h = dot_t(parts[4 + half, :, cols], queries)
                    u = 1.0 + jnp.tanh(h)
                    seen = u * mask[...]
                    weight = h * seen
                    weights.append(weight.astype(BF16))
                    slope = seen + weight * (2.0 - u)
                    grads.append((dot_t(parts[6 + half, :, cols], dafter) * slope).astype(BF16))
                dk_ref[:, cols] += dot(jnp.concatenate(grads, axis=1), both(queries))
                dv_ref[:, cols] += dot(jnp.concatenate(weights, axis=1), both(dafter))

            slabs(work)

        return carry

    lax.fori_loop(0, span, by_key, 0)
    for ring in (kv_ring, q_ring, da_ring):
        ring.sent()


def interleave(upper, lower, rows, out_ref):
    count, cols = upper.shape
    top = (iota((count, cols), 0) % (2 * rows)) < rows
    first = jnp.where(top, upper, pltpu.roll(lower, rows, 0))
    second = jnp.where(top, pltpu.roll(upper, count - rows, 0), lower)
    out_ref[0] = first.reshape(out_ref.shape[1:])
    out_ref[1] = second.reshape(out_ref.shape[1:])


def weigh(g, grad, z_ref, turned_ref, w_ref, dxn_ref):
    width = grad.shape[1]
    cols = slice(g * width, (g + 1) * width)
    h = 0.5 * z_ref[:, cols]
    t = jnp.tanh(h)
    slope = 0.5 * (1.0 + t) * (1.0 + h * (1.0 - t))
    dz = (grad * slope).astype(BF16)
    dxn_ref[...] += dot_t(dz, w_ref[:, cols])
    return dot(turned_ref[...], dz)


def finish(dxn_ref, x_ref, og_ref, tr_ref, send_ref):
    size = x_ref.shape[0]
    normed, spread = normalize(x_ref[...].astype(F32))
    dx = norm_back(dxn_ref[...], normed, spread) + og_ref[...].astype(F32)
    count = send_ref.shape[0] * send_ref.shape[1]
    pick = jnp.where(iota((count, size), 0) == tr_ref[...], 1.0, 0.0).astype(BF16)
    send_ref[...] = dot(pick, dx.astype(BF16)).astype(BF16).reshape(send_ref.shape)


def partner(k, groups, span):
    g, p = lax.axis_index("dp"), lax.axis_index("pair")
    chips, side = span // 2, math.isqrt(groups)
    to_p = ((p // 2 + (k // 2) % chips) % chips) * 2 + (p % 2 + k % 2) % 2
    shift = k // span
    to_g = ((g // side + shift // side) % side) * side + (g % side + shift % side) % side
    return to_g, to_p


def greet(groups, span):
    g, p = lax.axis_index("dp"), lax.axis_index("pair")
    barrier = pltpu.get_barrier_semaphore()

    def hello(device):
        pl.semaphore_signal(barrier, inc=1, device_id=device, device_id_type=MESH)

    def hello_pair(k, carry):
        hello((g, partner(k, groups, span)[1]))
        return carry

    def hello_group(k, carry):
        hello((partner(k * span, groups, span)[0], p))
        return carry

    lax.fori_loop(1, span, hello_pair, 0)
    lax.fori_loop(1, groups, hello_group, 0)
    return lambda: pl.semaphore_wait(barrier, span + groups - 2)


def ask(request, middle, slots, sems, groups, span):
    g, p = lax.axis_index("dp"), lax.axis_index("pair")
    own = pltpu.make_async_copy(request.at[:, p], middle.at[p], sems.at[0])
    own.start()

    def over_pair(k, carry):
        to_p = partner(k, groups, span)[1]
        pltpu.make_async_remote_copy(
            src_ref=request.at[:, to_p],
            dst_ref=middle.at[p],
            send_sem=sems.at[1],
            recv_sem=sems.at[2],
            device_id=(g, to_p),
            device_id_type=MESH,
        ).start()
        return carry

    lax.fori_loop(1, span, over_pair, 0)
    own.wait()
    drain(middle, span - 1, sems.at[1])
    drain(middle, span - 1, sems.at[2])
    own = pltpu.make_async_copy(middle.at[:, g], slots.at[g], sems.at[3])
    own.start()

    def over_groups(k, carry):
        to_g = partner(k * span, groups, span)[0]
        pltpu.make_async_remote_copy(
            src_ref=middle.at[:, to_g],
            dst_ref=slots.at[g],
            send_sem=sems.at[4],
            recv_sem=sems.at[5],
            device_id=(to_g, p),
            device_id_type=MESH,
        ).start()
        return carry

    lax.fori_loop(1, groups, over_groups, 0)
    own.wait()
    if groups > 1:
        drain(slots, groups - 1, sems.at[4])
        drain(slots, groups - 1, sems.at[5])


def drain(ref, count, sem):
    part = ref.at[pl.ds(0, count)]
    pltpu.make_async_copy(part, part, sem).wait()


def push_all(source, target, send, recv, groups, span, rows):
    me = lax.axis_index("dp") * span + lax.axis_index("pair")
    used = pl.ds(0, rows)

    def push(k, carry):
        to_g, to_p = partner(k, groups, span)
        pltpu.make_async_remote_copy(
            src_ref=source.at[to_g * span + to_p, used],
            dst_ref=target.at[me, used],
            send_sem=send,
            recv_sem=recv,
            device_id=(to_g, to_p),
            device_id_type=MESH,
        ).start()
        return carry

    lax.fori_loop(1, groups * span, push, 0)

    def wait():
        all_of = target.at[pl.ds(0, groups * span - 1), used]
        pltpu.make_async_copy(all_of, all_of, send).wait()
        pltpu.make_async_copy(all_of, all_of, recv).wait()

    return wait


def keep(source, target, sem, span):
    me = lax.axis_index("dp") * span + lax.axis_index("pair")
    copy = pltpu.make_async_copy(source.at[me], target.at[me], sem)
    copy.start()
    return copy


def push_early(early_ref, arrived_ref, cols, sems, groups, span):
    g, p = lax.axis_index("dp"), lax.axis_index("pair")
    count = early_ref.shape[0] // groups

    def mine(to_g):
        return early_ref.at[pl.ds(pl.multiple_of(to_g * count, count), count), cols]

    own = pltpu.make_async_copy(mine(g), arrived_ref.at[g, :, cols], sems.at[0])
    own.start()

    def push(k, carry):
        to_g = partner(k * span, groups, span)[0]
        pltpu.make_async_remote_copy(
            src_ref=mine(to_g),
            dst_ref=arrived_ref.at[g, :, cols],
            send_sem=sems.at[1],
            recv_sem=sems.at[2],
            device_id=(to_g, p),
            device_id_type=MESH,
        ).start()
        return carry

    lax.fori_loop(1, groups, push, 0)


def wait_early(early_ref, arrived_ref, cols, sems, groups):
    pltpu.make_async_copy(arrived_ref.at[0, :, cols], arrived_ref.at[0, :, cols], sems.at[0]).wait()
    if groups > 1:
        others = arrived_ref.at[pl.ds(0, groups - 1), :, cols]
        pltpu.make_async_copy(others, others, sems.at[1]).wait()
        pltpu.make_async_copy(others, others, sems.at[2]).wait()


def settle(arrived_ref, halves_ref, settled_ref, sems, groups, span, rows):
    g, p = lax.axis_index("dp"), lax.axis_index("pair")
    count, cols = arrived_ref.shape[1:]

    def add(k, summed):
        return summed + arrived_ref[k].astype(F32)

    summed = lax.fori_loop(0, groups, add, jnp.zeros((count, cols), F32))
    interleave(summed[:, : cols // 2], summed[:, cols // 2 :], rows, halves_ref)
    own = pltpu.make_async_copy(halves_ref.at[p % 2, p // 2], settled_ref.at[p], sems.at[0])
    own.start()

    def push(k, carry):
        to_p = partner(k, groups, span)[1]
        pltpu.make_async_remote_copy(
            src_ref=halves_ref.at[to_p % 2, to_p // 2],
            dst_ref=settled_ref.at[p],
            send_sem=sems.at[1],
            recv_sem=sems.at[2],
            device_id=(g, to_p),
            device_id_type=MESH,
        ).start()
        return carry

    lax.fori_loop(1, span, push, 0)

    def wait():
        own.wait()
        drain(settled_ref, span - 1, sems.at[1])
        drain(settled_ref, span - 1, sems.at[2])

    return wait


def exchange_gradients(rows_ref, grads_ref, back_ref, parts_ref, got, part, sems, between, *, groups, span, bound):
    total = groups * span
    g, p = lax.axis_index("dp"), lax.axis_index("pair")
    me, core = g * span + p, p % 2
    chip, chips = me // 2, total // 2
    swap = pltpu.make_async_remote_copy(
        src_ref=grads_ref.at[1 - core],
        dst_ref=got,
        send_sem=sems.at[1],
        recv_sem=sems.at[2],
        device_id=(g, p + 1 - 2 * core),
        device_id_type=MESH,
    )
    swap.start()
    own = keep(rows_ref, back_ref, sems.at[0], span)
    landed = push_all(rows_ref, back_ref, sems.at[3], sems.at[4], groups, span, bound)
    settled = between()
    swap.wait()

    def add(m, carry):
        part[m] = (grads_ref[core, m] + got[m]).astype(BF16)
        return carry

    lax.fori_loop(0, chips, add, 0)
    mine = pltpu.make_async_copy(part.at[chip], parts_ref.at[chip], sems.at[5])
    mine.start()

    def push_part(k, carry):
        to_g, to_p = partner(2 * k, groups, span)
        pltpu.make_async_remote_copy(
            src_ref=part.at[(to_g * span + to_p) // 2],
            dst_ref=parts_ref.at[chip],
            send_sem=sems.at[6],
            recv_sem=sems.at[7],
            device_id=(to_g, to_p),
            device_id_type=MESH,
        ).start()
        return carry

    lax.fori_loop(1, chips, push_part, 0)
    own.wait()
    mine.wait()
    settled()
    landed()
    drain(parts_ref, chips - 1, sems.at[6])
    drain(parts_ref, chips - 1, sems.at[7])


def update(
    slots_ref, back_ref, table_ref, accum_ref, parts_ref, settled_ref, tnew_ref, anew_ref, gin_ref, gout_ref, *, width,
    factor
):
    shards = slots_ref.shape[0] * slots_ref.shape[1]
    rows_dev, model = table_ref.shape
    count = shards * width
    spread = ((iota((shards, count), 1) // width) == iota((shards, count), 0)).astype(F32).astype(BF16)
    high, low = slot_halves(slots_ref[...].reshape(shards, 128))
    turn = lambda a: lax.dot_general(a, spread, (((0,), (0,)), ((), ())), preferred_element_type=F32)
    value = 2.0 * turn(high) + turn(low)
    mine = iota((128, count), 0) == (iota((128, count), 1) % width)
    slot = jnp.sum(jnp.where(mine, value, 0.0), axis=0, keepdims=True).astype(I32)
    pick = jnp.where(iota((rows_dev, count), 0) == slot, 1.0, 0.0).astype(BF16)
    total = dot(pick, back_ref[...].reshape(count, model))
    square = jnp.mean(total * total, axis=1, keepdims=True)
    eye = iota((rows_dev, rows_dev), 0) == iota((rows_dev, rows_dev), 1)
    accum = jnp.sum(jnp.where(eye, accum_ref[...], 0.0), axis=1, keepdims=True) + square
    anew_ref[...] = jnp.sum(jnp.where(eye, accum, 0.0), axis=0, keepdims=True)
    tnew_ref[...] = table_ref[...] - LEARN_RATE * total / jnp.sqrt(accum)

    def total_of(ref):
        def add(m, summed):
            return summed + ref[m].astype(F32)

        summed = lax.fori_loop(0, ref.shape[0], add, jnp.zeros(ref.shape[1:], F32)) * factor
        return summed[:rows], summed[rows:]

    rows = gin_ref.shape[0]
    half = model // 2
    gin_ref[:, model : 2 * model], gin_ref[:, 3 * model :] = total_of(parts_ref)
    upper, lower = total_of(settled_ref)
    gin_ref[:, :model] = upper[:, :model]
    gin_ref[:, 2 * model : 3 * model] = lower[:, half:]
    gout_ref[:, :half] = upper[:, model:]
    gout_ref[:, half:] = lower[:, :half]


def layer_kernel(
    row_ref, seg_ref, pair_ref, w_in_ref, w_out_ref, og_ref, table_ref, accum_ref, out_ref, tnew_ref, anew_ref, gin_ref,
    gout_ref, request, middle, slots, target_r, target_c, meta, found, fetched, x, z, u, q, kv, dhu, wgrad, dq, dk, dv, kv_all,
    q_all, da_all, da, parts, acc, mask, turned, dxn, early, arrived, halves, settled, grads, sending, back, got, part, landed, local, send, recv, front, sems,
    first_sems, second_sems, settle_sems, *,
    groups, span, width, rows, factor
):
    tokens, rows_dev = row_ref.shape[1], table_ref.shape[0]
    bound = 2 * tokens // (groups * span)
    fetched[...] = jnp.zeros_like(fetched)
    back[...] = jnp.zeros_like(back)
    ready = greet(groups, span)
    route(row_ref, seg_ref, pair_ref, request, target_r, target_c, meta, rows_dev=rows_dev, width=width)
    ready()
    ask(request, middle, slots, front, groups, span)
    find(slots, table_ref, found, width=width)
    own = keep(found, fetched, front.at[6], span)
    answered = push_all(found, fetched, front.at[7], front.at[8], groups, span, bound)
    own.wait()
    answered()
    group = project(fetched, target_c, w_in_ref, x, z, u, q, kv, turned)
    dxn[...] = jnp.zeros_like(dxn)
    model = x.shape[1]
    stages = ((slice(0, 2 * model), first_sems), (slice(2 * model, 3 * model), second_sems))

    def weight(g, grad):
        return weigh(g, grad[...], z, turned, w_in_ref, dxn)

    def begin(stage):
        if stage == 0:
            early[:, :model] = weight(0, dhu).astype(BF16)
            early[:, model : 2 * model] = wgrad[...].astype(BF16)
        else:
            early[:, 2 * model :] = weight(2, dq).astype(BF16)
        push_early(early, arrived, *stages[stage], groups, span)

    def between():
        for stage in stages:
            wait_early(early, arrived, *stage, groups)
        return settle(arrived, halves, settled, settle_sems, groups, span, rows)

    attend(
        meta, q, kv, u, x, w_out_ref, og_ref, out_ref, dhu, wgrad, dq, dk, dv, kv_all, q_all, da_all, da, parts, acc,
        mask, local, send, recv, group, begin, span=span
    )
    interleave(weight(1, dv), weight(3, dk), rows, grads)
    finish(dxn, x, og_ref, target_r, sending)
    exchange_gradients(
        sending, grads, back, landed, got, part, sems, between, groups=groups, span=span, bound=bound
    )
    update(
        slots, back, table_ref, accum_ref, landed, settled, tnew_ref, anew_ref, gin_ref, gout_ref, width=width, factor=factor
    )


def shape(dims, dtype):
    return jax.ShapeDtypeStruct(dims, dtype)


def body(table, accum, item_row, segments, pairs, w_in, w_out, out_grad):
    tokens = item_row.shape[0]
    rows_dev, model = table.shape
    shards = lax.axis_size(("dp", "pair"))
    span = lax.axis_size("pair")
    width = -(-(2 * tokens // shards) // 8) * 8
    rows = model // shards
    chunk = (2 * rows, model)
    groups = shards // span
    settling = (2 * rows, 3 * model // 2)
    half_grads = (shards // 2,) + chunk
    block = lambda cols: VMEM((span, tokens, cols), BF16)
    low = lambda cols: VMEM((tokens, cols), BF16)
    high = lambda cols: VMEM((tokens, cols), F32)
    layer_out, table_new, accum_new, grad_in, grad_out = pl.pallas_call(
        functools.partial(
            layer_kernel,
            groups=shards // span,
            span=span,
            width=width,
            rows=rows,
            factor=1.0 / math.sqrt(tokens * shards),
        ),
        out_shape=(
            shape((tokens, model), BF16),
            shape((rows_dev, model), F32),
            shape((1, rows_dev), F32),
            shape((rows, 4 * model), F32),
            shape((rows, model), F32),
        ),
        in_specs=[whole()] * 8,
        out_specs=[whole()] * 5,
        scratch_shapes=[
            VMEM((shards // span, span, 1, 128), I32),
            VMEM((span, shards // span, 1, 128), I32),
            VMEM((shards // span, span, 1, 128), I32),
            VMEM((1, tokens), I32),
            VMEM((tokens, 1), I32),
            VMEM((8, 128), F32),
            VMEM((shards, width, model), BF16),
            VMEM((shards, width, model), BF16),
            low(model),
            high(4 * model),
            low(model),
            low(model),
            low(2 * model),
            high(model),
            VMEM((model, model), F32),
            high(model),
            high(model),
            high(model),
            block(2 * model),
            block(model),
            block(model),
            low(model),
            VMEM((8, tokens, model), BF16),
            high(model),
            high(tokens),
            VMEM((model, tokens), BF16),
            high(model),
            VMEM((model, 3 * model), BF16),
            VMEM((groups, model // groups, 3 * model), BF16),
            VMEM((2, span // 2) + settling, F32),
            VMEM((span,) + settling, F32),
            VMEM((2,) + half_grads, F32),
            VMEM((shards, width, model), BF16),
            VMEM((shards, width, model), BF16),
            VMEM(half_grads, F32),
            VMEM(half_grads, BF16),
            VMEM(half_grads, BF16),
            pltpu.SemaphoreType.DMA((3,)),
            pltpu.SemaphoreType.DMA((3, 15)),
            pltpu.SemaphoreType.DMA((3, 15)),
            pltpu.SemaphoreType.DMA((9,)),
            pltpu.SemaphoreType.DMA((8,)),
            pltpu.SemaphoreType.DMA((3,)),
            pltpu.SemaphoreType.DMA((3,)),
            pltpu.SemaphoreType.DMA((3,)),
        ],
        compiler_params=params(collective_id=0, has_side_effects=True),
    )(item_row.reshape(1, tokens), segments, pairs[0].T, w_in, w_out, out_grad, table, accum.reshape(1, rows_dev))
    return layer_out, table_new, accum_new.reshape(rows_dev), grad_in, grad_out


def solution(mesh):
    both = ("dp", "pair")
    return jax.shard_map(
        body,
        mesh=mesh,
        in_specs=(
            P(both, None),
            P(both),
            P(both),
            P("dp", None),
            P("dp", None, None),
            P(),
            P(),
            P(both, None),
        ),
        out_specs=(P(both, None), P(both, None), P(both), P(both, None), P(both, None)),
        check_vma=False,
    )
```

```python
import functools
import math

import jax
import jax.numpy as jnp
from jax import lax
from jax.experimental import pallas as pl
from jax.experimental.pallas import tpu as pltpu
from jax.sharding import PartitionSpec as P

HEADS = 8
NORM_EPS = 1e-05
LEARN_RATE = 0.5
F32, BF16, I32 = jnp.float32, jnp.bfloat16, jnp.int32
VMEM = pltpu.VMEM
MESH = pl.DeviceIdType.MESH
BIG = 62 * 1024 * 1024


def whole():
    return pl.BlockSpec(memory_space=pltpu.VMEM)


def params(**kw):
    return pltpu.CompilerParams(vmem_limit_bytes=BIG, **kw)


def dot(a, b):
    return lax.dot_general(a, b, (((1,), (0,)), ((), ())), preferred_element_type=F32)


def dot_t(a, b):
    return lax.dot_general(a, b, (((1,), (1,)), ((), ())), preferred_element_type=F32)


def iota(shape, axis):
    return lax.broadcasted_iota(I32, shape, axis)


def normalize(values):
    row_mean = jnp.mean(values, axis=-1, keepdims=True)
    centred = values - row_mean
    spread = jnp.sqrt(jnp.mean(centred * centred, axis=-1, keepdims=True) + NORM_EPS)
    return centred / spread, spread


def norm_back(grad_rows, normed, spread):
    first = jnp.mean(grad_rows, axis=-1, keepdims=True)
    second = jnp.mean(grad_rows * normed, axis=-1, keepdims=True)
    return (grad_rows - first - normed * second) / spread


def even_half(rows):
    lane = iota(rows.shape, 1) & 127
    return jnp.where(lane < 64, rows, jnp.zeros_like(rows))


def odd_half(rows):
    lane = iota(rows.shape, 1) & 127
    return jnp.where(lane < 64, jnp.zeros_like(rows), rows)


def route(row_ref, seg_ref, pair_ref, req_ref, tr_ref, tc_ref, meta_ref, *, rows_dev, width):
    tokens = row_ref.shape[0]
    shards = req_ref.shape[0] * req_ref.shape[1]
    shift = rows_dev.bit_length() - 1
    sub, lane = iota((tokens, tokens), 0), iota((tokens, tokens), 1)
    row = row_ref[...].reshape(1, tokens)
    owner_r = row >> shift
    slot_r = (row & (rows_dev - 1)).astype(F32)
    owner_c = jnp.sum(jnp.where(sub == lane, owner_r.astype(F32), 0.0), axis=1, keepdims=True).astype(I32)
    same = owner_c == owner_r
    rank_c = jnp.sum(jnp.where(same & (lane < sub), 1.0, 0.0), axis=1, keepdims=True).astype(I32)
    rank_r = jnp.sum(jnp.where(same & (sub < lane), 1.0, 0.0), axis=0, keepdims=True).astype(I32)
    tr_ref[...] = owner_r * width + rank_r
    tc_ref[...] = owner_c * width + rank_c
    dest = iota((shards, tokens), 0) == owner_r
    place = iota((shards, 128), 1)
    req = jnp.zeros((shards, 128), F32)
    for k in range(2 * tokens // shards):
        picked = jnp.sum(jnp.where(dest & (rank_r == k), slot_r, 0.0), axis=1, keepdims=True)
        req = jnp.where(place == k, picked, req)
    req_ref[...] = req.astype(I32).reshape(req_ref.shape)
    own = lax.axis_index("pair")
    first, second = pair_ref[0:1, :], pair_ref[1:2, :]
    span = iota((8, first.shape[1]), 0)
    as_query = jnp.max(jnp.where((first == own) & (second == span), 1.0, 0.0), axis=1, keepdims=True)
    as_key = jnp.max(jnp.where((second == own) & (first == span), 1.0, 0.0), axis=1, keepdims=True)
    zeros = jnp.sum(jnp.where(seg_ref[...] == 0, 1.0, 0.0), axis=1, keepdims=True)
    at = iota((8, 128), 1)
    meta_ref[...] = jnp.where(at == 0, as_query, jnp.where(at == 1, as_key, jnp.where(at == 2, zeros, 0.0)))


def slot_halves(slots):
    high = (slots >> 1).astype(F32).astype(BF16)
    low = (slots & 1).astype(F32).astype(BF16)
    return high, low


def find(slots_ref, table_ref, found_ref, *, width):
    shards = slots_ref.shape[0] * slots_ref.shape[1]
    rows_dev = table_ref.shape[0]
    count = shards * width
    spread = ((iota((count, shards), 0) // width) == iota((count, shards), 1)).astype(F32).astype(BF16)
    high, low = slot_halves(slots_ref[...].reshape(shards, 128))
    value = 2.0 * dot(spread, high) + dot(spread, low)
    mine = iota((count, 128), 1) == (iota((count, 128), 0) % width)
    slot = jnp.sum(jnp.where(mine, value, 0.0), axis=1, keepdims=True).astype(I32)
    pick = jnp.where(iota((count, rows_dev), 1) == slot, 1.0, 0.0).astype(BF16)
    found_ref[...] = dot(pick, table_ref[...].astype(BF16)).astype(BF16).reshape(found_ref.shape)


def project(fetched_ref, tc_ref, w_ref, x_ref, z_ref, u_ref, q_ref, kv_ref, turned_ref):
    width = fetched_ref.shape[2]
    count = fetched_ref.shape[0] * fetched_ref.shape[1]
    tokens = tc_ref.shape[0]
    pick = jnp.where(iota((tokens, count), 1) == tc_ref[...], 1.0, 0.0).astype(BF16)
    rows = dot(pick, fetched_ref[...].reshape(count, width))
    x_ref[...] = rows.astype(BF16)
    normed, _ = normalize(rows)
    low = normed.astype(BF16)
    turned_ref[...] = jnp.transpose(normed).astype(BF16)
    outs = (u_ref.at[...], kv_ref.at[:, width:], q_ref.at[...], kv_ref.at[:, :width])

    def group(g):
        z = dot(low, w_ref[:, g * width : (g + 1) * width])
        z_ref[:, g * width : (g + 1) * width] = z
        half = 0.5 * z
        outs[g][...] = (half + half * jnp.tanh(half)).astype(BF16)

    return group


def visible(q_axis, size, q_block, k_block, zeros):
    q_pos = iota((size, size), q_axis) + q_block * size
    k_pos = iota((size, size), 1 - q_axis) + k_block * size
    least = jnp.where(q_pos >= zeros, zeros, 0)
    return jnp.where((k_pos >= least) & (k_pos <= q_pos), 1.0, 0.0)


class Ring:
    RISING = (0, 1, 2, 3, 4, 5, 7), (0, 1, 2, 4, 5, 6, 8, 9), (0, 1, 4, 5, 6, 8, 9, 12, 13), (4, 5, 7, 8, 9, 10, 11, 12, 13)
    FALLING = (0, 1, 2, 3, 4, 5), (0, 1, 4, 5, 6, 8, 9), (0, 1, 4, 5, 6, 14, 8, 9, 12, 13), (4, 5, 7, 8, 9, 10, 11, 12, 13)

    def __init__(self, source, gathered, send, recv, local, span, falling):
        self.source, self.gathered, self.send, self.recv, self.local = source, gathered, send, recv, local
        chips = span // 2
        self.g, self.p = lax.axis_index("dp"), lax.axis_index("pair")
        core, chip = self.p % 2, self.p // 2
        at = lambda step: ((chip + step) % chips) * 2 + core
        self.up, self.down, self.far = at(chips - 1 if falling else 1), at(1 if falling else chips - 1), at(2)
        self.rank = chips - 1 - chip if falling else chip
        self.falling, self.sends = falling, self.FALLING if falling else self.RISING
        self.other = chip * 2 + 1 - core

    def copy(self, i):
        p, up, down, far, other = self.p, self.up, self.down, self.far, self.other
        owner, part, to = (
            (p, 0, up),
            (p, 1, up),
            (p, 1, down),
            (p, 0, down),
            (p, 0, other),
            (p, 1, other),
            (down, 0, up),
            (up, 1, down),
            (down, 0, other),
            (down, 1, other),
            (up, 1, other),
            (up, 0, other),
            (far, 0, other),
            (far, 1, other),
            (down, 1, up),
        )[i]
        half = self.source.shape[0] // 2
        rows = pl.ds(part * half, half)
        return pltpu.make_async_remote_copy(
            src_ref=self.source.at[rows] if i < 6 else self.gathered.at[owner, rows],
            dst_ref=self.gathered.at[owner, rows],
            send_sem=self.send.at[i],
            recv_sem=self.recv.at[i],
            device_id=(self.g, to),
            device_id_type=MESH,
        )

    def own(self):
        return pltpu.make_async_copy(self.source, self.gathered.at[self.p], self.local)

    def when(self, *ranks):
        def decorate(steps):
            for rank in ranks:
                pl.when(self.rank == rank)(functools.partial(steps, rank))

        return decorate

    def start(self):
        self.own().start()

        @self.when(0, 1, 2, 3)
        def _(rank):
            for i in (0, 2, 1, 3, 4, 5):
                if i in self.sends[rank]:
                    self.copy(i).start()

    def arrive(self, *which):
        for i in which:
            self.copy(i).wait_recv()

    def after(self, arrived, *sent):
        self.arrive(arrived)
        for i in sent:
            self.copy(i).start()

    def relay_near(self):
        @self.when(0, 1, 2, 3)
        def _(rank):
            if rank == 0:
                if not self.falling:
                    self.after(2, 7)
            elif rank == 3:
                self.after(0, 8)
                self.after(1, 9)
            else:
                self.after(0, 6, 8)
                self.after(1, *((14, 9) if self.falling and rank == 2 else (9,)))

    def relay_wrap(self):
        @self.when(3)
        def _(rank):
            self.after(2, 7, 10)
            self.after(3, 11)

    def relay_far(self):
        @self.when(2, 3)
        def _(rank):
            self.after(6, 12)
            self.after(14 if self.falling and rank == 3 else 7, 13)

    def handed_own(self):
        self.arrive(4, 5)

    def handed_near(self):
        @self.when(1, 2, 3)
        def _(rank):
            self.arrive(8, 9)

    def handed_wrap(self):
        @self.when(3)
        def _(rank):
            self.arrive(10, 11)

    def handed_far(self):
        @self.when(2, 3)
        def _(rank):
            self.arrive(12, 13)

    def sent(self):
        @self.when(0, 1, 2, 3)
        def _(rank):
            for i in self.sends[rank]:
                self.copy(i).wait_send()


def attend(
    meta_ref, q_ref, kv_ref, u_ref, x_ref, w_ref, og_ref, out_ref, dhu_ref, gout_ref, dq_ref, dk_ref, dv_ref, kv_all,
    q_all, da_all, da, parts, acc, mask, local, send, recv, group, early, *, span
):
    own = lax.axis_index("pair")
    chips, core, chip = span // 2, own % 2, own // 2
    size, width = q_ref.shape
    kv_ring, q_ring, da_ring = (
        Ring(source, gathered, send.at[i], recv.at[i], local.at[i], span, falling)
        for i, (source, gathered, falling) in enumerate(
            ((kv_ref, kv_all, False), (q_ref, q_all, True), (da, da_all, True))
        )
    )
    for g in (3, 1, 2):
        group(g)
    kv_ring.start()
    q_ring.start()
    group(0)
    dhu_ref[...] = dot_t(og_ref[...], w_ref[...])

    def on_step(step, *actions):
        for k, action in enumerate(actions):
            if action:
                pl.when(step == k)(action)

    def block_at(step, falling):
        turn = step // 2
        shift = turn if falling else (3 * turn - (turn * (turn - 1)) // 2) % 4
        return ((chip + shift) % chips) * 2 + (core + step % 2) % 2

    def split(value, at):
        parts[at] = even_half(value)
        parts[at + 1] = odd_half(value)

    def slabs(work):
        def one(s, carry):
            first = pl.multiple_of(s * 128, 128)
            work(pl.ds(first, 128), pl.ds(pl.multiple_of(width + s * 128, 128), 128))
            return carry

        lax.fori_loop(0, width // 128, one, 0)

    def both(rows):
        return jnp.concatenate([even_half(rows), odd_half(rows)], axis=0)

    zeros = meta_ref[0:1, 2:3].astype(I32)
    split(q_ref[...] * 0.0625, 0)
    split(kv_ref[:, :width] * 0.0625, 4)
    split(kv_ref[:, width:] * 0.0625, 6)
    acc[...] = jnp.zeros_like(acc)
    dq_ref[...] = jnp.zeros_like(dq_ref)
    dk_ref[...] = jnp.zeros_like(dk_ref)
    dv_ref[...] = jnp.zeros_like(dv_ref)

    def forward(step, carry):
        j = block_at(step, False)

        def near():
            kv_ring.relay_wrap()
            kv_ring.relay_near()
            q_ring.relay_near()
            q_ring.relay_wrap()

        def far():
            kv_ring.relay_far()
            q_ring.relay_far()

        on_step(
            step, kv_ring.own().wait, kv_ring.handed_own, near, kv_ring.handed_near, None, kv_ring.handed_wrap, far,
            kv_ring.handed_far
        )

        @pl.when(j <= own)
        def _():
            mask[...] = visible(0, size, own, j, zeros) * meta_ref[pl.ds(j, 1), 0:1]

            def work(cols, late):
                keys = kv_all[j, :, cols]
                weights = []
                for half in range(2):
                    h = dot_t(parts[half, :, cols], keys)
                    weights.append((h * ((1.0 + jnp.tanh(h)) * mask[...])).astype(BF16))
                acc[:, cols] += dot(jnp.concatenate(weights, axis=1), both(kv_all[j, :, late]))

            slabs(work)

        return carry

    lax.fori_loop(0, span, forward, 0)

    normed, spread = normalize(acc[...])
    gate = u_ref[...].astype(F32)
    gated = (normed * gate).astype(BF16)
    dy = dhu_ref[...]
    da[...] = norm_back(dy * gate, normed, spread).astype(BF16)
    da_ring.start()
    split(da[...] * 0.0625, 2)
    dhu_ref[...] = dy * normed
    out_ref[...] = (dot(gated, w_ref[...]) + x_ref[...].astype(F32)).astype(BF16)
    gout_ref[...] = lax.dot_general(gated, og_ref[...], (((0,), (0,)), ((), ())), preferred_element_type=F32)
    early(0)

    def by_query(step, carry):
        j = block_at(step, False)

        @pl.when(j <= own)
        def _():
            mask[...] = visible(0, size, own, j, zeros) * meta_ref[pl.ds(j, 1), 0:1]

            def work(cols, late):
                keys = kv_all[j, :, cols]
                values = kv_all[j, :, late]
                grads = []
                for half in range(2):
                    h = dot_t(parts[half, :, cols], keys)
                    u = 1.0 + jnp.tanh(h)
                    seen = u * mask[...]
                    slope = seen + h * seen * (2.0 - u)
                    grads.append((dot_t(parts[2 + half, :, cols], values) * slope).astype(BF16))
                dq_ref[:, cols] += dot(jnp.concatenate(grads, axis=1), both(keys))

            slabs(work)

        return carry

    lax.fori_loop(0, span, by_query, 0)
    early(1)

    def by_key(step, carry):
        i = block_at(step, True)

        def mine():
            q_ring.own().wait()
            da_ring.own().wait()

        def pair(name):
            def action():
                getattr(q_ring, name)()
                getattr(da_ring, name)()

            return action

        on_step(
            step, mine, pair("handed_own"), da_ring.relay_near, pair("handed_near"), da_ring.relay_far, pair("handed_far"),
            da_ring.relay_wrap, pair("handed_wrap")
        )

        @pl.when(i >= own)
        def _():
            mask[...] = visible(1, size, i, own, zeros) * meta_ref[pl.ds(i, 1), 1:2]

            def work(cols, late):
                queries = q_all[i, :, cols]
                dafter = da_all[i, :, cols]
                grads, weights = [], []
                for half in range(2):
                    h = dot_t(parts[4 + half, :, cols], queries)
                    u = 1.0 + jnp.tanh(h)
                    seen = u * mask[...]
                    weight = h * seen
                    weights.append(weight.astype(BF16))
                    slope = seen + weight * (2.0 - u)
                    grads.append((dot_t(parts[6 + half, :, cols], dafter) * slope).astype(BF16))
                dk_ref[:, cols] += dot(jnp.concatenate(grads, axis=1), both(queries))
                dv_ref[:, cols] += dot(jnp.concatenate(weights, axis=1), both(dafter))

            slabs(work)

        return carry

    lax.fori_loop(0, span, by_key, 0)
    for ring in (kv_ring, q_ring, da_ring):
        ring.sent()


def interleave(upper, lower, rows, out_ref):
    count, cols = upper.shape
    top = (iota((count, cols), 0) % (2 * rows)) < rows
    first = jnp.where(top, upper, pltpu.roll(lower, rows, 0))
    second = jnp.where(top, pltpu.roll(upper, count - rows, 0), lower)
    out_ref[0] = first.reshape(out_ref.shape[1:])
    out_ref[1] = second.reshape(out_ref.shape[1:])


def weigh(g, grad, z_ref, turned_ref, w_ref, dxn_ref):
    width = grad.shape[1]
    cols = slice(g * width, (g + 1) * width)
    h = 0.5 * z_ref[:, cols]
    t = jnp.tanh(h)
    slope = 0.5 * (1.0 + t) * (1.0 + h * (1.0 - t))
    dz = (grad * slope).astype(BF16)
    dxn_ref[...] += dot_t(dz, w_ref[:, cols])
    return dot(turned_ref[...], dz)


def finish(dxn_ref, x_ref, og_ref, tr_ref, send_ref):
    size = x_ref.shape[0]
    normed, spread = normalize(x_ref[...].astype(F32))
    dx = norm_back(dxn_ref[...], normed, spread) + og_ref[...].astype(F32)
    count = send_ref.shape[0] * send_ref.shape[1]
    pick = jnp.where(iota((count, size), 0) == tr_ref[...], 1.0, 0.0).astype(BF16)
    send_ref[...] = dot(pick, dx.astype(BF16)).astype(BF16).reshape(send_ref.shape)


def partner(k, groups, span):
    g, p = lax.axis_index("dp"), lax.axis_index("pair")
    chips, side = span // 2, math.isqrt(groups)
    to_p = ((p // 2 + (k // 2) % chips) % chips) * 2 + (p % 2 + k % 2) % 2
    shift = k // span
    to_g = ((g // side + shift // side) % side) * side + (g % side + shift % side) % side
    return to_g, to_p


def greet(groups, span):
    g, p = lax.axis_index("dp"), lax.axis_index("pair")
    barrier = pltpu.get_barrier_semaphore()

    def hello(device):
        pl.semaphore_signal(barrier, inc=1, device_id=device, device_id_type=MESH)

    def hello_pair(k, carry):
        hello((g, partner(k, groups, span)[1]))
        return carry

    def hello_group(k, carry):
        hello((partner(k * span, groups, span)[0], p))
        return carry

    lax.fori_loop(1, span, hello_pair, 0)
    lax.fori_loop(1, groups, hello_group, 0)
    return lambda: pl.semaphore_wait(barrier, span + groups - 2)


def ask(request, middle, slots, sems, groups, span):
    g, p = lax.axis_index("dp"), lax.axis_index("pair")
    own = pltpu.make_async_copy(request.at[:, p], middle.at[p], sems.at[0])
    own.start()

    def over_pair(k, carry):
        to_p = partner(k, groups, span)[1]
        pltpu.make_async_remote_copy(
            src_ref=request.at[:, to_p],
            dst_ref=middle.at[p],
            send_sem=sems.at[1],
            recv_sem=sems.at[2],
            device_id=(g, to_p),
            device_id_type=MESH,
        ).start()
        return carry

    lax.fori_loop(1, span, over_pair, 0)
    own.wait()
    drain(middle, span - 1, sems.at[1])
    drain(middle, span - 1, sems.at[2])
    own = pltpu.make_async_copy(middle.at[:, g], slots.at[g], sems.at[3])
    own.start()

    def over_groups(k, carry):
        to_g = partner(k * span, groups, span)[0]
        pltpu.make_async_remote_copy(
            src_ref=middle.at[:, to_g],
            dst_ref=slots.at[g],
            send_sem=sems.at[4],
            recv_sem=sems.at[5],
            device_id=(to_g, p),
            device_id_type=MESH,
        ).start()
        return carry

    lax.fori_loop(1, groups, over_groups, 0)
    own.wait()
    if groups > 1:
        drain(slots, groups - 1, sems.at[4])
        drain(slots, groups - 1, sems.at[5])


def drain(ref, count, sem):
    part = ref.at[pl.ds(0, count)]
    pltpu.make_async_copy(part, part, sem).wait()


def push_all(source, target, send, recv, groups, span, rows):
    me = lax.axis_index("dp") * span + lax.axis_index("pair")
    used = pl.ds(0, rows)

    def push(k, carry):
        to_g, to_p = partner(k, groups, span)
        pltpu.make_async_remote_copy(
            src_ref=source.at[to_g * span + to_p, used],
            dst_ref=target.at[me, used],
            send_sem=send,
            recv_sem=recv,
            device_id=(to_g, to_p),
            device_id_type=MESH,
        ).start()
        return carry

    lax.fori_loop(1, groups * span, push, 0)

    def wait():
        all_of = target.at[pl.ds(0, groups * span - 1), used]
        pltpu.make_async_copy(all_of, all_of, send).wait()
        pltpu.make_async_copy(all_of, all_of, recv).wait()

    return wait


def keep(source, target, sem, span):
    me = lax.axis_index("dp") * span + lax.axis_index("pair")
    copy = pltpu.make_async_copy(source.at[me], target.at[me], sem)
    copy.start()
    return copy


def push_early(early_ref, arrived_ref, cols, sems, groups, span):
    g, p = lax.axis_index("dp"), lax.axis_index("pair")
    count = early_ref.shape[0] // groups

    def mine(to_g):
        return early_ref.at[pl.ds(pl.multiple_of(to_g * count, count), count), cols]

    own = pltpu.make_async_copy(mine(g), arrived_ref.at[g, :, cols], sems.at[0])
    own.start()

    def push(k, carry):
        to_g = partner(k * span, groups, span)[0]
        pltpu.make_async_remote_copy(
            src_ref=mine(to_g),
            dst_ref=arrived_ref.at[g, :, cols],
            send_sem=sems.at[1],
            recv_sem=sems.at[2],
            device_id=(to_g, p),
            device_id_type=MESH,
        ).start()
        return carry

    lax.fori_loop(1, groups, push, 0)


def wait_early(early_ref, arrived_ref, cols, sems, groups):
    pltpu.make_async_copy(arrived_ref.at[0, :, cols], arrived_ref.at[0, :, cols], sems.at[0]).wait()
    if groups > 1:
        others = arrived_ref.at[pl.ds(0, groups - 1), :, cols]
        pltpu.make_async_copy(others, others, sems.at[1]).wait()
        pltpu.make_async_copy(others, others, sems.at[2]).wait()


def settle(arrived_ref, halves_ref, settled_ref, sems, groups, span, rows):
    g, p = lax.axis_index("dp"), lax.axis_index("pair")
    count, cols = arrived_ref.shape[1:]

    def add(k, summed):
        return summed + arrived_ref[k].astype(F32)

    summed = lax.fori_loop(0, groups, add, jnp.zeros((count, cols), F32))
    interleave(summed[:, : cols // 2], summed[:, cols // 2 :], rows, halves_ref)
    own = pltpu.make_async_copy(halves_ref.at[p % 2, p // 2], settled_ref.at[p], sems.at[0])
    own.start()

    def push(k, carry):
        to_p = partner(k, groups, span)[1]
        pltpu.make_async_remote_copy(
            src_ref=halves_ref.at[to_p % 2, to_p // 2],
            dst_ref=settled_ref.at[p],
            send_sem=sems.at[1],
            recv_sem=sems.at[2],
            device_id=(g, to_p),
            device_id_type=MESH,
        ).start()
        return carry

    lax.fori_loop(1, span, push, 0)

    def wait():
        own.wait()
        drain(settled_ref, span - 1, sems.at[1])
        drain(settled_ref, span - 1, sems.at[2])

    return wait


def swap_halves(grads_ref, got, sems):
    g, p = lax.axis_index("dp"), lax.axis_index("pair")
    core = p % 2
    swap = pltpu.make_async_remote_copy(
        src_ref=grads_ref.at[1 - core],
        dst_ref=got,
        send_sem=sems.at[1],
        recv_sem=sems.at[2],
        device_id=(g, p + 1 - 2 * core),
        device_id_type=MESH,
    )
    swap.start()
    return swap


def exchange_gradients(
    rows_ref, grads_ref, back_ref, parts_ref, got, part, sems, swap, between, *, groups, span, bound
):
    total = groups * span
    g, p = lax.axis_index("dp"), lax.axis_index("pair")
    me, core = g * span + p, p % 2
    chip, chips = me // 2, total // 2
    own = keep(rows_ref, back_ref, sems.at[0], span)
    landed = push_all(rows_ref, back_ref, sems.at[3], sems.at[4], groups, span, bound)
    swap.wait()

    def add(m, carry):
        part[m] = (grads_ref[core, m] + got[m]).astype(BF16)
        return carry

    lax.fori_loop(0, chips, add, 0)
    mine = pltpu.make_async_copy(part.at[chip], parts_ref.at[chip], sems.at[5])
    mine.start()

    def push_part(k, carry):
        to_g, to_p = partner(2 * k, groups, span)
        pltpu.make_async_remote_copy(
            src_ref=part.at[(to_g * span + to_p) // 2],
            dst_ref=parts_ref.at[chip],
            send_sem=sems.at[6],
            recv_sem=sems.at[7],
            device_id=(to_g, to_p),
            device_id_type=MESH,
        ).start()
        return carry

    lax.fori_loop(1, chips, push_part, 0)
    settled = between()
    own.wait()
    mine.wait()
    settled()
    landed()
    drain(parts_ref, chips - 1, sems.at[6])
    drain(parts_ref, chips - 1, sems.at[7])


def update_kernel(
    slots_ref, back_ref, table_ref, accum_ref, parts_ref, settled_ref, layer_ref, tnew_ref, anew_ref, gin_ref, gout_ref,
    out_ref, *, width, factor
):
    shards = slots_ref.shape[0] * slots_ref.shape[1]
    rows_dev, model = table_ref.shape
    count = shards * width
    spread = ((iota((shards, count), 1) // width) == iota((shards, count), 0)).astype(F32).astype(BF16)
    high, low = slot_halves(slots_ref[...].reshape(shards, 128))
    turn = lambda a: lax.dot_general(a, spread, (((0,), (0,)), ((), ())), preferred_element_type=F32)
    value = 2.0 * turn(high) + turn(low)
    mine = iota((128, count), 0) == (iota((128, count), 1) % width)
    slot = jnp.sum(jnp.where(mine, value, 0.0), axis=0, keepdims=True).astype(I32)
    pick = jnp.where(iota((rows_dev, count), 0) == slot, 1.0, 0.0).astype(BF16)
    total = dot(pick, back_ref[...].reshape(count, model))
    square = jnp.mean(total * total, axis=1, keepdims=True)
    eye = iota((rows_dev, rows_dev), 0) == iota((rows_dev, rows_dev), 1)
    accum = jnp.sum(jnp.where(eye, accum_ref[...], 0.0), axis=1, keepdims=True) + square
    anew_ref[...] = jnp.sum(jnp.where(eye, accum, 0.0), axis=0, keepdims=True)
    tnew_ref[...] = table_ref[...] - LEARN_RATE * total / jnp.sqrt(accum)

    def total_of(ref):
        def add(m, summed):
            return summed + ref[m].astype(F32)

        summed = lax.fori_loop(0, ref.shape[0], add, jnp.zeros(ref.shape[1:], F32)) * factor
        return summed[:rows], summed[rows:]

    rows = gin_ref.shape[0]
    half = model // 2
    gin_ref[:, model : 2 * model], gin_ref[:, 3 * model :] = total_of(parts_ref)
    upper, lower = total_of(settled_ref)
    gin_ref[:, :model] = upper[:, :model]
    gin_ref[:, 2 * model : 3 * model] = lower[:, half:]
    gout_ref[:, :half] = upper[:, model:]
    gout_ref[:, half:] = lower[:, :half]
    out_ref[...] = layer_ref[...]


def layer_kernel(
    row_ref, seg_ref, pair_ref, w_in_hbm, w_out_hbm, og_hbm, table_hbm, out_ref, slots, back, landed, settled,
    w_in_ref, w_out_ref, og_ref, table_ref, request, middle, target_r, target_c, meta, found, fetched, x, z, u, q, kv, dhu, wgrad, dq, dk, dv, kv_all,
    q_all, da_all, da, parts, acc, mask, turned, dxn, early, arrived, halves, grads, sending, got, part, local, send, recv, front, sems,
    load_sems, first_sems, second_sems, settle_sems, *,
    groups, span, width, rows
):
    tokens, rows_dev = row_ref.shape[0], table_ref.shape[0]
    bound = 2 * tokens // (groups * span)
    loads = [
        pltpu.make_async_copy(source, target, load_sems.at[i])
        for i, (source, target) in enumerate(
            ((table_hbm, table_ref), (w_in_hbm, w_in_ref), (w_out_hbm, w_out_ref), (og_hbm, og_ref))
        )
    ]
    for load in loads:
        load.start()
    fetched[...] = jnp.zeros_like(fetched)
    back[...] = jnp.zeros_like(back)
    ready = greet(groups, span)
    route(row_ref, seg_ref, pair_ref, request, target_r, target_c, meta, rows_dev=rows_dev, width=width)
    ready()
    ask(request, middle, slots, front, groups, span)
    for load in loads:
        load.wait()
    find(slots, table_ref, found, width=width)
    own = keep(found, fetched, front.at[6], span)
    answered = push_all(found, fetched, front.at[7], front.at[8], groups, span, bound)
    own.wait()
    answered()
    group = project(fetched, target_c, w_in_ref, x, z, u, q, kv, turned)
    dxn[...] = jnp.zeros_like(dxn)
    model = x.shape[1]
    stages = ((slice(0, 2 * model), first_sems), (slice(2 * model, 3 * model), second_sems))

    def weight(g, grad):
        return weigh(g, grad[...], z, turned, w_in_ref, dxn)

    def begin(stage):
        if stage == 0:
            early[:, :model] = weight(0, dhu).astype(BF16)
            early[:, model : 2 * model] = wgrad[...].astype(BF16)
        else:
            early[:, 2 * model :] = weight(2, dq).astype(BF16)
        push_early(early, arrived, *stages[stage], groups, span)

    def between():
        for stage in stages:
            wait_early(early, arrived, *stage, groups)
        return settle(arrived, halves, settled, settle_sems, groups, span, rows)

    attend(
        meta, q, kv, u, x, w_out_ref, og_ref, out_ref, dhu, wgrad, dq, dk, dv, kv_all, q_all, da_all, da, parts, acc,
        mask, local, send, recv, group, begin, span=span
    )
    interleave(weight(1, dv), weight(3, dk), rows, grads)
    swap = swap_halves(grads, got, sems)
    finish(dxn, x, og_ref, target_r, sending)
    exchange_gradients(
        sending, grads, back, landed, got, part, sems, swap, between, groups=groups, span=span, bound=bound
    )


def shape(dims, dtype):
    return jax.ShapeDtypeStruct(dims, dtype)


def body(table, accum, item_row, segments, pairs, w_in, w_out, out_grad):
    tokens = item_row.shape[0]
    rows_dev, model = table.shape
    shards = lax.axis_size(("dp", "pair"))
    span = lax.axis_size("pair")
    width = -(-(2 * tokens // shards) // 8) * 8
    rows = model // shards
    chunk = (2 * rows, model)
    groups = shards // span
    settling = (2 * rows, 3 * model // 2)
    half_grads = (shards // 2,) + chunk
    block = lambda cols: VMEM((span, tokens, cols), BF16)
    low = lambda cols: VMEM((tokens, cols), BF16)
    high = lambda cols: VMEM((tokens, cols), F32)
    request = (groups, span, 1, 128)
    parcel = (shards, width, model)
    layer_out, slots, back, landed, settled = pl.pallas_call(
        functools.partial(layer_kernel, groups=groups, span=span, width=width, rows=rows),
        out_shape=(
            shape((tokens, model), BF16),
            shape(request, I32),
            shape(parcel, BF16),
            shape(half_grads, BF16),
            shape((span,) + settling, F32),
        ),
        in_specs=[whole()] * 3 + [pl.BlockSpec(memory_space=pl.ANY)] * 4,
        out_specs=[whole()] * 5,
        scratch_shapes=[
            VMEM(w_in.shape, BF16),
            VMEM(w_out.shape, BF16),
            VMEM(out_grad.shape, BF16),
            VMEM(table.shape, F32),
            VMEM(request, I32),
            VMEM((span, groups, 1, 128), I32),
            VMEM((1, tokens), I32),
            VMEM((tokens, 1), I32),
            VMEM((8, 128), F32),
            VMEM((shards, width, model), BF16),
            VMEM((shards, width, model), BF16),
            low(model),
            high(4 * model),
            low(model),
            low(model),
            low(2 * model),
            high(model),
            VMEM((model, model), F32),
            high(model),
            high(model),
            high(model),
            block(2 * model),
            block(model),
            block(model),
            low(model),
            VMEM((8, tokens, model), BF16),
            high(model),
            high(tokens),
            VMEM((model, tokens), BF16),
            high(model),
            VMEM((model, 3 * model), BF16),
            VMEM((groups, model // groups, 3 * model), BF16),
            VMEM((2, span // 2) + settling, F32),
            VMEM((2,) + half_grads, F32),
            VMEM(parcel, BF16),
            VMEM(half_grads, F32),
            VMEM(half_grads, BF16),
            pltpu.SemaphoreType.DMA((3,)),
            pltpu.SemaphoreType.DMA((3, 15)),
            pltpu.SemaphoreType.DMA((3, 15)),
            pltpu.SemaphoreType.DMA((9,)),
            pltpu.SemaphoreType.DMA((8,)),
            pltpu.SemaphoreType.DMA((4,)),
            pltpu.SemaphoreType.DMA((3,)),
            pltpu.SemaphoreType.DMA((3,)),
            pltpu.SemaphoreType.DMA((3,)),
        ],
        compiler_params=params(collective_id=0, has_side_effects=True),
    )(item_row, segments, pairs[0].T, w_in, w_out, out_grad, table)
    table_new, accum_new, grad_in, grad_out, layer_out = pl.pallas_call(
        functools.partial(update_kernel, width=width, factor=1.0 / math.sqrt(tokens * shards)),
        out_shape=(
            shape((rows_dev, model), F32),
            shape((1, rows_dev), F32),
            shape((rows, 4 * model), F32),
            shape((rows, model), F32),
            shape((tokens, model), BF16),
        ),
        in_specs=[whole()] * 7,
        out_specs=[whole()] * 5,
        compiler_params=params(),
    )(slots, back, table, accum.reshape(1, rows_dev), landed, settled, layer_out)
    return layer_out, table_new, accum_new.reshape(rows_dev), grad_in, grad_out


def solution(mesh):
    both = ("dp", "pair")
    return jax.shard_map(
        body,
        mesh=mesh,
        in_specs=(
            P(both, None),
            P(both),
            P(both),
            P("dp", None),
            P("dp", None, None),
            P(),
            P(),
            P(both, None),
        ),
        out_specs=(P(both, None), P(both, None), P(both), P(both, None), P(both, None)),
        check_vma=False,
    )
```

```python
import functools
import math

import jax
import jax.numpy as jnp
from jax import lax
from jax.experimental import pallas as pl
from jax.experimental.pallas import tpu as pltpu
from jax.sharding import PartitionSpec as P

HEADS = 8
NORM_EPS = 1e-05
LEARN_RATE = 0.5
F32, BF16, I32 = jnp.float32, jnp.bfloat16, jnp.int32
VMEM = pltpu.VMEM
MESH = pl.DeviceIdType.MESH
BIG = 62 * 1024 * 1024


def whole():
    return pl.BlockSpec(memory_space=pltpu.VMEM)


def params(**kw):
    return pltpu.CompilerParams(vmem_limit_bytes=BIG, **kw)


def dot(a, b):
    return lax.dot_general(a, b, (((1,), (0,)), ((), ())), preferred_element_type=F32)


def dot_t(a, b):
    return lax.dot_general(a, b, (((1,), (1,)), ((), ())), preferred_element_type=F32)


def iota(shape, axis):
    return lax.broadcasted_iota(I32, shape, axis)


def normalize(values):
    row_mean = jnp.mean(values, axis=-1, keepdims=True)
    centred = values - row_mean
    spread = jnp.sqrt(jnp.mean(centred * centred, axis=-1, keepdims=True) + NORM_EPS)
    return centred / spread, spread


def norm_back(grad_rows, normed, spread):
    first = jnp.mean(grad_rows, axis=-1, keepdims=True)
    second = jnp.mean(grad_rows * normed, axis=-1, keepdims=True)
    return (grad_rows - first - normed * second) / spread


def even_half(rows):
    lane = iota(rows.shape, 1) & 127
    return jnp.where(lane < 64, rows, jnp.zeros_like(rows))


def odd_half(rows):
    lane = iota(rows.shape, 1) & 127
    return jnp.where(lane < 64, jnp.zeros_like(rows), rows)


def route(row_ref, seg_ref, pair_ref, req_ref, tr_ref, tc_ref, meta_ref, *, rows_dev, width):
    tokens = row_ref.shape[0]
    shards = req_ref.shape[0] * req_ref.shape[1]
    shift = rows_dev.bit_length() - 1
    sub, lane = iota((tokens, tokens), 0), iota((tokens, tokens), 1)
    row = row_ref[...].reshape(1, tokens)
    owner_r = row >> shift
    slot_r = (row & (rows_dev - 1)).astype(F32)
    owner_c = jnp.sum(jnp.where(sub == lane, owner_r.astype(F32), 0.0), axis=1, keepdims=True).astype(I32)
    same = owner_c == owner_r
    rank_c = jnp.sum(jnp.where(same & (lane < sub), 1.0, 0.0), axis=1, keepdims=True).astype(I32)
    rank_r = jnp.sum(jnp.where(same & (sub < lane), 1.0, 0.0), axis=0, keepdims=True).astype(I32)
    tr_ref[...] = owner_r * width + rank_r
    tc_ref[...] = owner_c * width + rank_c
    dest = iota((shards, tokens), 0) == owner_r
    place = iota((shards, 128), 1)
    req = jnp.zeros((shards, 128), F32)
    for k in range(2 * tokens // shards):
        picked = jnp.sum(jnp.where(dest & (rank_r == k), slot_r, 0.0), axis=1, keepdims=True)
        req = jnp.where(place == k, picked, req)
    req_ref[...] = req.astype(I32).reshape(req_ref.shape)
    own = lax.axis_index("pair")
    first, second = pair_ref[0:1, :], pair_ref[1:2, :]
    span = iota((8, first.shape[1]), 0)
    as_query = jnp.max(jnp.where((first == own) & (second == span), 1.0, 0.0), axis=1, keepdims=True)
    as_key = jnp.max(jnp.where((second == own) & (first == span), 1.0, 0.0), axis=1, keepdims=True)
    zeros = jnp.sum(jnp.where(seg_ref[...] == 0, 1.0, 0.0), axis=1, keepdims=True)
    at = iota((8, 128), 1)
    meta_ref[...] = jnp.where(at == 0, as_query, jnp.where(at == 1, as_key, jnp.where(at == 2, zeros, 0.0)))


def slot_halves(slots):
    high = (slots >> 1).astype(F32).astype(BF16)
    low = (slots & 1).astype(F32).astype(BF16)
    return high, low


def find(slots_ref, table_ref, found_ref, *, width):
    shards = slots_ref.shape[0] * slots_ref.shape[1]
    rows_dev = table_ref.shape[0]
    count = shards * width
    spread = ((iota((count, shards), 0) // width) == iota((count, shards), 1)).astype(F32).astype(BF16)
    high, low = slot_halves(slots_ref[...].reshape(shards, 128))
    value = 2.0 * dot(spread, high) + dot(spread, low)
    mine = iota((count, 128), 1) == (iota((count, 128), 0) % width)
    slot = jnp.sum(jnp.where(mine, value, 0.0), axis=1, keepdims=True).astype(I32)
    pick = jnp.where(iota((count, rows_dev), 1) == slot, 1.0, 0.0).astype(BF16)
    found_ref[...] = dot(pick, table_ref[...].astype(BF16)).astype(BF16).reshape(found_ref.shape)


def project(fetched_ref, tc_ref, w_ref, x_ref, z_ref, u_ref, q_ref, kv_ref, turned_ref):
    width = fetched_ref.shape[2]
    count = fetched_ref.shape[0] * fetched_ref.shape[1]
    tokens = tc_ref.shape[0]
    pick = jnp.where(iota((tokens, count), 1) == tc_ref[...], 1.0, 0.0).astype(BF16)
    rows = dot(pick, fetched_ref[...].reshape(count, width))
    x_ref[...] = rows.astype(BF16)
    normed, _ = normalize(rows)
    low = normed.astype(BF16)
    turned_ref[...] = jnp.transpose(normed).astype(BF16)
    outs = (u_ref.at[...], kv_ref.at[:, width:], q_ref.at[...], kv_ref.at[:, :width])

    def group(g):
        z = dot(low, w_ref[:, g * width : (g + 1) * width])
        z_ref[:, g * width : (g + 1) * width] = z
        half = 0.5 * z
        outs[g][...] = (half + half * jnp.tanh(half)).astype(BF16)

    return group


def visible(q_axis, size, q_block, k_block, zeros):
    q_pos = iota((size, size), q_axis) + q_block * size
    k_pos = iota((size, size), 1 - q_axis) + k_block * size
    least = jnp.where(q_pos >= zeros, zeros, 0)
    return jnp.where((k_pos >= least) & (k_pos <= q_pos), 1.0, 0.0)


class Ring:
    RISING = (0, 1, 2, 3, 4, 5, 7), (0, 1, 2, 4, 5, 6, 8, 9), (0, 1, 4, 5, 6, 8, 9, 12, 13), (4, 5, 7, 8, 9, 10, 11, 12, 13)
    FALLING = (0, 1, 2, 3, 4, 5), (0, 1, 4, 5, 6, 8, 9), (0, 1, 4, 5, 6, 14, 8, 9, 12, 13), (4, 5, 7, 8, 9, 10, 11, 12, 13)

    def __init__(self, source, gathered, send, recv, local, span, falling):
        self.source, self.gathered, self.send, self.recv, self.local = source, gathered, send, recv, local
        chips = span // 2
        self.g, self.p = lax.axis_index("dp"), lax.axis_index("pair")
        core, chip = self.p % 2, self.p // 2
        at = lambda step: ((chip + step) % chips) * 2 + core
        self.up, self.down, self.far = at(chips - 1 if falling else 1), at(1 if falling else chips - 1), at(2)
        self.rank = chips - 1 - chip if falling else chip
        self.falling, self.sends = falling, self.FALLING if falling else self.RISING
        self.other = chip * 2 + 1 - core

    def copy(self, i):
        p, up, down, far, other = self.p, self.up, self.down, self.far, self.other
        owner, part, to = (
            (p, 0, up),
            (p, 1, up),
            (p, 1, down),
            (p, 0, down),
            (p, 0, other),
            (p, 1, other),
            (down, 0, up),
            (up, 1, down),
            (down, 0, other),
            (down, 1, other),
            (up, 1, other),
            (up, 0, other),
            (far, 0, other),
            (far, 1, other),
            (down, 1, up),
        )[i]
        half = self.source.shape[0] // 2
        rows = pl.ds(part * half, half)
        return pltpu.make_async_remote_copy(
            src_ref=self.source.at[rows] if i < 6 else self.gathered.at[owner, rows],
            dst_ref=self.gathered.at[owner, rows],
            send_sem=self.send.at[i],
            recv_sem=self.recv.at[i],
            device_id=(self.g, to),
            device_id_type=MESH,
        )

    def own(self):
        return pltpu.make_async_copy(self.source, self.gathered.at[self.p], self.local)

    def when(self, *ranks):
        def decorate(steps):
            for rank in ranks:
                pl.when(self.rank == rank)(functools.partial(steps, rank))

        return decorate

    def start(self):
        self.own().start()

        @self.when(0, 1, 2, 3)
        def _(rank):
            for i in (0, 2, 1, 3, 4, 5):
                if i in self.sends[rank]:
                    self.copy(i).start()

    def arrive(self, *which):
        for i in which:
            self.copy(i).wait_recv()

    def after(self, arrived, *sent):
        self.arrive(arrived)
        for i in sent:
            self.copy(i).start()

    def relay_near(self):
        @self.when(0, 1, 2, 3)
        def _(rank):
            if rank == 0:
                if not self.falling:
                    self.after(2, 7)
            elif rank == 3:
                self.after(0, 8)
                self.after(1, 9)
            else:
                self.after(0, 6, 8)
                self.after(1, *((14, 9) if self.falling and rank == 2 else (9,)))

    def relay_wrap(self):
        @self.when(3)
        def _(rank):
            self.after(2, 7, 10)
            self.after(3, 11)

    def relay_far(self):
        @self.when(2, 3)
        def _(rank):
            self.after(6, 12)
            self.after(14 if self.falling and rank == 3 else 7, 13)

    def handed_own(self):
        self.arrive(4, 5)

    def handed_near(self):
        @self.when(1, 2, 3)
        def _(rank):
            self.arrive(8, 9)

    def handed_wrap(self):
        @self.when(3)
        def _(rank):
            self.arrive(10, 11)

    def handed_far(self):
        @self.when(2, 3)
        def _(rank):
            self.arrive(12, 13)

    def sent(self):
        @self.when(0, 1, 2, 3)
        def _(rank):
            for i in self.sends[rank]:
                self.copy(i).wait_send()


def attend(
    meta_ref, q_ref, kv_ref, u_ref, x_ref, w_ref, og_ref, out_ref, dhu_ref, gout_ref, dq_ref, dk_ref, dv_ref, kv_all,
    q_all, da_all, da, parts, acc, mask, local, send, recv, group, early, *, span
):
    own = lax.axis_index("pair")
    chips, core, chip = span // 2, own % 2, own // 2
    size, width = q_ref.shape
    kv_ring, q_ring, da_ring = (
        Ring(source, gathered, send.at[i], recv.at[i], local.at[i], span, falling)
        for i, (source, gathered, falling) in enumerate(
            ((kv_ref, kv_all, False), (q_ref, q_all, True), (da, da_all, True))
        )
    )
    for g in (3, 1, 2):
        group(g)
    kv_ring.start()
    q_ring.start()
    group(0)
    dhu_ref[...] = dot_t(og_ref[...], w_ref[...])

    def on_step(step, *actions):
        for k, action in enumerate(actions):
            if action:
                pl.when(step == k)(action)

    def block_at(step, falling):
        turn = step // 2
        shift = turn if falling else (3 * turn - (turn * (turn - 1)) // 2) % 4
        return ((chip + shift) % chips) * 2 + (core + step % 2) % 2

    def split(value, at):
        parts[at] = even_half(value)
        parts[at + 1] = odd_half(value)

    def slabs(work):
        def one(s, carry):
            first = pl.multiple_of(s * 128, 128)
            work(pl.ds(first, 128), pl.ds(pl.multiple_of(width + s * 128, 128), 128))
            return carry

        lax.fori_loop(0, width // 128, one, 0, unroll=True)

    def both(rows):
        return jnp.concatenate([even_half(rows), odd_half(rows)], axis=0)

    zeros = meta_ref[0:1, 2:3].astype(I32)
    split(q_ref[...] * 0.0625, 0)
    split(kv_ref[:, :width] * 0.0625, 4)
    split(kv_ref[:, width:] * 0.0625, 6)
    acc[...] = jnp.zeros_like(acc)
    dq_ref[...] = jnp.zeros_like(dq_ref)
    dk_ref[...] = jnp.zeros_like(dk_ref)
    dv_ref[...] = jnp.zeros_like(dv_ref)

    def forward(step, carry):
        j = block_at(step, False)

        def near():
            kv_ring.relay_wrap()
            kv_ring.relay_near()
            q_ring.relay_near()
            q_ring.relay_wrap()

        def far():
            kv_ring.relay_far()
            q_ring.relay_far()

        on_step(
            step, kv_ring.own().wait, kv_ring.handed_own, near, kv_ring.handed_near, None, kv_ring.handed_wrap, far,
            kv_ring.handed_far
        )

        @pl.when(j <= own)
        def _():
            mask[...] = visible(0, size, own, j, zeros) * meta_ref[pl.ds(j, 1), 0:1]

            def work(cols, late):
                keys = kv_all[j, :, cols]
                weights = []
                for half in range(2):
                    h = dot_t(parts[half, :, cols], keys)
                    weights.append((h * ((1.0 + jnp.tanh(h)) * mask[...])).astype(BF16))
                acc[:, cols] += dot(jnp.concatenate(weights, axis=1), both(kv_all[j, :, late]))

            slabs(work)

        return carry

    lax.fori_loop(0, span, forward, 0)

    normed, spread = normalize(acc[...])
    gate = u_ref[...].astype(F32)
    gated = (normed * gate).astype(BF16)
    dy = dhu_ref[...]
    da[...] = norm_back(dy * gate, normed, spread).astype(BF16)
    da_ring.start()
    split(da[...] * 0.0625, 2)
    dhu_ref[...] = dy * normed
    out_ref[...] = (dot(gated, w_ref[...]) + x_ref[...].astype(F32)).astype(BF16)
    gout_ref[...] = lax.dot_general(gated, og_ref[...], (((0,), (0,)), ((), ())), preferred_element_type=F32)
    early(0)

    def by_query(step, carry):
        j = block_at(step, False)

        @pl.when(j <= own)
        def _():
            mask[...] = visible(0, size, own, j, zeros) * meta_ref[pl.ds(j, 1), 0:1]

            def work(cols, late):
                keys = kv_all[j, :, cols]
                values = kv_all[j, :, late]
                grads = []
                for half in range(2):
                    h = dot_t(parts[half, :, cols], keys)
                    u = 1.0 + jnp.tanh(h)
                    seen = u * mask[...]
                    slope = seen + h * seen * (2.0 - u)
                    grads.append((dot_t(parts[2 + half, :, cols], values) * slope).astype(BF16))
                dq_ref[:, cols] += dot(jnp.concatenate(grads, axis=1), both(keys))

            slabs(work)

        return carry

    lax.fori_loop(0, span, by_query, 0)
    early(1)

    def by_key(step, carry):
        i = block_at(step, True)

        def mine():
            q_ring.own().wait()
            da_ring.own().wait()

        def pair(name):
            def action():
                getattr(q_ring, name)()
                getattr(da_ring, name)()

            return action

        on_step(
            step, mine, pair("handed_own"), da_ring.relay_near, pair("handed_near"), da_ring.relay_far, pair("handed_far"),
            da_ring.relay_wrap, pair("handed_wrap")
        )

        @pl.when(i >= own)
        def _():
            mask[...] = visible(1, size, i, own, zeros) * meta_ref[pl.ds(i, 1), 1:2]

            def work(cols, late):
                queries = q_all[i, :, cols]
                dafter = da_all[i, :, cols]
                grads, weights = [], []
                for half in range(2):
                    h = dot_t(parts[4 + half, :, cols], queries)
                    u = 1.0 + jnp.tanh(h)
                    seen = u * mask[...]
                    weight = h * seen
                    weights.append(weight.astype(BF16))
                    slope = seen + weight * (2.0 - u)
                    grads.append((dot_t(parts[6 + half, :, cols], dafter) * slope).astype(BF16))
                dk_ref[:, cols] += dot(jnp.concatenate(grads, axis=1), both(queries))
                dv_ref[:, cols] += dot(jnp.concatenate(weights, axis=1), both(dafter))

            slabs(work)

        return carry

    lax.fori_loop(0, span, by_key, 0)
    for ring in (kv_ring, q_ring, da_ring):
        ring.sent()


def interleave(upper, lower, rows, out_ref):
    count, cols = upper.shape
    top = (iota((count, cols), 0) % (2 * rows)) < rows
    first = jnp.where(top, upper, pltpu.roll(lower, rows, 0))
    second = jnp.where(top, pltpu.roll(upper, count - rows, 0), lower)
    out_ref[0] = first.reshape(out_ref.shape[1:])
    out_ref[1] = second.reshape(out_ref.shape[1:])


def weigh(g, grad, z_ref, turned_ref, w_ref, dxn_ref):
    width = grad.shape[1]
    cols = slice(g * width, (g + 1) * width)
    h = 0.5 * z_ref[:, cols]
    t = jnp.tanh(h)
    slope = 0.5 * (1.0 + t) * (1.0 + h * (1.0 - t))
    dz = (grad * slope).astype(BF16)
    dxn_ref[...] += dot_t(dz, w_ref[:, cols])
    return dot(turned_ref[...], dz)


def finish(dxn_ref, x_ref, og_ref, tr_ref, send_ref):
    size = x_ref.shape[0]
    normed, spread = normalize(x_ref[...].astype(F32))
    dx = norm_back(dxn_ref[...], normed, spread) + og_ref[...].astype(F32)
    count = send_ref.shape[0] * send_ref.shape[1]
    pick = jnp.where(iota((count, size), 0) == tr_ref[...], 1.0, 0.0).astype(BF16)
    send_ref[...] = dot(pick, dx.astype(BF16)).astype(BF16).reshape(send_ref.shape)


def partner(k, groups, span):
    g, p = lax.axis_index("dp"), lax.axis_index("pair")
    chips, side = span // 2, math.isqrt(groups)
    to_p = ((p // 2 + (k // 2) % chips) % chips) * 2 + (p % 2 + k % 2) % 2
    shift = k // span
    to_g = ((g // side + shift // side) % side) * side + (g % side + shift % side) % side
    return to_g, to_p


def greet(groups, span):
    g, p = lax.axis_index("dp"), lax.axis_index("pair")
    barrier = pltpu.get_barrier_semaphore()

    def hello(device):
        pl.semaphore_signal(barrier, inc=1, device_id=device, device_id_type=MESH)

    def hello_pair(k, carry):
        hello((g, partner(k, groups, span)[1]))
        return carry

    def hello_group(k, carry):
        hello((partner(k * span, groups, span)[0], p))
        return carry

    lax.fori_loop(1, span, hello_pair, 0)
    lax.fori_loop(1, groups, hello_group, 0)
    return lambda: pl.semaphore_wait(barrier, span + groups - 2)


def ask(request, middle, slots, sems, groups, span):
    g, p = lax.axis_index("dp"), lax.axis_index("pair")
    own = pltpu.make_async_copy(request.at[:, p], middle.at[p], sems.at[0])
    own.start()

    def over_pair(k, carry):
        to_p = partner(k, groups, span)[1]
        pltpu.make_async_remote_copy(
            src_ref=request.at[:, to_p],
            dst_ref=middle.at[p],
            send_sem=sems.at[1],
            recv_sem=sems.at[2],
            device_id=(g, to_p),
            device_id_type=MESH,
        ).start()
        return carry

    lax.fori_loop(1, span, over_pair, 0)
    own.wait()
    drain(middle, span - 1, sems.at[1])
    drain(middle, span - 1, sems.at[2])
    own = pltpu.make_async_copy(middle.at[:, g], slots.at[g], sems.at[3])
    own.start()

    def over_groups(k, carry):
        to_g = partner(k * span, groups, span)[0]
        pltpu.make_async_remote_copy(
            src_ref=middle.at[:, to_g],
            dst_ref=slots.at[g],
            send_sem=sems.at[4],
            recv_sem=sems.at[5],
            device_id=(to_g, p),
            device_id_type=MESH,
        ).start()
        return carry

    lax.fori_loop(1, groups, over_groups, 0)
    own.wait()
    if groups > 1:
        drain(slots, groups - 1, sems.at[4])
        drain(slots, groups - 1, sems.at[5])


def drain(ref, count, sem):
    part = ref.at[pl.ds(0, count)]
    pltpu.make_async_copy(part, part, sem).wait()


def push_all(source, target, send, recv, groups, span, rows):
    me = lax.axis_index("dp") * span + lax.axis_index("pair")
    used = pl.ds(0, rows)

    def push(k, carry):
        to_g, to_p = partner(k, groups, span)
        pltpu.make_async_remote_copy(
            src_ref=source.at[to_g * span + to_p, used],
            dst_ref=target.at[me, used],
            send_sem=send,
            recv_sem=recv,
            device_id=(to_g, to_p),
            device_id_type=MESH,
        ).start()
        return carry

    lax.fori_loop(1, groups * span, push, 0)

    def wait():
        all_of = target.at[pl.ds(0, groups * span - 1), used]
        pltpu.make_async_copy(all_of, all_of, send).wait()
        pltpu.make_async_copy(all_of, all_of, recv).wait()

    return wait


def keep(source, target, sem, span):
    me = lax.axis_index("dp") * span + lax.axis_index("pair")
    copy = pltpu.make_async_copy(source.at[me], target.at[me], sem)
    copy.start()
    return copy


def push_early(early_ref, arrived_ref, cols, sems, groups, span):
    g, p = lax.axis_index("dp"), lax.axis_index("pair")
    count = early_ref.shape[0] // groups

    def mine(to_g):
        return early_ref.at[pl.ds(pl.multiple_of(to_g * count, count), count), cols]

    own = pltpu.make_async_copy(mine(g), arrived_ref.at[g, :, cols], sems.at[0])
    own.start()

    def push(k, carry):
        to_g = partner(k * span, groups, span)[0]
        pltpu.make_async_remote_copy(
            src_ref=mine(to_g),
            dst_ref=arrived_ref.at[g, :, cols],
            send_sem=sems.at[1],
            recv_sem=sems.at[2],
            device_id=(to_g, p),
            device_id_type=MESH,
        ).start()
        return carry

    lax.fori_loop(1, groups, push, 0)


def wait_early(early_ref, arrived_ref, cols, sems, groups):
    pltpu.make_async_copy(arrived_ref.at[0, :, cols], arrived_ref.at[0, :, cols], sems.at[0]).wait()
    if groups > 1:
        others = arrived_ref.at[pl.ds(0, groups - 1), :, cols]
        pltpu.make_async_copy(others, others, sems.at[1]).wait()
        pltpu.make_async_copy(others, others, sems.at[2]).wait()


def settle(arrived_ref, halves_ref, settled_ref, sems, groups, span, rows):
    g, p = lax.axis_index("dp"), lax.axis_index("pair")
    count, cols = arrived_ref.shape[1:]

    def add(k, summed):
        return summed + arrived_ref[k].astype(F32)

    summed = lax.fori_loop(0, groups, add, jnp.zeros((count, cols), F32))
    interleave(summed[:, : cols // 2], summed[:, cols // 2 :], rows, halves_ref)
    own = pltpu.make_async_copy(halves_ref.at[p % 2, p // 2], settled_ref.at[p], sems.at[0])
    own.start()

    def push(k, carry):
        to_p = partner(k, groups, span)[1]
        pltpu.make_async_remote_copy(
            src_ref=halves_ref.at[to_p % 2, to_p // 2],
            dst_ref=settled_ref.at[p],
            send_sem=sems.at[1],
            recv_sem=sems.at[2],
            device_id=(g, to_p),
            device_id_type=MESH,
        ).start()
        return carry

    lax.fori_loop(1, span, push, 0)

    def wait():
        own.wait()
        drain(settled_ref, span - 1, sems.at[1])
        drain(settled_ref, span - 1, sems.at[2])

    return wait


def swap_halves(grads_ref, got, sems):
    g, p = lax.axis_index("dp"), lax.axis_index("pair")
    core = p % 2
    swap = pltpu.make_async_remote_copy(
        src_ref=grads_ref.at[1 - core],
        dst_ref=got,
        send_sem=sems.at[1],
        recv_sem=sems.at[2],
        device_id=(g, p + 1 - 2 * core),
        device_id_type=MESH,
    )
    swap.start()
    return swap


def exchange_gradients(
    rows_ref, grads_ref, back_ref, parts_ref, got, part, sems, swap, between, *, groups, span, bound
):
    total = groups * span
    g, p = lax.axis_index("dp"), lax.axis_index("pair")
    me, core = g * span + p, p % 2
    chip, chips = me // 2, total // 2
    own = keep(rows_ref, back_ref, sems.at[0], span)
    landed = push_all(rows_ref, back_ref, sems.at[3], sems.at[4], groups, span, bound)
    swap.wait()

    def add(m, carry):
        part[m] = (grads_ref[core, m] + got[m]).astype(BF16)
        return carry

    lax.fori_loop(0, chips, add, 0)
    mine = pltpu.make_async_copy(part.at[chip], parts_ref.at[chip], sems.at[5])
    mine.start()

    def push_part(k, carry):
        to_g, to_p = partner(2 * k, groups, span)
        pltpu.make_async_remote_copy(
            src_ref=part.at[(to_g * span + to_p) // 2],
            dst_ref=parts_ref.at[chip],
            send_sem=sems.at[6],
            recv_sem=sems.at[7],
            device_id=(to_g, to_p),
            device_id_type=MESH,
        ).start()
        return carry

    lax.fori_loop(1, chips, push_part, 0)
    settled = between()
    own.wait()
    mine.wait()
    settled()
    landed()
    drain(parts_ref, chips - 1, sems.at[6])
    drain(parts_ref, chips - 1, sems.at[7])


def update_kernel(
    slots_ref, back_ref, table_ref, accum_ref, parts_ref, settled_ref, layer_ref, tnew_ref, anew_ref, gin_ref, gout_ref,
    out_ref, *, width, factor
):
    shards = slots_ref.shape[0] * slots_ref.shape[1]
    rows_dev, model = table_ref.shape
    count = shards * width
    spread = ((iota((shards, count), 1) // width) == iota((shards, count), 0)).astype(F32).astype(BF16)
    high, low = slot_halves(slots_ref[...].reshape(shards, 128))
    turn = lambda a: lax.dot_general(a, spread, (((0,), (0,)), ((), ())), preferred_element_type=F32)
    value = 2.0 * turn(high) + turn(low)
    mine = iota((128, count), 0) == (iota((128, count), 1) % width)
    slot = jnp.sum(jnp.where(mine, value, 0.0), axis=0, keepdims=True).astype(I32)
    pick = jnp.where(iota((rows_dev, count), 0) == slot, 1.0, 0.0).astype(BF16)
    total = dot(pick, back_ref[...].reshape(count, model))
    square = jnp.mean(total * total, axis=1, keepdims=True)
    eye = iota((rows_dev, rows_dev), 0) == iota((rows_dev, rows_dev), 1)
    accum = jnp.sum(jnp.where(eye, accum_ref[...], 0.0), axis=1, keepdims=True) + square
    anew_ref[...] = jnp.sum(jnp.where(eye, accum, 0.0), axis=0, keepdims=True)
    tnew_ref[...] = table_ref[...] - LEARN_RATE * total / jnp.sqrt(accum)

    def total_of(ref):
        def add(m, summed):
            return summed + ref[m].astype(F32)

        summed = lax.fori_loop(0, ref.shape[0], add, jnp.zeros(ref.shape[1:], F32)) * factor
        return summed[:rows], summed[rows:]

    rows = gin_ref.shape[0]
    half = model // 2
    gin_ref[:, model : 2 * model], gin_ref[:, 3 * model :] = total_of(parts_ref)
    upper, lower = total_of(settled_ref)
    gin_ref[:, :model] = upper[:, :model]
    gin_ref[:, 2 * model : 3 * model] = lower[:, half:]
    gout_ref[:, :half] = upper[:, model:]
    gout_ref[:, half:] = lower[:, :half]
    out_ref[...] = layer_ref[...]


def layer_kernel(
    row_ref, seg_ref, pair_ref, w_in_hbm, w_out_hbm, og_hbm, table_hbm, out_ref, slots, back, landed, settled,
    w_in_ref, w_out_ref, og_ref, table_ref, request, middle, target_r, target_c, meta, found, fetched, x, z, u, q, kv, dhu, wgrad, dq, dk, dv, kv_all,
    q_all, da_all, da, parts, acc, mask, turned, dxn, early, arrived, halves, grads, sending, got, part, local, send, recv, front, sems,
    load_sems, first_sems, second_sems, settle_sems, *,
    groups, span, width, rows
):
    tokens, rows_dev = row_ref.shape[0], table_ref.shape[0]
    bound = 2 * tokens // (groups * span)
    loads = [
        pltpu.make_async_copy(source, target, load_sems.at[i])
        for i, (source, target) in enumerate(
            ((table_hbm, table_ref), (w_in_hbm, w_in_ref), (w_out_hbm, w_out_ref), (og_hbm, og_ref))
        )
    ]
    for load in loads:
        load.start()
    fetched[...] = jnp.zeros_like(fetched)
    back[...] = jnp.zeros_like(back)
    ready = greet(groups, span)
    route(row_ref, seg_ref, pair_ref, request, target_r, target_c, meta, rows_dev=rows_dev, width=width)
    ready()
    ask(request, middle, slots, front, groups, span)
    for load in loads:
        load.wait()
    find(slots, table_ref, found, width=width)
    own = keep(found, fetched, front.at[6], span)
    answered = push_all(found, fetched, front.at[7], front.at[8], groups, span, bound)
    own.wait()
    answered()
    group = project(fetched, target_c, w_in_ref, x, z, u, q, kv, turned)
    dxn[...] = jnp.zeros_like(dxn)
    model = x.shape[1]
    stages = ((slice(0, 2 * model), first_sems), (slice(2 * model, 3 * model), second_sems))

    def weight(g, grad):
        return weigh(g, grad[...], z, turned, w_in_ref, dxn)

    def begin(stage):
        if stage == 0:
            early[:, :model] = weight(0, dhu).astype(BF16)
            early[:, model : 2 * model] = wgrad[...].astype(BF16)
        else:
            early[:, 2 * model :] = weight(2, dq).astype(BF16)
        push_early(early, arrived, *stages[stage], groups, span)

    def between():
        for stage in stages:
            wait_early(early, arrived, *stage, groups)
        return settle(arrived, halves, settled, settle_sems, groups, span, rows)

    attend(
        meta, q, kv, u, x, w_out_ref, og_ref, out_ref, dhu, wgrad, dq, dk, dv, kv_all, q_all, da_all, da, parts, acc,
        mask, local, send, recv, group, begin, span=span
    )
    interleave(weight(1, dv), weight(3, dk), rows, grads)
    swap = swap_halves(grads, got, sems)
    finish(dxn, x, og_ref, target_r, sending)
    exchange_gradients(
        sending, grads, back, landed, got, part, sems, swap, between, groups=groups, span=span, bound=bound
    )


def shape(dims, dtype):
    return jax.ShapeDtypeStruct(dims, dtype)


def body(table, accum, item_row, segments, pairs, w_in, w_out, out_grad):
    tokens = item_row.shape[0]
    rows_dev, model = table.shape
    shards = lax.axis_size(("dp", "pair"))
    span = lax.axis_size("pair")
    width = -(-(2 * tokens // shards) // 8) * 8
    rows = model // shards
    chunk = (2 * rows, model)
    groups = shards // span
    settling = (2 * rows, 3 * model // 2)
    half_grads = (shards // 2,) + chunk
    block = lambda cols: VMEM((span, tokens, cols), BF16)
    low = lambda cols: VMEM((tokens, cols), BF16)
    high = lambda cols: VMEM((tokens, cols), F32)
    request = (groups, span, 1, 128)
    parcel = (shards, width, model)
    layer_out, slots, back, landed, settled = pl.pallas_call(
        functools.partial(layer_kernel, groups=groups, span=span, width=width, rows=rows),
        out_shape=(
            shape((tokens, model), BF16),
            shape(request, I32),
            shape(parcel, BF16),
            shape(half_grads, BF16),
            shape((span,) + settling, F32),
        ),
        in_specs=[whole()] * 3 + [pl.BlockSpec(memory_space=pl.ANY)] * 4,
        out_specs=[whole()] * 5,
        scratch_shapes=[
            VMEM(w_in.shape, BF16),
            VMEM(w_out.shape, BF16),
            VMEM(out_grad.shape, BF16),
            VMEM(table.shape, F32),
            VMEM(request, I32),
            VMEM((span, groups, 1, 128), I32),
            VMEM((1, tokens), I32),
            VMEM((tokens, 1), I32),
            VMEM((8, 128), F32),
            VMEM((shards, width, model), BF16),
            VMEM((shards, width, model), BF16),
            low(model),
            high(4 * model),
            low(model),
            low(model),
            low(2 * model),
            high(model),
            VMEM((model, model), F32),
            high(model),
            high(model),
            high(model),
            block(2 * model),
            block(model),
            block(model),
            low(model),
            VMEM((8, tokens, model), BF16),
            high(model),
            high(tokens),
            VMEM((model, tokens), BF16),
            high(model),
            VMEM((model, 3 * model), BF16),
            VMEM((groups, model // groups, 3 * model), BF16),
            VMEM((2, span // 2) + settling, F32),
            VMEM((2,) + half_grads, F32),
            VMEM(parcel, BF16),
            VMEM(half_grads, F32),
            VMEM(half_grads, BF16),
            pltpu.SemaphoreType.DMA((3,)),
            pltpu.SemaphoreType.DMA((3, 15)),
            pltpu.SemaphoreType.DMA((3, 15)),
            pltpu.SemaphoreType.DMA((9,)),
            pltpu.SemaphoreType.DMA((8,)),
            pltpu.SemaphoreType.DMA((4,)),
            pltpu.SemaphoreType.DMA((3,)),
            pltpu.SemaphoreType.DMA((3,)),
            pltpu.SemaphoreType.DMA((3,)),
        ],
        compiler_params=params(collective_id=0, has_side_effects=True),
    )(item_row, segments, pairs[0].T, w_in, w_out, out_grad, table)
    table_new, accum_new, grad_in, grad_out, layer_out = pl.pallas_call(
        functools.partial(update_kernel, width=width, factor=1.0 / math.sqrt(tokens * shards)),
        out_shape=(
            shape((rows_dev, model), F32),
            shape((1, rows_dev), F32),
            shape((rows, 4 * model), F32),
            shape((rows, model), F32),
            shape((tokens, model), BF16),
        ),
        in_specs=[whole()] * 7,
        out_specs=[whole()] * 5,
        compiler_params=params(),
    )(slots, back, table, accum.reshape(1, rows_dev), landed, settled, layer_out)
    return layer_out, table_new, accum_new.reshape(rows_dev), grad_in, grad_out


def solution(mesh):
    both = ("dp", "pair")
    return jax.shard_map(
        body,
        mesh=mesh,
        in_specs=(
            P(both, None),
            P(both),
            P(both),
            P("dp", None),
            P("dp", None, None),
            P(),
            P(),
            P(both, None),
        ),
        out_specs=(P(both, None), P(both, None), P(both), P(both, None), P(both, None)),
        check_vma=False,
    )
```

```python
import functools
import math

import jax
import jax.numpy as jnp
from jax import lax
from jax.experimental import pallas as pl
from jax.experimental.pallas import tpu as pltpu
from jax.sharding import PartitionSpec as P

HEADS = 8
NORM_EPS = 1e-05
LEARN_RATE = 0.5
F32, BF16, I32 = jnp.float32, jnp.bfloat16, jnp.int32
VMEM = pltpu.VMEM
MESH = pl.DeviceIdType.MESH
BIG = 62 * 1024 * 1024


def whole():
    return pl.BlockSpec(memory_space=pltpu.VMEM)


def params(**kw):
    return pltpu.CompilerParams(vmem_limit_bytes=BIG, **kw)


def dot(a, b):
    return lax.dot_general(a, b, (((1,), (0,)), ((), ())), preferred_element_type=F32)


def dot_t(a, b):
    return lax.dot_general(a, b, (((1,), (1,)), ((), ())), preferred_element_type=F32)


def iota(shape, axis):
    return lax.broadcasted_iota(I32, shape, axis)


def normalize(values):
    row_mean = jnp.mean(values, axis=-1, keepdims=True)
    centred = values - row_mean
    spread = jnp.sqrt(jnp.mean(centred * centred, axis=-1, keepdims=True) + NORM_EPS)
    return centred / spread, spread


def norm_back(grad_rows, normed, spread):
    first = jnp.mean(grad_rows, axis=-1, keepdims=True)
    second = jnp.mean(grad_rows * normed, axis=-1, keepdims=True)
    return (grad_rows - first - normed * second) / spread


def even_half(rows):
    lane = iota(rows.shape, 1) & 127
    return jnp.where(lane < 64, rows, jnp.zeros_like(rows))


def odd_half(rows):
    lane = iota(rows.shape, 1) & 127
    return jnp.where(lane < 64, jnp.zeros_like(rows), rows)


def route(row_ref, seg_ref, pair_ref, req_ref, tr_ref, tc_ref, meta_ref, *, rows_dev, width):
    tokens = row_ref.shape[0]
    shards = req_ref.shape[0] * req_ref.shape[1]
    shift = rows_dev.bit_length() - 1
    sub, lane = iota((tokens, tokens), 0), iota((tokens, tokens), 1)
    row = row_ref[...].reshape(1, tokens)
    owner_r = row >> shift
    slot_r = (row & (rows_dev - 1)).astype(F32)
    owner_c = jnp.sum(jnp.where(sub == lane, owner_r.astype(F32), 0.0), axis=1, keepdims=True).astype(I32)
    same = owner_c == owner_r
    rank_c = jnp.sum(jnp.where(same & (lane < sub), 1.0, 0.0), axis=1, keepdims=True).astype(I32)
    rank_r = jnp.sum(jnp.where(same & (sub < lane), 1.0, 0.0), axis=0, keepdims=True).astype(I32)
    tr_ref[...] = owner_r * width + rank_r
    tc_ref[...] = owner_c * width + rank_c
    dest = iota((shards, tokens), 0) == owner_r
    place = iota((shards, 128), 1)
    req = jnp.zeros((shards, 128), F32)
    for k in range(2 * tokens // shards):
        picked = jnp.sum(jnp.where(dest & (rank_r == k), slot_r, 0.0), axis=1, keepdims=True)
        req = jnp.where(place == k, picked, req)
    req_ref[...] = req.astype(I32).reshape(req_ref.shape)
    own = lax.axis_index("pair")
    first, second = pair_ref[0:1, :], pair_ref[1:2, :]
    span = iota((8, first.shape[1]), 0)
    as_query = jnp.max(jnp.where((first == own) & (second == span), 1.0, 0.0), axis=1, keepdims=True)
    as_key = jnp.max(jnp.where((second == own) & (first == span), 1.0, 0.0), axis=1, keepdims=True)
    zeros = jnp.sum(jnp.where(seg_ref[...] == 0, 1.0, 0.0), axis=1, keepdims=True)
    at = iota((8, 128), 1)
    meta_ref[...] = jnp.where(at == 0, as_query, jnp.where(at == 1, as_key, jnp.where(at == 2, zeros, 0.0)))


def slot_halves(slots):
    high = (slots >> 1).astype(F32).astype(BF16)
    low = (slots & 1).astype(F32).astype(BF16)
    return high, low


def find(slots_ref, table_ref, found_ref, *, width):
    shards = slots_ref.shape[0] * slots_ref.shape[1]
    rows_dev = table_ref.shape[0]
    count = shards * width
    spread = ((iota((count, shards), 0) // width) == iota((count, shards), 1)).astype(F32).astype(BF16)
    high, low = slot_halves(slots_ref[...].reshape(shards, 128))
    value = 2.0 * dot(spread, high) + dot(spread, low)
    mine = iota((count, 128), 1) == (iota((count, 128), 0) % width)
    slot = jnp.sum(jnp.where(mine, value, 0.0), axis=1, keepdims=True).astype(I32)
    pick = jnp.where(iota((count, rows_dev), 1) == slot, 1.0, 0.0).astype(BF16)
    found_ref[...] = dot(pick, table_ref[...].astype(BF16)).astype(BF16).reshape(found_ref.shape)


def project(fetched_ref, tc_ref, w_ref, x_ref, z_ref, u_ref, q_ref, kv_ref, turned_ref):
    width = fetched_ref.shape[2]
    count = fetched_ref.shape[0] * fetched_ref.shape[1]
    tokens = tc_ref.shape[0]
    pick = jnp.where(iota((tokens, count), 1) == tc_ref[...], 1.0, 0.0).astype(BF16)
    rows = dot(pick, fetched_ref[...].reshape(count, width))
    x_ref[...] = rows.astype(BF16)
    normed, _ = normalize(rows)
    low = normed.astype(BF16)
    turned_ref[...] = jnp.transpose(normed).astype(BF16)
    outs = (u_ref.at[...], kv_ref.at[:, width:], q_ref.at[...], kv_ref.at[:, :width])

    def group(g):
        z = dot(low, w_ref[:, g * width : (g + 1) * width])
        z_ref[:, g * width : (g + 1) * width] = z
        half = 0.5 * z
        outs[g][...] = (half + half * jnp.tanh(half)).astype(BF16)

    return group


def visible(q_axis, size, q_block, k_block, zeros):
    q_pos = iota((size, size), q_axis) + q_block * size
    k_pos = iota((size, size), 1 - q_axis) + k_block * size
    least = jnp.where(q_pos >= zeros, zeros, 0)
    return jnp.where((k_pos >= least) & (k_pos <= q_pos), 1.0, 0.0)


class Ring:
    RISING = (0, 1, 2, 3, 4, 5, 7), (0, 1, 2, 4, 5, 6, 8, 9), (0, 1, 4, 5, 6, 8, 9, 12, 13), (4, 5, 7, 8, 9, 10, 11, 12, 13)
    FALLING = (0, 1, 2, 3, 4, 5), (0, 1, 4, 5, 6, 8, 9), (0, 1, 4, 5, 6, 14, 8, 9, 12, 13), (4, 5, 7, 8, 9, 10, 11, 12, 13)

    def __init__(self, source, gathered, send, recv, local, span, falling):
        self.source, self.gathered, self.send, self.recv, self.local = source, gathered, send, recv, local
        chips = span // 2
        self.g, self.p = lax.axis_index("dp"), lax.axis_index("pair")
        core, chip = self.p % 2, self.p // 2
        at = lambda step: ((chip + step) % chips) * 2 + core
        self.up, self.down, self.far = at(chips - 1 if falling else 1), at(1 if falling else chips - 1), at(2)
        self.rank = chips - 1 - chip if falling else chip
        self.falling, self.sends = falling, self.FALLING if falling else self.RISING
        self.other = chip * 2 + 1 - core

    def copy(self, i):
        p, up, down, far, other = self.p, self.up, self.down, self.far, self.other
        owner, part, to = (
            (p, 0, up),
            (p, 1, up),
            (p, 1, down),
            (p, 0, down),
            (p, 0, other),
            (p, 1, other),
            (down, 0, up),
            (up, 1, down),
            (down, 0, other),
            (down, 1, other),
            (up, 1, other),
            (up, 0, other),
            (far, 0, other),
            (far, 1, other),
            (down, 1, up),
        )[i]
        half = self.source.shape[0] // 2
        rows = pl.ds(part * half, half)
        return pltpu.make_async_remote_copy(
            src_ref=self.source.at[rows] if i < 6 else self.gathered.at[owner, rows],
            dst_ref=self.gathered.at[owner, rows],
            send_sem=self.send.at[i],
            recv_sem=self.recv.at[i],
            device_id=(self.g, to),
            device_id_type=MESH,
        )

    def own(self):
        return pltpu.make_async_copy(self.source, self.gathered.at[self.p], self.local)

    def when(self, *ranks):
        def decorate(steps):
            for rank in ranks:
                pl.when(self.rank == rank)(functools.partial(steps, rank))

        return decorate

    def start(self):
        self.own().start()

        @self.when(0, 1, 2, 3)
        def _(rank):
            for i in (0, 2, 1, 3, 4, 5):
                if i in self.sends[rank]:
                    self.copy(i).start()

    def start_part(self, part):
        if part == 1:
            self.own().start()

        @self.when(0, 1, 2, 3)
        def _(rank):
            for i in ((0, 3, 4), (1, 2, 5))[part]:
                if i in self.sends[rank]:
                    self.copy(i).start()

    def arrive(self, *which):
        for i in which:
            self.copy(i).wait_recv()

    def after(self, arrived, *sent):
        self.arrive(arrived)
        for i in sent:
            self.copy(i).start()

    def relay_near(self):
        @self.when(0, 1, 2, 3)
        def _(rank):
            if rank == 0:
                if not self.falling:
                    self.after(2, 7)
            elif rank == 3:
                self.after(0, 8)
                self.after(1, 9)
            else:
                self.after(0, 6, 8)
                self.after(1, *((14, 9) if self.falling and rank == 2 else (9,)))

    def relay_wrap(self):
        @self.when(3)
        def _(rank):
            self.after(2, 7, 10)
            self.after(3, 11)

    def relay_far(self):
        @self.when(2, 3)
        def _(rank):
            self.after(6, 12)
            self.after(14 if self.falling and rank == 3 else 7, 13)

    def handed_own(self):
        self.arrive(4, 5)

    def handed_near(self):
        @self.when(1, 2, 3)
        def _(rank):
            self.arrive(8, 9)

    def handed_wrap(self):
        @self.when(3)
        def _(rank):
            self.arrive(10, 11)

    def handed_far(self):
        @self.when(2, 3)
        def _(rank):
            self.arrive(12, 13)

    def sent(self):
        @self.when(0, 1, 2, 3)
        def _(rank):
            for i in self.sends[rank]:
                self.copy(i).wait_send()


def attend(
    meta_ref, q_ref, kv_ref, u_ref, x_ref, w_ref, og_ref, out_ref, dhu_ref, gout_ref, dq_ref, dk_ref, dv_ref, kv_all,
    q_all, da_all, da, parts, acc, mask, local, send, recv, group, early, *, span
):
    own = lax.axis_index("pair")
    chips, core, chip = span // 2, own % 2, own // 2
    size, width = q_ref.shape
    kv_ring, q_ring, da_ring = (
        Ring(source, gathered, send.at[i], recv.at[i], local.at[i], span, falling)
        for i, (source, gathered, falling) in enumerate(
            ((kv_ref, kv_all, False), (q_ref, q_all, True), (da, da_all, True))
        )
    )
    for g in (3, 1, 2):
        group(g)
    kv_ring.start()
    q_ring.start()
    group(0)
    dhu_ref[...] = dot_t(og_ref[...], w_ref[...])

    def on_step(step, *actions):
        for k, action in enumerate(actions):
            if action:
                pl.when(step == k)(action)

    def block_at(step, falling):
        turn = step // 2
        shift = turn if falling else (3 * turn - (turn * (turn - 1)) // 2) % 4
        return ((chip + shift) % chips) * 2 + (core + step % 2) % 2

    def split(value, at):
        parts[at] = even_half(value)
        parts[at + 1] = odd_half(value)

    def slabs(work):
        def one(s, carry):
            first = pl.multiple_of(s * 128, 128)
            work(pl.ds(first, 128), pl.ds(pl.multiple_of(width + s * 128, 128), 128))
            return carry

        lax.fori_loop(0, width // 128, one, 0, unroll=True)

    def both(rows):
        return jnp.concatenate([even_half(rows), odd_half(rows)], axis=0)

    zeros = meta_ref[0:1, 2:3].astype(I32)
    split(q_ref[...] * 0.0625, 0)
    split(kv_ref[:, :width] * 0.0625, 4)
    split(kv_ref[:, width:] * 0.0625, 6)
    acc[...] = jnp.zeros_like(acc)
    dq_ref[...] = jnp.zeros_like(dq_ref)
    dk_ref[...] = jnp.zeros_like(dk_ref)
    dv_ref[...] = jnp.zeros_like(dv_ref)

    def forward(step, carry):
        j = block_at(step, False)

        def near():
            kv_ring.relay_wrap()
            kv_ring.relay_near()
            q_ring.relay_near()
            q_ring.relay_wrap()

        def far():
            kv_ring.relay_far()
            q_ring.relay_far()

        on_step(
            step, kv_ring.own().wait, kv_ring.handed_own, near, kv_ring.handed_near, None, kv_ring.handed_wrap, far,
            kv_ring.handed_far
        )

        @pl.when(j <= own)
        def _():
            mask[...] = visible(0, size, own, j, zeros) * meta_ref[pl.ds(j, 1), 0:1]

            def work(cols, late):
                keys = kv_all[j, :, cols]
                weights = []
                for half in range(2):
                    h = dot_t(parts[half, :, cols], keys)
                    weights.append((h * ((1.0 + jnp.tanh(h)) * mask[...])).astype(BF16))
                acc[:, cols] += dot(jnp.concatenate(weights, axis=1), both(kv_all[j, :, late]))

            slabs(work)

        return carry

    lax.fori_loop(0, span, forward, 0)

    for part in range(2):
        rows = slice(part * (size // 2), (part + 1) * (size // 2))
        normed, spread = normalize(acc[rows])
        acc[rows] = normed
        da[rows] = norm_back(dhu_ref[rows] * u_ref[rows].astype(F32), normed, spread).astype(BF16)
        da_ring.start_part(part)
    normed = acc[...]
    dy = dhu_ref[...]
    gated = (normed * u_ref[...].astype(F32)).astype(BF16)
    split(da[...] * 0.0625, 2)
    dhu_ref[...] = dy * normed
    out_ref[...] = (dot(gated, w_ref[...]) + x_ref[...].astype(F32)).astype(BF16)
    gout_ref[...] = lax.dot_general(gated, og_ref[...], (((0,), (0,)), ((), ())), preferred_element_type=F32)
    early(0)

    def by_query(step, carry):
        j = block_at(step, False)

        @pl.when(j <= own)
        def _():
            mask[...] = visible(0, size, own, j, zeros) * meta_ref[pl.ds(j, 1), 0:1]

            def work(cols, late):
                keys = kv_all[j, :, cols]
                values = kv_all[j, :, late]
                grads = []
                for half in range(2):
                    h = dot_t(parts[half, :, cols], keys)
                    u = 1.0 + jnp.tanh(h)
                    seen = u * mask[...]
                    slope = seen + h * seen * (2.0 - u)
                    grads.append((dot_t(parts[2 + half, :, cols], values) * slope).astype(BF16))
                dq_ref[:, cols] += dot(jnp.concatenate(grads, axis=1), both(keys))

            slabs(work)

        return carry

    lax.fori_loop(0, span, by_query, 0)
    early(1)

    def by_key(step, carry):
        i = block_at(step, True)

        def mine():
            q_ring.own().wait()
            da_ring.own().wait()

        def pair(name):
            def action():
                getattr(q_ring, name)()
                getattr(da_ring, name)()

            return action

        on_step(
            step, mine, pair("handed_own"), da_ring.relay_near, pair("handed_near"), da_ring.relay_far, pair("handed_far"),
            da_ring.relay_wrap, pair("handed_wrap")
        )

        @pl.when(i >= own)
        def _():
            mask[...] = visible(1, size, i, own, zeros) * meta_ref[pl.ds(i, 1), 1:2]

            def work(cols, late):
                queries = q_all[i, :, cols]
                dafter = da_all[i, :, cols]
                grads, weights = [], []
                for half in range(2):
                    h = dot_t(parts[4 + half, :, cols], queries)
                    u = 1.0 + jnp.tanh(h)
                    seen = u * mask[...]
                    weight = h * seen
                    weights.append(weight.astype(BF16))
                    slope = seen + weight * (2.0 - u)
                    grads.append((dot_t(parts[6 + half, :, cols], dafter) * slope).astype(BF16))
                dk_ref[:, cols] += dot(jnp.concatenate(grads, axis=1), both(queries))
                dv_ref[:, cols] += dot(jnp.concatenate(weights, axis=1), both(dafter))

            slabs(work)

        return carry

    lax.fori_loop(0, span, by_key, 0)
    for ring in (kv_ring, q_ring, da_ring):
        ring.sent()


def interleave(upper, lower, rows, out_ref):
    count, cols = upper.shape
    top = (iota((count, cols), 0) % (2 * rows)) < rows
    first = jnp.where(top, upper, pltpu.roll(lower, rows, 0))
    second = jnp.where(top, pltpu.roll(upper, count - rows, 0), lower)
    out_ref[0] = first.reshape(out_ref.shape[1:])
    out_ref[1] = second.reshape(out_ref.shape[1:])


def weigh(g, grad, z_ref, turned_ref, w_ref, dxn_ref):
    width = grad.shape[1]
    cols = slice(g * width, (g + 1) * width)
    h = 0.5 * z_ref[:, cols]
    t = jnp.tanh(h)
    slope = 0.5 * (1.0 + t) * (1.0 + h * (1.0 - t))
    dz = (grad * slope).astype(BF16)
    dxn_ref[...] += dot_t(dz, w_ref[:, cols])
    return dot(turned_ref[...], dz)


def finish(dxn_ref, x_ref, og_ref, tr_ref, send_ref):
    size = x_ref.shape[0]
    normed, spread = normalize(x_ref[...].astype(F32))
    dx = norm_back(dxn_ref[...], normed, spread) + og_ref[...].astype(F32)
    count = send_ref.shape[0] * send_ref.shape[1]
    pick = jnp.where(iota((count, size), 0) == tr_ref[...], 1.0, 0.0).astype(BF16)
    send_ref[...] = dot(pick, dx.astype(BF16)).astype(BF16).reshape(send_ref.shape)


def partner(k, groups, span):
    g, p = lax.axis_index("dp"), lax.axis_index("pair")
    chips, side = span // 2, math.isqrt(groups)
    to_p = ((p // 2 + (k // 2) % chips) % chips) * 2 + (p % 2 + k % 2) % 2
    shift = k // span
    to_g = ((g // side + shift // side) % side) * side + (g % side + shift % side) % side
    return to_g, to_p


def greet(groups, span):
    g, p = lax.axis_index("dp"), lax.axis_index("pair")
    barrier = pltpu.get_barrier_semaphore()

    def hello(device):
        pl.semaphore_signal(barrier, inc=1, device_id=device, device_id_type=MESH)

    def hello_pair(k, carry):
        hello((g, partner(k, groups, span)[1]))
        return carry

    def hello_group(k, carry):
        hello((partner(k * span, groups, span)[0], p))
        return carry

    lax.fori_loop(1, span, hello_pair, 0)
    lax.fori_loop(1, groups, hello_group, 0)
    return lambda: pl.semaphore_wait(barrier, span + groups - 2)


def ask(request, middle, slots, sems, groups, span):
    g, p = lax.axis_index("dp"), lax.axis_index("pair")
    own = pltpu.make_async_copy(request.at[:, p], middle.at[p], sems.at[0])
    own.start()

    def over_pair(k, carry):
        to_p = partner(k, groups, span)[1]
        pltpu.make_async_remote_copy(
            src_ref=request.at[:, to_p],
            dst_ref=middle.at[p],
            send_sem=sems.at[1],
            recv_sem=sems.at[2],
            device_id=(g, to_p),
            device_id_type=MESH,
        ).start()
        return carry

    lax.fori_loop(1, span, over_pair, 0)
    own.wait()
    drain(middle, span - 1, sems.at[1])
    drain(middle, span - 1, sems.at[2])
    own = pltpu.make_async_copy(middle.at[:, g], slots.at[g], sems.at[3])
    own.start()

    def over_groups(k, carry):
        to_g = partner(k * span, groups, span)[0]
        pltpu.make_async_remote_copy(
            src_ref=middle.at[:, to_g],
            dst_ref=slots.at[g],
            send_sem=sems.at[4],
            recv_sem=sems.at[5],
            device_id=(to_g, p),
            device_id_type=MESH,
        ).start()
        return carry

    lax.fori_loop(1, groups, over_groups, 0)
    own.wait()
    if groups > 1:
        drain(slots, groups - 1, sems.at[4])
        drain(slots, groups - 1, sems.at[5])


def drain(ref, count, sem):
    part = ref.at[pl.ds(0, count)]
    pltpu.make_async_copy(part, part, sem).wait()


def push_all(source, target, send, recv, groups, span, rows):
    me = lax.axis_index("dp") * span + lax.axis_index("pair")
    used = pl.ds(0, rows)

    def push(k, carry):
        to_g, to_p = partner(k, groups, span)
        pltpu.make_async_remote_copy(
            src_ref=source.at[to_g * span + to_p, used],
            dst_ref=target.at[me, used],
            send_sem=send,
            recv_sem=recv,
            device_id=(to_g, to_p),
            device_id_type=MESH,
        ).start()
        return carry

    lax.fori_loop(1, groups * span, push, 0)

    def wait():
        all_of = target.at[pl.ds(0, groups * span - 1), used]
        pltpu.make_async_copy(all_of, all_of, send).wait()
        pltpu.make_async_copy(all_of, all_of, recv).wait()

    return wait


def keep(source, target, sem, span):
    me = lax.axis_index("dp") * span + lax.axis_index("pair")
    copy = pltpu.make_async_copy(source.at[me], target.at[me], sem)
    copy.start()
    return copy


def push_early(early_ref, arrived_ref, cols, sems, groups, span):
    g, p = lax.axis_index("dp"), lax.axis_index("pair")
    count = early_ref.shape[0] // groups

    def mine(to_g):
        return early_ref.at[pl.ds(pl.multiple_of(to_g * count, count), count), cols]

    own = pltpu.make_async_copy(mine(g), arrived_ref.at[g, :, cols], sems.at[0])
    own.start()

    def push(k, carry):
        to_g = partner(k * span, groups, span)[0]
        pltpu.make_async_remote_copy(
            src_ref=mine(to_g),
            dst_ref=arrived_ref.at[g, :, cols],
            send_sem=sems.at[1],
            recv_sem=sems.at[2],
            device_id=(to_g, p),
            device_id_type=MESH,
        ).start()
        return carry

    lax.fori_loop(1, groups, push, 0)


def wait_early(early_ref, arrived_ref, cols, sems, groups):
    pltpu.make_async_copy(arrived_ref.at[0, :, cols], arrived_ref.at[0, :, cols], sems.at[0]).wait()
    if groups > 1:
        others = arrived_ref.at[pl.ds(0, groups - 1), :, cols]
        pltpu.make_async_copy(others, others, sems.at[1]).wait()
        pltpu.make_async_copy(others, others, sems.at[2]).wait()


def settle(arrived_ref, halves_ref, settled_ref, sems, groups, span, rows):
    g, p = lax.axis_index("dp"), lax.axis_index("pair")
    count, cols = arrived_ref.shape[1:]

    def add(k, summed):
        return summed + arrived_ref[k].astype(F32)

    summed = lax.fori_loop(0, groups, add, jnp.zeros((count, cols), F32))
    interleave(summed[:, : cols // 2], summed[:, cols // 2 :], rows, halves_ref)
    own = pltpu.make_async_copy(halves_ref.at[p % 2, p // 2], settled_ref.at[p], sems.at[0])
    own.start()

    def push(k, carry):
        to_p = partner(k, groups, span)[1]
        pltpu.make_async_remote_copy(
            src_ref=halves_ref.at[to_p % 2, to_p // 2],
            dst_ref=settled_ref.at[p],
            send_sem=sems.at[1],
            recv_sem=sems.at[2],
            device_id=(g, to_p),
            device_id_type=MESH,
        ).start()
        return carry

    lax.fori_loop(1, span, push, 0)

    def wait():
        own.wait()
        drain(settled_ref, span - 1, sems.at[1])
        drain(settled_ref, span - 1, sems.at[2])

    return wait


def swap_halves(grads_ref, got, sems):
    g, p = lax.axis_index("dp"), lax.axis_index("pair")
    core = p % 2
    swap = pltpu.make_async_remote_copy(
        src_ref=grads_ref.at[1 - core],
        dst_ref=got,
        send_sem=sems.at[1],
        recv_sem=sems.at[2],
        device_id=(g, p + 1 - 2 * core),
        device_id_type=MESH,
    )
    swap.start()
    return swap


def exchange_gradients(
    rows_ref, grads_ref, back_ref, parts_ref, got, part, sems, swap, between, *, groups, span, bound
):
    total = groups * span
    g, p = lax.axis_index("dp"), lax.axis_index("pair")
    me, core = g * span + p, p % 2
    chip, chips = me // 2, total // 2
    own = keep(rows_ref, back_ref, sems.at[0], span)
    landed = push_all(rows_ref, back_ref, sems.at[3], sems.at[4], groups, span, bound)
    swap.wait()

    def add(m, carry):
        part[m] = (grads_ref[core, m] + got[m]).astype(BF16)
        return carry

    lax.fori_loop(0, chips, add, 0)
    mine = pltpu.make_async_copy(part.at[chip], parts_ref.at[chip], sems.at[5])
    mine.start()

    def push_part(k, carry):
        to_g, to_p = partner(2 * k, groups, span)
        pltpu.make_async_remote_copy(
            src_ref=part.at[(to_g * span + to_p) // 2],
            dst_ref=parts_ref.at[chip],
            send_sem=sems.at[6],
            recv_sem=sems.at[7],
            device_id=(to_g, to_p),
            device_id_type=MESH,
        ).start()
        return carry

    lax.fori_loop(1, chips, push_part, 0)
    settled = between()
    own.wait()
    mine.wait()
    settled()
    landed()
    drain(parts_ref, chips - 1, sems.at[6])
    drain(parts_ref, chips - 1, sems.at[7])


def update_kernel(
    slots_ref, back_ref, table_ref, accum_ref, parts_ref, settled_ref, layer_ref, tnew_ref, anew_ref, gin_ref, gout_ref,
    out_ref, *, width, factor
):
    shards = slots_ref.shape[0] * slots_ref.shape[1]
    rows_dev, model = table_ref.shape
    count = shards * width
    spread = ((iota((shards, count), 1) // width) == iota((shards, count), 0)).astype(F32).astype(BF16)
    high, low = slot_halves(slots_ref[...].reshape(shards, 128))
    turn = lambda a: lax.dot_general(a, spread, (((0,), (0,)), ((), ())), preferred_element_type=F32)
    value = 2.0 * turn(high) + turn(low)
    mine = iota((128, count), 0) == (iota((128, count), 1) % width)
    slot = jnp.sum(jnp.where(mine, value, 0.0), axis=0, keepdims=True).astype(I32)
    pick = jnp.where(iota((rows_dev, count), 0) == slot, 1.0, 0.0).astype(BF16)
    total = dot(pick, back_ref[...].reshape(count, model))
    square = jnp.mean(total * total, axis=1, keepdims=True)
    eye = iota((rows_dev, rows_dev), 0) == iota((rows_dev, rows_dev), 1)
    accum = jnp.sum(jnp.where(eye, accum_ref[...], 0.0), axis=1, keepdims=True) + square
    anew_ref[...] = jnp.sum(jnp.where(eye, accum, 0.0), axis=0, keepdims=True)
    tnew_ref[...] = table_ref[...] - LEARN_RATE * total / jnp.sqrt(accum)

    def total_of(ref):
        def add(m, summed):
            return summed + ref[m].astype(F32)

        summed = lax.fori_loop(0, ref.shape[0], add, jnp.zeros(ref.shape[1:], F32)) * factor
        return summed[:rows], summed[rows:]

    rows = gin_ref.shape[0]
    half = model // 2
    gin_ref[:, model : 2 * model], gin_ref[:, 3 * model :] = total_of(parts_ref)
    upper, lower = total_of(settled_ref)
    gin_ref[:, :model] = upper[:, :model]
    gin_ref[:, 2 * model : 3 * model] = lower[:, half:]
    gout_ref[:, :half] = upper[:, model:]
    gout_ref[:, half:] = lower[:, :half]
    out_ref[...] = layer_ref[...]


def layer_kernel(
    row_ref, seg_ref, pair_ref, w_in_hbm, w_out_hbm, og_hbm, table_hbm, out_ref, slots, back, landed, settled,
    w_in_ref, w_out_ref, og_ref, table_ref, request, middle, target_r, target_c, meta, found, fetched, x, z, u, q, kv, dhu, wgrad, dq, dk, dv, kv_all,
    q_all, da_all, da, parts, acc, mask, turned, dxn, early, arrived, halves, grads, sending, got, part, local, send, recv, front, sems,
    load_sems, first_sems, second_sems, settle_sems, *,
    groups, span, width, rows
):
    tokens, rows_dev = row_ref.shape[0], table_ref.shape[0]
    bound = 2 * tokens // (groups * span)
    loads = [
        pltpu.make_async_copy(source, target, load_sems.at[i])
        for i, (source, target) in enumerate(
            ((table_hbm, table_ref), (w_in_hbm, w_in_ref), (w_out_hbm, w_out_ref), (og_hbm, og_ref))
        )
    ]
    for load in loads:
        load.start()
    fetched[...] = jnp.zeros_like(fetched)
    back[...] = jnp.zeros_like(back)
    ready = greet(groups, span)
    route(row_ref, seg_ref, pair_ref, request, target_r, target_c, meta, rows_dev=rows_dev, width=width)
    ready()
    ask(request, middle, slots, front, groups, span)
    for load in loads:
        load.wait()
    find(slots, table_ref, found, width=width)
    own = keep(found, fetched, front.at[6], span)
    answered = push_all(found, fetched, front.at[7], front.at[8], groups, span, bound)
    own.wait()
    answered()
    group = project(fetched, target_c, w_in_ref, x, z, u, q, kv, turned)
    dxn[...] = jnp.zeros_like(dxn)
    model = x.shape[1]
    stages = ((slice(0, 2 * model), first_sems), (slice(2 * model, 3 * model), second_sems))

    def weight(g, grad):
        return weigh(g, grad[...], z, turned, w_in_ref, dxn)

    def begin(stage):
        if stage == 0:
            early[:, :model] = weight(0, dhu).astype(BF16)
            early[:, model : 2 * model] = wgrad[...].astype(BF16)
        else:
            early[:, 2 * model :] = weight(2, dq).astype(BF16)
        push_early(early, arrived, *stages[stage], groups, span)

    def between():
        for stage in stages:
            wait_early(early, arrived, *stage, groups)
        return settle(arrived, halves, settled, settle_sems, groups, span, rows)

    attend(
        meta, q, kv, u, x, w_out_ref, og_ref, out_ref, dhu, wgrad, dq, dk, dv, kv_all, q_all, da_all, da, parts, acc,
        mask, local, send, recv, group, begin, span=span
    )
    interleave(weight(1, dv), weight(3, dk), rows, grads)
    swap = swap_halves(grads, got, sems)
    finish(dxn, x, og_ref, target_r, sending)
    exchange_gradients(
        sending, grads, back, landed, got, part, sems, swap, between, groups=groups, span=span, bound=bound
    )


def shape(dims, dtype):
    return jax.ShapeDtypeStruct(dims, dtype)


def body(table, accum, item_row, segments, pairs, w_in, w_out, out_grad):
    tokens = item_row.shape[0]
    rows_dev, model = table.shape
    shards = lax.axis_size(("dp", "pair"))
    span = lax.axis_size("pair")
    width = -(-(2 * tokens // shards) // 8) * 8
    rows = model // shards
    chunk = (2 * rows, model)
    groups = shards // span
    settling = (2 * rows, 3 * model // 2)
    half_grads = (shards // 2,) + chunk
    block = lambda cols: VMEM((span, tokens, cols), BF16)
    low = lambda cols: VMEM((tokens, cols), BF16)
    high = lambda cols: VMEM((tokens, cols), F32)
    request = (groups, span, 1, 128)
    parcel = (shards, width, model)
    layer_out, slots, back, landed, settled = pl.pallas_call(
        functools.partial(layer_kernel, groups=groups, span=span, width=width, rows=rows),
        out_shape=(
            shape((tokens, model), BF16),
            shape(request, I32),
            shape(parcel, BF16),
            shape(half_grads, BF16),
            shape((span,) + settling, F32),
        ),
        in_specs=[whole()] * 3 + [pl.BlockSpec(memory_space=pl.ANY)] * 4,
        out_specs=[whole()] * 5,
        scratch_shapes=[
            VMEM(w_in.shape, BF16),
            VMEM(w_out.shape, BF16),
            VMEM(out_grad.shape, BF16),
            VMEM(table.shape, F32),
            VMEM(request, I32),
            VMEM((span, groups, 1, 128), I32),
            VMEM((1, tokens), I32),
            VMEM((tokens, 1), I32),
            VMEM((8, 128), F32),
            VMEM((shards, width, model), BF16),
            VMEM((shards, width, model), BF16),
            low(model),
            high(4 * model),
            low(model),
            low(model),
            low(2 * model),
            high(model),
            VMEM((model, model), F32),
            high(model),
            high(model),
            high(model),
            block(2 * model),
            block(model),
            block(model),
            low(model),
            VMEM((8, tokens, model), BF16),
            high(model),
            high(tokens),
            VMEM((model, tokens), BF16),
            high(model),
            VMEM((model, 3 * model), BF16),
            VMEM((groups, model // groups, 3 * model), BF16),
            VMEM((2, span // 2) + settling, F32),
            VMEM((2,) + half_grads, F32),
            VMEM(parcel, BF16),
            VMEM(half_grads, F32),
            VMEM(half_grads, BF16),
            pltpu.SemaphoreType.DMA((3,)),
            pltpu.SemaphoreType.DMA((3, 15)),
            pltpu.SemaphoreType.DMA((3, 15)),
            pltpu.SemaphoreType.DMA((9,)),
            pltpu.SemaphoreType.DMA((8,)),
            pltpu.SemaphoreType.DMA((4,)),
            pltpu.SemaphoreType.DMA((3,)),
            pltpu.SemaphoreType.DMA((3,)),
            pltpu.SemaphoreType.DMA((3,)),
        ],
        compiler_params=params(collective_id=0, has_side_effects=True),
    )(item_row, segments, pairs[0].T, w_in, w_out, out_grad, table)
    table_new, accum_new, grad_in, grad_out, layer_out = pl.pallas_call(
        functools.partial(update_kernel, width=width, factor=1.0 / math.sqrt(tokens * shards)),
        out_shape=(
            shape((rows_dev, model), F32),
            shape((1, rows_dev), F32),
            shape((rows, 4 * model), F32),
            shape((rows, model), F32),
            shape((tokens, model), BF16),
        ),
        in_specs=[whole()] * 7,
        out_specs=[whole()] * 5,
        compiler_params=params(),
    )(slots, back, table, accum.reshape(1, rows_dev), landed, settled, layer_out)
    return layer_out, table_new, accum_new.reshape(rows_dev), grad_in, grad_out


def solution(mesh):
    both = ("dp", "pair")
    return jax.shard_map(
        body,
        mesh=mesh,
        in_specs=(
            P(both, None),
            P(both),
            P(both),
            P("dp", None),
            P("dp", None, None),
            P(),
            P(),
            P(both, None),
        ),
        out_specs=(P(both, None), P(both, None), P(both), P(both, None), P(both, None)),
        check_vma=False,
    )
```
